128 devices in a mesh: seg: 8 (over y_lo, z), grp: 16 (over x, y_hi, core).
Axes of the slice: x: 4, y: 4 (y_hi: 2, y_lo: 2; y = y_hi * 2 + y_lo), z: 4, core: 2. Of those that a mesh axis runs over, the one named last changes fastest.
Arguments:
- frames_in: bfloat16 [128, 32, 120, 128], P(('seg', 'grp')), may hold values from -6 to 6
- spatial_weight: bfloat16 [9, 128, 128], replicated, may hold values from -0.1875 to 0.1875
- temporal_weight: bfloat16 [2, 5, 128, 128], replicated, may hold values from -0.25 to 0.25
- uniting_weight: bfloat16 [2, 128, 128], replicated, may hold values from -0.375 to 0.375
- key_index: int32 [8], replicated, may hold values from 0 to 15
- dilation: int32 [2], replicated, may hold values from 1 to 8, as said below
- cotangent: bfloat16 [128, 32, 120, 128], P(('seg', 'grp')), may hold values from -6 to 6
Outputs:
- united: bfloat16 [128, 32, 120, 128], P(('seg', 'grp'))
- grad_frames: bfloat16 [128, 32, 120, 128], P(('seg', 'grp'))
- grad_spatial: float32 [9, 128, 128], replicated
- grad_temporal: float32 [2, 5, 128, 128], replicated
- grad_uniting: float32 [2, 128, 128], replicated
The draws below stay inside these ranges and needn't reach their ends.
Inputs may be any that keep to these rules, and one draw needn't show every extreme that they name: `key_index`: position of a segment's keyframe within its 16 frames. Exactly one layer uses dilation 8; the others use less.
All inputs are finite; a program needn't handle non-finite values.
Results may differ from the reference program's by a relative error of at most 0.0095.
Values may be sent and summed in bfloat16 or wider, within the bound.
A program may use at most 128 MiB of HBM per device.

```python
import jax
import jax.numpy as jnp
from jax import lax

C = 128
H = 32
W = 120
LAYERS = 2
DMAX = 8
FRAMES = 128
SEGLEN = 16
N_SEG = 8


def draw_dilation(key, part):
    first_key, second_key = jax.random.split(jax.random.fold_in(key, 17))
    values = jax.random.randint(first_key, (LAYERS,), 1, DMAX)
    chosen = jax.random.randint(second_key, (), 0, LAYERS)
    return jnp.where(jnp.arange(LAYERS) == chosen, DMAX, values).astype(jnp.int32)


def touch_ends(values, own_key, low, high):
    extent = values.shape
    index_at = [jax.random.randint(jax.random.fold_in(own_key, axis), (), 0, extent[axis]) for axis in range(len(extent))]
    values = values.at[tuple(index_at)].set(low)
    longest = extent.index(max(extent))
    index_at[longest] = (index_at[longest] + 1) % extent[longest]
    return values.at[tuple(index_at)].set(high)


def level_of(stream_key, dims, cuts, smallest, high):
    level = 1.0
    for position, blocks in cuts:
        heights = jax.random.uniform(jax.random.fold_in(jax.random.fold_in(stream_key, 6), position), (blocks,), jnp.float32, smallest / len(cuts), high / len(cuts))
        level = level * jnp.repeat(jnp.exp(heights), dims[position] // blocks).reshape((-1,) + (1,) * (len(dims) - 1 - position))
    return level


def normal_values(stream_key, dims, scale, limit, pieces=(), kind=jnp.bfloat16):
    drawn = scale * jax.random.normal(stream_key, dims, jnp.float32)
    if pieces:
        drawn = drawn * level_of(stream_key, dims, pieces, -0.22, 0.18)
    return jnp.clip(drawn, -limit, limit).astype(kind)


def setup_inputs(seed: int = 0) -> dict:
    streams_of = jax.random.split(jax.random.key(seed), 8)
    frames_in = normal_values(streams_of[0], (FRAMES, H, W, C), 1.0, 6.0, ((0, 128),))
    spatial_weight = normal_values(streams_of[1], (9, C, C), (9 * C) ** -0.5, 0.1875)
    temporal_weight = normal_values(streams_of[2], (LAYERS, 5, C, C), (5 * C) ** -0.5, 0.25)
    uniting_weight = normal_values(streams_of[3], (2, C, C), (2 * C) ** -0.5, 0.375)
    key_index = touch_ends(jax.random.randint(streams_of[4], (N_SEG,), 0, SEGLEN), jax.random.fold_in(streams_of[4], 1), 0, SEGLEN - 1).astype(jnp.int32)
    dilation = draw_dilation(jax.random.fold_in(streams_of[7], 71), 0)
    cotangent = normal_values(streams_of[6], (FRAMES, H, W, C), 1.0, 6.0, ((0, 128),))
    return {"frames_in": frames_in, "spatial_weight": spatial_weight, "temporal_weight": temporal_weight, "uniting_weight": uniting_weight, "key_index": key_index, "dilation": dilation, "cotangent": cotangent}


def silu_grad(value):
    sigma = jax.nn.sigmoid(value)
    return sigma * (1.0 + value * (1.0 - sigma))

def inner(left, right):
    return lax.dot_general(left, right, (((0,), (0,)), ((), ())), preferred_element_type=jnp.float32)

def spatial_forward(frames, kernel):
    count, rows, cols, chans = frames.shape
    padded = jnp.pad(frames, ((0, 0), (1, 1), (1, 1), (0, 0)))
    total = jnp.zeros((count * rows * cols, chans), jnp.float32)
    for row_tap in range(3):
        for col_tap in range(3):
            piece = padded[:, row_tap:row_tap + rows, col_tap:col_tap + cols, :].reshape(-1, chans)
            total = total + jnp.dot(piece, kernel[3 * row_tap + col_tap], preferred_element_type=jnp.float32)
    return total.reshape(frames.shape)

def spatial_back(grads, kernel):
    count, rows, cols, chans = grads.shape
    padded = jnp.pad(grads, ((0, 0), (1, 1), (1, 1), (0, 0)))
    total = jnp.zeros((count * rows * cols, chans), jnp.float32)
    for row_tap in range(3):
        for col_tap in range(3):
            piece = padded[:, 2 - row_tap:2 - row_tap + rows, 2 - col_tap:2 - col_tap + cols, :].reshape(-1, chans)
            total = total + jnp.dot(piece, kernel[3 * row_tap + col_tap].T, preferred_element_type=jnp.float32)
    return total.reshape(grads.shape)

def spatial_wgrad(frames, grads):
    count, rows, cols, chans = frames.shape
    padded = jnp.pad(frames, ((0, 0), (1, 1), (1, 1), (0, 0)))
    flat_grads = grads.reshape(-1, chans)
    result = []
    for row_tap in range(3):
        for col_tap in range(3):
            piece = padded[:, row_tap:row_tap + rows, col_tap:col_tap + cols, :].reshape(-1, chans)
            result.append(inner(piece, flat_grads))
    return jnp.stack(result)

def shifted(values, offset):
    padded = jnp.pad(values, ((2 * DMAX, 2 * DMAX), (0, 0), (0, 0)))
    start = (2 * DMAX + offset).astype(jnp.int32)
    return lax.dynamic_slice_in_dim(padded, start, values.shape[0], 0)

def temporal_forward(acts, kernel, step_size):
    chans = acts.shape[2]
    total = jnp.zeros((acts.shape[0] * acts.shape[1], chans), jnp.float32)
    for tap in range(5):
        piece = shifted(acts, (tap - 2) * step_size).reshape(-1, chans)
        total = total + jnp.dot(piece, kernel[tap], preferred_element_type=jnp.float32)
    return total.reshape(acts.shape)

def temporal_back(grads, kernel, step_size):
    chans = grads.shape[2]
    total = jnp.zeros((grads.shape[0] * grads.shape[1], chans), jnp.float32)
    for tap in range(5):
        piece = shifted(grads, (2 - tap) * step_size).reshape(-1, chans)
        total = total + jnp.dot(piece, kernel[tap].T, preferred_element_type=jnp.float32)
    return total.reshape(grads.shape)

def temporal_wgrad(acts, grads, step_size):
    chans = acts.shape[2]
    flat_grads = grads.reshape(-1, chans)
    return jnp.stack([inner(shifted(acts, (tap - 2) * step_size).reshape(-1, chans), flat_grads) for tap in range(5)])

def reference(frames_in, spatial_weight, temporal_weight, uniting_weight, key_index, dilation, cotangent):
    pixels = H * W
    pre_spatial = spatial_forward(frames_in, spatial_weight)
    act = jax.nn.silu(pre_spatial).astype(jnp.bfloat16).reshape(FRAMES, pixels, C)
    acts = [act]
    pres = []
    for layer in range(LAYERS):
        pre = temporal_forward(acts[-1], temporal_weight[layer], dilation[layer])
        pres.append(pre)
        acts.append(jax.nn.silu(pre).astype(jnp.bfloat16))
    feat = acts[-1]
    feat_seg = feat.reshape(N_SEG, SEGLEN, pixels, C)
    keys = feat_seg[jnp.arange(N_SEG), key_index]
    key_full = jnp.broadcast_to(keys[:, None], feat_seg.shape).reshape(-1, C)
    feat_flat = feat.reshape(-1, C)
    united = (jnp.dot(feat_flat, uniting_weight[0], preferred_element_type=jnp.float32) + jnp.dot(key_full, uniting_weight[1], preferred_element_type=jnp.float32)).astype(jnp.bfloat16)
    cot_flat = cotangent.reshape(-1, C)
    grad_feat = jnp.dot(cot_flat, uniting_weight[0].T, preferred_element_type=jnp.float32).reshape(FRAMES, pixels, C)
    seg_cot = lax.optimization_barrier(jnp.sum(cotangent.reshape(N_SEG, SEGLEN, pixels, C).astype(jnp.float32), axis=1))
    key_term = jnp.dot(seg_cot.reshape(-1, C), uniting_weight[1].T.astype(jnp.float32), precision=lax.Precision.HIGHEST).reshape(N_SEG, pixels, C)
    onehot = (jnp.arange(SEGLEN, dtype=jnp.int32)[None, :] == key_index[:, None]).astype(jnp.float32)
    grad_feat = grad_feat + (onehot[:, :, None, None] * key_term[:, None]).reshape(FRAMES, pixels, C)
    grad_uniting = jnp.stack([inner(feat_flat, cot_flat), inner(key_full, cot_flat)])
    grad_pre = (grad_feat * silu_grad(pres[-1])).astype(jnp.bfloat16)
    tgrads = [None] * LAYERS
    grad_act0 = None
    for layer in range(LAYERS - 1, -1, -1):
        tgrads[layer] = temporal_wgrad(acts[layer], grad_pre, dilation[layer])
        grad_act = temporal_back(grad_pre, temporal_weight[layer], dilation[layer])
        if layer > 0:
            grad_pre = (grad_act * silu_grad(pres[layer - 1])).astype(jnp.bfloat16)
        else:
            grad_act0 = grad_act.astype(jnp.bfloat16)
    grad_spre = (grad_act0.reshape(frames_in.shape).astype(jnp.float32) * silu_grad(pre_spatial)).astype(jnp.bfloat16)
    grad_frames = spatial_back(grad_spre, spatial_weight).astype(jnp.bfloat16)
    grad_spatial = spatial_wgrad(frames_in, grad_spre)
    scale = 1.0 / jnp.sqrt(jnp.float32(FRAMES * H * W))
    return (united.reshape(frames_in.shape), grad_frames, grad_spatial * scale, jnp.stack(tgrads) * scale, grad_uniting * scale)
```

```python
import jax
import jax.numpy as jnp
from jax import lax
from jax.sharding import PartitionSpec as P

LAYERS = 2
DMAX = 8


def from_root(value, axis, root):
    mine = lax.axis_index(axis) == root
    return lax.psum(jnp.where(mine, value, jnp.zeros_like(value)), axis)


def silu_grad(value):
    sigma = jax.nn.sigmoid(value)
    return sigma * (1.0 + value * (1.0 - sigma))


def inner(left, right):
    return lax.dot_general(
        left, right, (((0,), (0,)), ((), ())), preferred_element_type=jnp.float32
    )


def spatial_forward(frames, kernel):
    count, rows, cols, chans = frames.shape
    padded = jnp.pad(frames, ((0, 0), (1, 1), (1, 1), (0, 0)))
    total = jnp.zeros((count * rows * cols, chans), jnp.float32)
    for row_tap in range(3):
        for col_tap in range(3):
            piece = padded[:, row_tap : row_tap + rows, col_tap : col_tap + cols, :].reshape(
                -1, chans
            )
            total = total + jnp.dot(
                piece, kernel[3 * row_tap + col_tap], preferred_element_type=jnp.float32
            )
    return total.reshape(frames.shape)


def spatial_back(grads, kernel):
    count, rows, cols, chans = grads.shape
    padded = jnp.pad(grads, ((0, 0), (1, 1), (1, 1), (0, 0)))
    total = jnp.zeros((count * rows * cols, chans), jnp.float32)
    for row_tap in range(3):
        for col_tap in range(3):
            piece = padded[
                :, 2 - row_tap : 2 - row_tap + rows, 2 - col_tap : 2 - col_tap + cols, :
            ].reshape(-1, chans)
            total = total + jnp.dot(
                piece, kernel[3 * row_tap + col_tap].T, preferred_element_type=jnp.float32
            )
    return total.reshape(grads.shape)


def spatial_wgrad(frames, grads):
    count, rows, cols, chans = frames.shape
    padded = jnp.pad(frames, ((0, 0), (1, 1), (1, 1), (0, 0)))
    flat_grads = grads.reshape(-1, chans)
    result = []
    for row_tap in range(3):
        for col_tap in range(3):
            piece = padded[:, row_tap : row_tap + rows, col_tap : col_tap + cols, :].reshape(
                -1, chans
            )
            result.append(inner(piece, flat_grads))
    return jnp.stack(result)


def shifted(values, offset):
    padded = jnp.pad(values, ((2 * DMAX, 2 * DMAX), (0, 0), (0, 0)))
    start = 2 * DMAX + offset
    return lax.dynamic_slice_in_dim(padded, start, values.shape[0], 0)


def temporal_forward(acts, kernel, step_size):
    chans = acts.shape[2]
    total = jnp.zeros((acts.shape[0] * acts.shape[1], chans), jnp.float32)
    for tap in range(5):
        piece = shifted(acts, (tap - 2) * step_size).reshape(-1, chans)
        total = total + jnp.dot(piece, kernel[tap], preferred_element_type=jnp.float32)
    return total.reshape(acts.shape)


def temporal_back(grads, kernel, step_size):
    chans = grads.shape[2]
    total = jnp.zeros((grads.shape[0] * grads.shape[1], chans), jnp.float32)
    for tap in range(5):
        piece = shifted(grads, (2 - tap) * step_size).reshape(-1, chans)
        total = total + jnp.dot(piece, kernel[tap].T, preferred_element_type=jnp.float32)
    return total.reshape(grads.shape)


def temporal_wgrad(acts, grads, step_size):
    chans = acts.shape[2]
    flat_grads = grads.reshape(-1, chans)
    return jnp.stack(
        [
            inner(shifted(acts, (tap - 2) * step_size).reshape(-1, chans), flat_grads)
            for tap in range(5)
        ]
    )


def to_pixels(flat):
    return lax.all_to_all(flat, ("seg", "grp"), split_axis=1, concat_axis=0, tiled=True)


def to_frames(blocks):
    return lax.all_to_all(blocks, ("seg", "grp"), split_axis=0, concat_axis=1, tiled=True)


def all_sum(parts):
    flat = jnp.concatenate([p.reshape(-1) for p in parts])
    count = lax.axis_size(("seg", "grp"))
    chunk = flat.shape[0] // count
    pieces = lax.all_to_all(
        flat.reshape(count, chunk), ("seg", "grp"), split_axis=0, concat_axis=0, tiled=True
    )
    mine = jnp.sum(pieces, axis=0)
    spread = jnp.broadcast_to(mine[None], (count, chunk))
    whole = lax.all_to_all(spread, ("seg", "grp"), split_axis=0, concat_axis=0, tiled=True)
    whole = whole.reshape(-1)
    out = []
    offset = 0
    for p in parts:
        out.append(whole[offset : offset + p.size].reshape(p.shape))
        offset += p.size
    return out


def local(
    frames_in, spatial_weight, temporal_weight, uniting_weight, key_index, dilation, cotangent
):
    local_frames, rows, cols, chans = frames_in.shape
    pixels = rows * cols
    seg_count = lax.axis_size("seg")
    pre_spatial = spatial_forward(frames_in, spatial_weight)
    act_zero = jax.nn.silu(pre_spatial).astype(jnp.bfloat16).reshape(local_frames, pixels, chans)
    cot_local = cotangent.reshape(local_frames, pixels, chans)
    act_blocks = to_pixels(act_zero)
    cot_blocks = to_pixels(cot_local)
    acts = [act_blocks]
    total_frames = acts[0].shape[0]
    block = acts[0].shape[1]
    seg_frames = total_frames // seg_count
    pres = []
    for layer in range(LAYERS):
        pre = temporal_forward(acts[-1], temporal_weight[layer], dilation[layer])
        pres.append(pre)
        acts.append(jax.nn.silu(pre).astype(jnp.bfloat16))
    feat = acts[-1]
    feat_seg = feat.reshape(seg_count, seg_frames, block, chans)
    positions = jnp.arange(seg_frames, dtype=jnp.int32)
    onehot = positions[None, :] == key_index[:, None]
    keys = jnp.einsum(
        "ns,nspc->npc", onehot.astype(jnp.bfloat16), feat_seg, preferred_element_type=jnp.float32
    ).astype(jnp.bfloat16)
    key_full = jnp.broadcast_to(keys[:, None], feat_seg.shape).reshape(-1, chans)
    feat_flat = feat.reshape(-1, chans)
    key_part = jnp.dot(
        keys.reshape(-1, chans), uniting_weight[1], preferred_element_type=jnp.float32
    ).reshape(seg_count, 1, block, chans)
    main_part = jnp.dot(feat_flat, uniting_weight[0], preferred_element_type=jnp.float32)
    united_blocks = (
        main_part.reshape(seg_count, seg_frames, block, chans) + key_part
    ).astype(jnp.bfloat16).reshape(total_frames, block, chans)
    united = to_frames(united_blocks)
    cot_flat = cot_blocks.reshape(-1, chans)
    grad_feat = jnp.dot(cot_flat, uniting_weight[0].T, preferred_element_type=jnp.float32)
    seg_cot = jnp.sum(
        cot_blocks.reshape(seg_count, seg_frames, block, chans).astype(jnp.float32), axis=1
    )
    key_term = jnp.dot(
        seg_cot.reshape(-1, chans),
        uniting_weight[1].T.astype(jnp.float32),
        precision=lax.Precision.HIGHEST,
    ).reshape(seg_count, 1, block, chans)
    placed = onehot.astype(jnp.float32)[:, :, None, None] * key_term
    grad_feat = grad_feat.reshape(seg_count, seg_frames, block, chans) + placed
    grad_feat = grad_feat.reshape(total_frames, block, chans)
    grad_uniting = jnp.stack([inner(feat_flat, cot_flat), inner(key_full, cot_flat)])
    grad_pre = (grad_feat * silu_grad(pres[-1])).astype(jnp.bfloat16)
    tgrads = [None] * LAYERS
    grad_act0 = None
    for layer in range(LAYERS - 1, -1, -1):
        tgrads[layer] = temporal_wgrad(acts[layer], grad_pre, dilation[layer])
        grad_act = temporal_back(grad_pre, temporal_weight[layer], dilation[layer])
        if layer > 0:
            grad_pre = (grad_act * silu_grad(pres[layer - 1])).astype(jnp.bfloat16)
        else:
            grad_act0 = grad_act.astype(jnp.bfloat16)
    grad_time = to_frames(grad_act0).reshape(frames_in.shape)
    grad_spre = (grad_time.astype(jnp.float32) * silu_grad(pre_spatial)).astype(jnp.bfloat16)
    grad_frames = spatial_back(grad_spre, spatial_weight).astype(jnp.bfloat16)
    grad_spatial = spatial_wgrad(frames_in, grad_spre)
    summed = all_sum((grad_spatial, jnp.stack(tgrads), grad_uniting))
    scale = 1.0 / jnp.sqrt(jnp.float32(total_frames * pixels))
    return (
        united.reshape(frames_in.shape),
        grad_frames,
        summed[0] * scale,
        summed[1] * scale,
        summed[2] * scale,
    )


def solution(mesh):
    placed = (
        P(("seg", "grp"), None, None, None),
        P(),
        P(),
        P(),
        P(),
        P(),
        P(("seg", "grp"), None, None, None),
    )
    return jax.shard_map(
        local,
        mesh=mesh,
        in_specs=placed,
        out_specs=(
            P(("seg", "grp"), None, None, None),
            P(("seg", "grp"), None, None, None),
            P(),
            P(),
            P(),
        ),
        check_vma=False,
    )
```

```python
import jax
import jax.numpy as jnp
from jax import lax
from jax.sharding import PartitionSpec as P

LAYERS = 2
DMAX = 8


def from_root(value, axis, root):
    mine = lax.axis_index(axis) == root
    return lax.psum(jnp.where(mine, value, jnp.zeros_like(value)), axis)


def silu_grad(value):
    sigma = jax.nn.sigmoid(value)
    return sigma * (1.0 + value * (1.0 - sigma))


def inner(left, right):
    return lax.dot_general(
        left, right, (((0,), (0,)), ((), ())), preferred_element_type=jnp.float32
    )


def spatial_forward(frames, kernel):
    count, rows, cols, chans = frames.shape
    padded = jnp.pad(frames, ((0, 0), (1, 1), (1, 1), (0, 0)))
    total = jnp.zeros((count * rows * cols, chans), jnp.float32)
    for row_tap in range(3):
        for col_tap in range(3):
            piece = padded[:, row_tap : row_tap + rows, col_tap : col_tap + cols, :].reshape(
                -1, chans
            )
            total = total + jnp.dot(
                piece, kernel[3 * row_tap + col_tap], preferred_element_type=jnp.float32
            )
    return total.reshape(frames.shape)


def spatial_back(grads, kernel):
    count, rows, cols, chans = grads.shape
    padded = jnp.pad(grads, ((0, 0), (1, 1), (1, 1), (0, 0)))
    total = jnp.zeros((count * rows * cols, chans), jnp.float32)
    for row_tap in range(3):
        for col_tap in range(3):
            piece = padded[
                :, 2 - row_tap : 2 - row_tap + rows, 2 - col_tap : 2 - col_tap + cols, :
            ].reshape(-1, chans)
            total = total + jnp.dot(
                piece, kernel[3 * row_tap + col_tap].T, preferred_element_type=jnp.float32
            )
    return total.reshape(grads.shape)


def spatial_wgrad(frames, grads):
    count, rows, cols, chans = frames.shape
    padded = jnp.pad(frames, ((0, 0), (1, 1), (1, 1), (0, 0)))
    flat_grads = grads.reshape(-1, chans)
    result = []
    for row_tap in range(3):
        for col_tap in range(3):
            piece = padded[:, row_tap : row_tap + rows, col_tap : col_tap + cols, :].reshape(
                -1, chans
            )
            result.append(inner(piece, flat_grads))
    return jnp.stack(result)


def shifted(values, offset):
    padded = jnp.pad(values, ((2 * DMAX, 2 * DMAX), (0, 0), (0, 0)))
    start = 2 * DMAX + offset
    return lax.dynamic_slice_in_dim(padded, start, values.shape[0], 0)


def temporal_forward(acts, kernel, step_size):
    chans = acts.shape[2]
    total = jnp.zeros((acts.shape[0] * acts.shape[1], chans), jnp.float32)
    for tap in range(5):
        piece = shifted(acts, (tap - 2) * step_size).reshape(-1, chans)
        total = total + jnp.dot(piece, kernel[tap], preferred_element_type=jnp.float32)
    return total.reshape(acts.shape)


def temporal_back(grads, kernel, step_size):
    chans = grads.shape[2]
    total = jnp.zeros((grads.shape[0] * grads.shape[1], chans), jnp.float32)
    for tap in range(5):
        piece = shifted(grads, (2 - tap) * step_size).reshape(-1, chans)
        total = total + jnp.dot(piece, kernel[tap].T, preferred_element_type=jnp.float32)
    return total.reshape(grads.shape)


def temporal_wgrad(acts, grads, step_size):
    chans = acts.shape[2]
    flat_grads = grads.reshape(-1, chans)
    return jnp.stack(
        [
            inner(shifted(acts, (tap - 2) * step_size).reshape(-1, chans), flat_grads)
            for tap in range(5)
        ]
    )


def to_pixels(flat):
    count = lax.axis_size(("seg", "grp"))
    chans = flat.shape[-1]
    strided = flat.reshape(-1, count, chans)
    return lax.all_to_all(strided, ("seg", "grp"), split_axis=1, concat_axis=1, tiled=True)


def to_frames(blocks):
    out = lax.all_to_all(blocks, ("seg", "grp"), split_axis=1, concat_axis=1, tiled=True)
    return out.reshape(1, -1, blocks.shape[-1])


def shifted1(values, offset):
    padded = jnp.pad(values, ((0, 0), (2 * DMAX, 2 * DMAX), (0, 0)))
    start = 2 * DMAX + offset
    return lax.dynamic_slice_in_dim(padded, start, values.shape[1], 1)


def temporal_forward1(acts, kernel, step_size):
    chans = acts.shape[2]
    total = jnp.zeros((acts.shape[0] * acts.shape[1], chans), jnp.float32)
    for tap in range(5):
        piece = shifted1(acts, (tap - 2) * step_size).reshape(-1, chans)
        total = total + jnp.dot(piece, kernel[tap], preferred_element_type=jnp.float32)
    return total.reshape(acts.shape)


def temporal_back1(grads, kernel, step_size):
    chans = grads.shape[2]
    total = jnp.zeros((grads.shape[0] * grads.shape[1], chans), jnp.float32)
    for tap in range(5):
        piece = shifted1(grads, (2 - tap) * step_size).reshape(-1, chans)
        total = total + jnp.dot(piece, kernel[tap].T, preferred_element_type=jnp.float32)
    return total.reshape(grads.shape)


def temporal_wgrad1(acts, grads, step_size):
    chans = acts.shape[2]
    flat_grads = grads.reshape(-1, chans)
    return jnp.stack(
        [
            inner(shifted1(acts, (tap - 2) * step_size).reshape(-1, chans), flat_grads)
            for tap in range(5)
        ]
    )


def all_sum(parts):
    flat = jnp.concatenate([p.reshape(-1) for p in parts])
    count = lax.axis_size(("seg", "grp"))
    chunk = flat.shape[0] // count
    pieces = lax.all_to_all(
        flat.reshape(count, chunk), ("seg", "grp"), split_axis=0, concat_axis=0, tiled=True
    )
    mine = jnp.sum(pieces, axis=0)
    spread = jnp.broadcast_to(mine[None], (count, chunk))
    whole = lax.all_to_all(spread, ("seg", "grp"), split_axis=0, concat_axis=0, tiled=True)
    whole = whole.reshape(-1)
    out = []
    offset = 0
    for p in parts:
        out.append(whole[offset : offset + p.size].reshape(p.shape))
        offset += p.size
    return out


def local(
    frames_in, spatial_weight, temporal_weight, uniting_weight, key_index, dilation, cotangent
):
    local_frames, rows, cols, chans = frames_in.shape
    pixels = rows * cols
    seg_count = lax.axis_size("seg")
    pre_spatial = spatial_forward(frames_in, spatial_weight)
    act_zero = jax.nn.silu(pre_spatial).astype(jnp.bfloat16).reshape(local_frames, pixels, chans)
    cot_local = cotangent.reshape(local_frames, pixels, chans)
    act_blocks = to_pixels(act_zero)
    cot_blocks = to_pixels(cot_local)
    acts = [act_blocks]
    block, total_frames = act_blocks.shape[0], act_blocks.shape[1]
    seg_frames = total_frames // seg_count
    pres = []
    for layer in range(LAYERS):
        pre = temporal_forward1(acts[-1], temporal_weight[layer], dilation[layer])
        pres.append(pre)
        acts.append(jax.nn.silu(pre).astype(jnp.bfloat16))
    feat = acts[-1]
    seg_shape = (block, seg_count, seg_frames, chans)
    feat_seg = feat.reshape(seg_shape)
    positions = jnp.arange(seg_frames, dtype=jnp.int32)
    onehot = positions[None, :] == key_index[:, None]
    keys = jnp.einsum(
        "ns,jnsc->jnc", onehot.astype(jnp.bfloat16), feat_seg, preferred_element_type=jnp.float32
    ).astype(jnp.bfloat16)
    key_full = jnp.broadcast_to(keys[:, :, None], seg_shape).reshape(-1, chans)
    feat_flat = feat.reshape(-1, chans)
    key_part = jnp.dot(
        keys.reshape(-1, chans), uniting_weight[1], preferred_element_type=jnp.float32
    ).reshape(block, seg_count, 1, chans)
    main_part = jnp.dot(feat_flat, uniting_weight[0], preferred_element_type=jnp.float32)
    united_blocks = (main_part.reshape(seg_shape) + key_part).astype(jnp.bfloat16)
    united = to_frames(united_blocks.reshape(block, total_frames, chans))
    cot_flat = cot_blocks.reshape(-1, chans)
    grad_feat = jnp.dot(cot_flat, uniting_weight[0].T, preferred_element_type=jnp.float32)
    seg_cot = jnp.sum(cot_blocks.reshape(seg_shape).astype(jnp.float32), axis=2)
    key_term = jnp.dot(
        seg_cot.reshape(-1, chans),
        uniting_weight[1].T.astype(jnp.float32),
        precision=lax.Precision.HIGHEST,
    ).reshape(block, seg_count, 1, chans)
    placed = onehot.astype(jnp.float32)[None, :, :, None] * key_term
    grad_feat = grad_feat.reshape(seg_shape) + placed
    grad_feat = grad_feat.reshape(block, total_frames, chans)
    grad_uniting = jnp.stack([inner(feat_flat, cot_flat), inner(key_full, cot_flat)])
    grad_pre = (grad_feat * silu_grad(pres[-1])).astype(jnp.bfloat16)
    tgrads = [None] * LAYERS
    grad_act0 = None
    for layer in range(LAYERS - 1, -1, -1):
        tgrads[layer] = temporal_wgrad1(acts[layer], grad_pre, dilation[layer])
        grad_act = temporal_back1(grad_pre, temporal_weight[layer], dilation[layer])
        if layer > 0:
            grad_pre = (grad_act * silu_grad(pres[layer - 1])).astype(jnp.bfloat16)
        else:
            grad_act0 = grad_act.astype(jnp.bfloat16)
    grad_time = to_frames(grad_act0).reshape(frames_in.shape)
    grad_spre = (grad_time.astype(jnp.float32) * silu_grad(pre_spatial)).astype(jnp.bfloat16)
    grad_frames = spatial_back(grad_spre, spatial_weight).astype(jnp.bfloat16)
    grad_spatial = spatial_wgrad(frames_in, grad_spre)
    summed = all_sum((grad_spatial, jnp.stack(tgrads), grad_uniting))
    scale = 1.0 / jnp.sqrt(jnp.float32(total_frames * pixels))
    return (
        united.reshape(frames_in.shape),
        grad_frames,
        summed[0] * scale,
        summed[1] * scale,
        summed[2] * scale,
    )


def solution(mesh):
    placed = (
        P(("seg", "grp"), None, None, None),
        P(),
        P(),
        P(),
        P(),
        P(),
        P(("seg", "grp"), None, None, None),
    )
    return jax.shard_map(
        local,
        mesh=mesh,
        in_specs=placed,
        out_specs=(
            P(("seg", "grp"), None, None, None),
            P(("seg", "grp"), None, None, None),
            P(),
            P(),
            P(),
        ),
        check_vma=False,
    )
```

```python
import jax
import jax.numpy as jnp
from jax import lax
from jax.sharding import PartitionSpec as P

LAYERS = 2
DMAX = 8


def from_root(value, axis, root):
    mine = lax.axis_index(axis) == root
    return lax.psum(jnp.where(mine, value, jnp.zeros_like(value)), axis)


def silu_grad(value):
    sigma = jax.nn.sigmoid(value)
    return sigma * (1.0 + value * (1.0 - sigma))


def inner(left, right):
    return lax.dot_general(
        left, right, (((0,), (0,)), ((), ())), preferred_element_type=jnp.float32
    )


def spatial_forward(frames, kernel):
    count, rows, cols, chans = frames.shape
    padded = jnp.pad(frames, ((0, 0), (1, 1), (1, 1), (0, 0)))
    total = jnp.zeros((count * rows * cols, chans), jnp.float32)
    for row_tap in range(3):
        for col_tap in range(3):
            piece = padded[:, row_tap : row_tap + rows, col_tap : col_tap + cols, :].reshape(
                -1, chans
            )
            total = total + jnp.dot(
                piece, kernel[3 * row_tap + col_tap], preferred_element_type=jnp.float32
            )
    return total.reshape(frames.shape)


def spatial_back(grads, kernel):
    count, rows, cols, chans = grads.shape
    padded = jnp.pad(grads, ((0, 0), (1, 1), (1, 1), (0, 0)))
    total = jnp.zeros((count * rows * cols, chans), jnp.float32)
    for row_tap in range(3):
        for col_tap in range(3):
            piece = padded[
                :, 2 - row_tap : 2 - row_tap + rows, 2 - col_tap : 2 - col_tap + cols, :
            ].reshape(-1, chans)
            total = total + jnp.dot(
                piece, kernel[3 * row_tap + col_tap].T, preferred_element_type=jnp.float32
            )
    return total.reshape(grads.shape)


def spatial_wgrad(frames, grads):
    count, rows, cols, chans = frames.shape
    padded = jnp.pad(frames, ((0, 0), (1, 1), (1, 1), (0, 0)))
    flat_grads = grads.reshape(-1, chans)
    result = []
    for row_tap in range(3):
        for col_tap in range(3):
            piece = padded[:, row_tap : row_tap + rows, col_tap : col_tap + cols, :].reshape(
                -1, chans
            )
            result.append(inner(piece, flat_grads))
    return jnp.stack(result)


def shifted(values, offset):
    padded = jnp.pad(values, ((2 * DMAX, 2 * DMAX), (0, 0), (0, 0)))
    start = 2 * DMAX + offset
    return lax.dynamic_slice_in_dim(padded, start, values.shape[0], 0)


def temporal_forward(acts, kernel, step_size):
    chans = acts.shape[2]
    total = jnp.zeros((acts.shape[0] * acts.shape[1], chans), jnp.float32)
    for tap in range(5):
        piece = shifted(acts, (tap - 2) * step_size).reshape(-1, chans)
        total = total + jnp.dot(piece, kernel[tap], preferred_element_type=jnp.float32)
    return total.reshape(acts.shape)


def temporal_back(grads, kernel, step_size):
    chans = grads.shape[2]
    total = jnp.zeros((grads.shape[0] * grads.shape[1], chans), jnp.float32)
    for tap in range(5):
        piece = shifted(grads, (2 - tap) * step_size).reshape(-1, chans)
        total = total + jnp.dot(piece, kernel[tap].T, preferred_element_type=jnp.float32)
    return total.reshape(grads.shape)


def temporal_wgrad(acts, grads, step_size):
    chans = acts.shape[2]
    flat_grads = grads.reshape(-1, chans)
    return jnp.stack(
        [
            inner(shifted(acts, (tap - 2) * step_size).reshape(-1, chans), flat_grads)
            for tap in range(5)
        ]
    )


def to_pixels(flat):
    count = lax.axis_size(("seg", "grp"))
    chans = flat.shape[-1]
    strided = flat.reshape(-1, count, chans)
    return lax.all_to_all(strided, ("seg", "grp"), split_axis=1, concat_axis=1, tiled=True)


def to_frames(blocks):
    out = lax.all_to_all(blocks, ("seg", "grp"), split_axis=1, concat_axis=1, tiled=True)
    return out.reshape(1, -1, blocks.shape[-1])


def shifted1(values, offset):
    padded = jnp.pad(values, ((0, 0), (2 * DMAX, 2 * DMAX), (0, 0)))
    start = 2 * DMAX + offset
    return lax.dynamic_slice_in_dim(padded, start, values.shape[1], 1)


def temporal_forward1(acts, kernel, step_size):
    chans = acts.shape[2]
    total = jnp.zeros((acts.shape[0] * acts.shape[1], chans), jnp.float32)
    for tap in range(5):
        piece = shifted1(acts, (tap - 2) * step_size).reshape(-1, chans)
        total = total + jnp.dot(piece, kernel[tap], preferred_element_type=jnp.float32)
    return total.reshape(acts.shape)


def temporal_back1(grads, kernel, step_size):
    chans = grads.shape[2]
    total = jnp.zeros((grads.shape[0] * grads.shape[1], chans), jnp.float32)
    for tap in range(5):
        piece = shifted1(grads, (2 - tap) * step_size).reshape(-1, chans)
        total = total + jnp.dot(piece, kernel[tap].T, preferred_element_type=jnp.float32)
    return total.reshape(grads.shape)


def temporal_wgrad1(acts, grads, step_size):
    chans = acts.shape[2]
    flat_grads = grads.reshape(-1, chans)
    return jnp.stack(
        [
            inner(shifted1(acts, (tap - 2) * step_size).reshape(-1, chans), flat_grads)
            for tap in range(5)
        ]
    )


def all_sum(parts, scale):
    flat = jnp.concatenate([p.reshape(-1) for p in parts])
    count = lax.axis_size(("seg", "grp"))
    chunk = flat.shape[0] // count
    pieces = lax.all_to_all(
        flat.reshape(count, chunk), ("seg", "grp"), split_axis=0, concat_axis=0, tiled=True
    )
    mine = jnp.sum(pieces, axis=0) * scale
    spread = jnp.broadcast_to(mine[None], (count, chunk))
    whole = lax.all_to_all(spread, ("seg", "grp"), split_axis=0, concat_axis=0, tiled=True)
    whole = whole.reshape(-1)
    out = []
    offset = 0
    for p in parts:
        out.append(whole[offset : offset + p.size].reshape(p.shape))
        offset += p.size
    return out


def local(
    frames_in, spatial_weight, temporal_weight, uniting_weight, key_index, dilation, cotangent
):
    local_frames, rows, cols, chans = frames_in.shape
    pixels = rows * cols
    seg_count = lax.axis_size("seg")
    pre_spatial = spatial_forward(frames_in, spatial_weight)
    act_zero = jax.nn.silu(pre_spatial).astype(jnp.bfloat16).reshape(local_frames, pixels, chans)
    cot_local = cotangent.reshape(local_frames, pixels, chans)
    act_blocks = to_pixels(act_zero)
    cot_blocks = to_pixels(cot_local)
    acts = [act_blocks]
    block, total_frames = act_blocks.shape[0], act_blocks.shape[1]
    seg_frames = total_frames // seg_count
    pres = []
    for layer in range(LAYERS):
        pre = temporal_forward1(acts[-1], temporal_weight[layer], dilation[layer])
        pres.append(pre)
        acts.append(jax.nn.silu(pre).astype(jnp.bfloat16))
    feat = acts[-1]
    seg_shape = (block, seg_count, seg_frames, chans)
    feat_seg = feat.reshape(seg_shape)
    positions = jnp.arange(seg_frames, dtype=jnp.int32)
    onehot = positions[None, :] == key_index[:, None]
    keys = jnp.einsum(
        "ns,jnsc->jnc", onehot.astype(jnp.bfloat16), feat_seg, preferred_element_type=jnp.float32
    ).astype(jnp.bfloat16)
    key_full = jnp.broadcast_to(keys[:, :, None], seg_shape).reshape(-1, chans)
    feat_flat = feat.reshape(-1, chans)
    key_part = jnp.dot(
        keys.reshape(-1, chans), uniting_weight[1], preferred_element_type=jnp.float32
    ).reshape(block, seg_count, 1, chans)
    main_part = jnp.dot(feat_flat, uniting_weight[0], preferred_element_type=jnp.float32)
    united_blocks = (main_part.reshape(seg_shape) + key_part).astype(jnp.bfloat16)
    united = to_frames(united_blocks.reshape(block, total_frames, chans))
    cot_flat = cot_blocks.reshape(-1, chans)
    grad_feat = jnp.dot(cot_flat, uniting_weight[0].T, preferred_element_type=jnp.float32)
    seg_cot = jnp.sum(cot_blocks.reshape(seg_shape).astype(jnp.float32), axis=2)
    key_term = jnp.dot(
        seg_cot.reshape(-1, chans),
        uniting_weight[1].T.astype(jnp.float32),
        precision=lax.Precision.HIGHEST,
    ).reshape(block, seg_count, 1, chans)
    placed = onehot.astype(jnp.float32)[None, :, :, None] * key_term
    grad_feat = grad_feat.reshape(seg_shape) + placed
    grad_feat = grad_feat.reshape(block, total_frames, chans)
    grad_uniting = jnp.stack([inner(feat_flat, cot_flat), inner(key_full, cot_flat)])
    grad_pre = (grad_feat * silu_grad(pres[-1])).astype(jnp.bfloat16)
    tgrads = [None] * LAYERS
    grad_act0 = None
    for layer in range(LAYERS - 1, -1, -1):
        tgrads[layer] = temporal_wgrad1(acts[layer], grad_pre, dilation[layer])
        grad_act = temporal_back1(grad_pre, temporal_weight[layer], dilation[layer])
        if layer > 0:
            grad_pre = (grad_act * silu_grad(pres[layer - 1])).astype(jnp.bfloat16)
        else:
            grad_act0 = grad_act.astype(jnp.bfloat16)
    scale = 1.0 / jnp.sqrt(jnp.float32(total_frames * pixels))
    grad_temporal, grad_unite = all_sum((jnp.stack(tgrads), grad_uniting), scale)
    grad_time = to_frames(grad_act0).reshape(frames_in.shape)
    grad_spre = (grad_time.astype(jnp.float32) * silu_grad(pre_spatial)).astype(jnp.bfloat16)
    grad_spatial = spatial_wgrad(frames_in, grad_spre)
    (grad_spatial,) = all_sum((grad_spatial,), scale)
    grad_frames = spatial_back(grad_spre, spatial_weight).astype(jnp.bfloat16)
    return (
        united.reshape(frames_in.shape),
        grad_frames,
        grad_spatial,
        grad_temporal,
        grad_unite,
    )


def solution(mesh):
    placed = (
        P(("seg", "grp"), None, None, None),
        P(),
        P(),
        P(),
        P(),
        P(),
        P(("seg", "grp"), None, None, None),
    )
    return jax.shard_map(
        local,
        mesh=mesh,
        in_specs=placed,
        out_specs=(
            P(("seg", "grp"), None, None, None),
            P(("seg", "grp"), None, None, None),
            P(),
            P(),
            P(),
        ),
        check_vma=False,
    )
```

```python
import functools

import jax
import jax.numpy as jnp
from jax import lax
from jax.sharding import PartitionSpec as P
from jax.experimental import pallas as pl
from jax.experimental.pallas import tpu as pltpu

LAYERS = 2
DMAX = 8


def from_root(value, axis, root):
    mine = lax.axis_index(axis) == root
    return lax.psum(jnp.where(mine, value, jnp.zeros_like(value)), axis)


def silu_grad(value):
    sigma = jax.nn.sigmoid(value)
    return sigma * (1.0 + value * (1.0 - sigma))


def inner(left, right):
    return lax.dot_general(
        left, right, (((0,), (0,)), ((), ())), preferred_element_type=jnp.float32
    )


def spatial_forward(frames, kernel):
    count, rows, cols, chans = frames.shape
    padded = jnp.pad(frames, ((0, 0), (1, 1), (1, 1), (0, 0)))
    total = jnp.zeros((count * rows * cols, chans), jnp.float32)
    for row_tap in range(3):
        for col_tap in range(3):
            piece = padded[:, row_tap : row_tap + rows, col_tap : col_tap + cols, :].reshape(
                -1, chans
            )
            total = total + jnp.dot(
                piece, kernel[3 * row_tap + col_tap], preferred_element_type=jnp.float32
            )
    return total.reshape(frames.shape)


def spatial_back(grads, kernel):
    count, rows, cols, chans = grads.shape
    padded = jnp.pad(grads, ((0, 0), (1, 1), (1, 1), (0, 0)))
    total = jnp.zeros((count * rows * cols, chans), jnp.float32)
    for row_tap in range(3):
        for col_tap in range(3):
            piece = padded[
                :, 2 - row_tap : 2 - row_tap + rows, 2 - col_tap : 2 - col_tap + cols, :
            ].reshape(-1, chans)
            total = total + jnp.dot(
                piece, kernel[3 * row_tap + col_tap].T, preferred_element_type=jnp.float32
            )
    return total.reshape(grads.shape)


def spatial_wgrad(frames, grads):
    count, rows, cols, chans = frames.shape
    padded = jnp.pad(frames, ((0, 0), (1, 1), (1, 1), (0, 0)))
    flat_grads = grads.reshape(-1, chans)
    result = []
    for row_tap in range(3):
        for col_tap in range(3):
            piece = padded[:, row_tap : row_tap + rows, col_tap : col_tap + cols, :].reshape(
                -1, chans
            )
            result.append(inner(piece, flat_grads))
    return jnp.stack(result)


def shifted(values, offset):
    padded = jnp.pad(values, ((2 * DMAX, 2 * DMAX), (0, 0), (0, 0)))
    start = 2 * DMAX + offset
    return lax.dynamic_slice_in_dim(padded, start, values.shape[0], 0)


def temporal_forward(acts, kernel, step_size):
    chans = acts.shape[2]
    total = jnp.zeros((acts.shape[0] * acts.shape[1], chans), jnp.float32)
    for tap in range(5):
        piece = shifted(acts, (tap - 2) * step_size).reshape(-1, chans)
        total = total + jnp.dot(piece, kernel[tap], preferred_element_type=jnp.float32)
    return total.reshape(acts.shape)


def temporal_back(grads, kernel, step_size):
    chans = grads.shape[2]
    total = jnp.zeros((grads.shape[0] * grads.shape[1], chans), jnp.float32)
    for tap in range(5):
        piece = shifted(grads, (2 - tap) * step_size).reshape(-1, chans)
        total = total + jnp.dot(piece, kernel[tap].T, preferred_element_type=jnp.float32)
    return total.reshape(grads.shape)


def temporal_wgrad(acts, grads, step_size):
    chans = acts.shape[2]
    flat_grads = grads.reshape(-1, chans)
    return jnp.stack(
        [
            inner(shifted(acts, (tap - 2) * step_size).reshape(-1, chans), flat_grads)
            for tap in range(5)
        ]
    )


def to_pixels(flat):
    count = lax.axis_size(("seg", "grp"))
    chans = flat.shape[-1]
    strided = flat.reshape(-1, count, chans)
    return lax.all_to_all(strided, ("seg", "grp"), split_axis=1, concat_axis=1, tiled=True)


def to_frames(blocks):
    out = lax.all_to_all(blocks, ("seg", "grp"), split_axis=1, concat_axis=1, tiled=True)
    return out.reshape(1, -1, blocks.shape[-1])


def shifted1(values, offset):
    padded = jnp.pad(values, ((0, 0), (2 * DMAX, 2 * DMAX), (0, 0)))
    start = 2 * DMAX + offset
    return lax.dynamic_slice_in_dim(padded, start, values.shape[1], 1)


def temporal_forward1(acts, kernel, step_size):
    chans = acts.shape[2]
    total = jnp.zeros((acts.shape[0] * acts.shape[1], chans), jnp.float32)
    for tap in range(5):
        piece = shifted1(acts, (tap - 2) * step_size).reshape(-1, chans)
        total = total + jnp.dot(piece, kernel[tap], preferred_element_type=jnp.float32)
    return total.reshape(acts.shape)


def temporal_back1(grads, kernel, step_size):
    chans = grads.shape[2]
    total = jnp.zeros((grads.shape[0] * grads.shape[1], chans), jnp.float32)
    for tap in range(5):
        piece = shifted1(grads, (2 - tap) * step_size).reshape(-1, chans)
        total = total + jnp.dot(piece, kernel[tap].T, preferred_element_type=jnp.float32)
    return total.reshape(grads.shape)


def temporal_wgrad1(acts, grads, step_size):
    chans = acts.shape[2]
    flat_grads = grads.reshape(-1, chans)
    return jnp.stack(
        [
            inner(shifted1(acts, (tap - 2) * step_size).reshape(-1, chans), flat_grads)
            for tap in range(5)
        ]
    )


JB = 10


def shift_matrix(offset, size):
    rows = lax.broadcasted_iota(jnp.int32, (size, size), 0)
    cols = lax.broadcasted_iota(jnp.int32, (size, size), 1)
    return (cols == rows + offset).astype(jnp.bfloat16)


def shifted_taps(x_ref, step, sign):
    blocks, frames, chans = x_ref.shape
    wide = jnp.concatenate([x_ref[j] for j in range(blocks)], axis=1)
    taps = []
    for tap in range(5):
        if tap == 2:
            taps.append(None)
            continue
        moved = jnp.dot(
            shift_matrix(sign * (tap - 2) * step, frames), wide,
            preferred_element_type=jnp.float32,
        ).astype(jnp.bfloat16)
        taps.append(moved)
    rows = []
    for j in range(blocks):
        parts = []
        for tap in range(5):
            if tap == 2:
                parts.append(x_ref[j])
            else:
                parts.append(taps[tap][:, j * chans : (j + 1) * chans])
        rows.append(jnp.concatenate(parts, axis=1))
    return jnp.concatenate(rows, axis=0)


def tfwd_kernel(dil_ref, act_ref, w_ref, pre_ref, out_ref):
    blocks, frames, chans = act_ref.shape
    stacked = shifted_taps(act_ref, dil_ref[0], 1)
    pre = jnp.dot(stacked, w_ref[...], preferred_element_type=jnp.float32)
    pre_ref[...] = pre.reshape(blocks, frames, chans)
    out_ref[...] = (pre / (1.0 + jnp.exp(-pre))).astype(jnp.bfloat16).reshape(blocks, frames, chans)


def temporal_forward_k(acts, kernel, step_size):
    count, frames, chans = acts.shape
    spec = pl.BlockSpec((JB, frames, chans), lambda j, d: (j, 0, 0))
    return pl.pallas_call(
        tfwd_kernel,
        grid_spec=pltpu.PrefetchScalarGridSpec(
            num_scalar_prefetch=1,
            grid=(count // JB,),
            in_specs=[spec, pl.BlockSpec((5 * chans, chans), lambda j, d: (0, 0))],
            out_specs=[spec, spec],
        ),
        out_shape=[
            jax.ShapeDtypeStruct(acts.shape, jnp.float32),
            jax.ShapeDtypeStruct(acts.shape, jnp.bfloat16),
        ],
    )(step_size.reshape(1), acts, kernel.reshape(5 * chans, chans))


def tbwd_kernel(with_pre, dil_ref, act_ref, grad_ref, wt_ref, *rest):
    if with_pre:
        pre_ref, out_ref, tg_ref = rest
    else:
        out_ref, tg_ref = rest
    blocks, frames, chans = act_ref.shape
    stacked = shifted_taps(grad_ref, dil_ref[0], -1)
    grad_act = jnp.dot(stacked, wt_ref[...], preferred_element_type=jnp.float32)
    flat_act = act_ref[...].reshape(blocks * frames, chans)
    part = lax.dot_general(
        flat_act, stacked, (((0,), (0,)), ((), ())), preferred_element_type=jnp.float32
    )

    @pl.when(pl.program_id(0) == 0)
    def _():
        tg_ref[...] = jnp.zeros_like(tg_ref)

    tg_ref[...] += part
    if with_pre:
        pre = pre_ref[...].reshape(blocks * frames, chans)
        sigma = 1.0 / (1.0 + jnp.exp(-pre))
        grad_act = grad_act * (sigma * (1.0 + pre * (1.0 - sigma)))
    out_ref[...] = grad_act.astype(jnp.bfloat16).reshape(blocks, frames, chans)


def temporal_backward_k(acts, grads, kernel, step_size, pre_below):
    count, frames, chans = acts.shape
    spec = pl.BlockSpec((JB, frames, chans), lambda j, d: (j, 0, 0))
    wt = jnp.concatenate([kernel[tap].T for tap in range(5)], axis=0)
    with_pre = pre_below is not None
    in_specs = [spec, spec, pl.BlockSpec((5 * chans, chans), lambda j, d: (0, 0))]
    operands = [step_size.reshape(1), acts, grads, wt]
    if with_pre:
        in_specs.append(spec)
        operands.append(pre_below)
    out, tg = pl.pallas_call(
        functools.partial(tbwd_kernel, with_pre),
        grid_spec=pltpu.PrefetchScalarGridSpec(
            num_scalar_prefetch=1,
            grid=(count // JB,),
            in_specs=in_specs,
            out_specs=[spec, pl.BlockSpec((chans, 5 * chans), lambda j, d: (0, 0))],
        ),
        out_shape=[
            jax.ShapeDtypeStruct(acts.shape, jnp.bfloat16),
            jax.ShapeDtypeStruct((chans, 5 * chans), jnp.float32),
        ],
        compiler_params=pltpu.CompilerParams(dimension_semantics=("arbitrary",)),
    )(*operands)
    tgrad = tg.reshape(chans, 5, chans).transpose(1, 0, 2)
    return out, tgrad


def all_sum(parts, scale):
    flat = jnp.concatenate([p.reshape(-1) for p in parts])
    count = lax.axis_size(("seg", "grp"))
    chunk = flat.shape[0] // count
    pieces = lax.all_to_all(
        flat.reshape(count, chunk), ("seg", "grp"), split_axis=0, concat_axis=0, tiled=True
    )
    mine = jnp.sum(pieces, axis=0) * scale
    spread = jnp.broadcast_to(mine[None], (count, chunk))
    whole = lax.all_to_all(spread, ("seg", "grp"), split_axis=0, concat_axis=0, tiled=True)
    whole = whole.reshape(-1)
    out = []
    offset = 0
    for p in parts:
        out.append(whole[offset : offset + p.size].reshape(p.shape))
        offset += p.size
    return out


def local(
    frames_in, spatial_weight, temporal_weight, uniting_weight, key_index, dilation, cotangent
):
    local_frames, rows, cols, chans = frames_in.shape
    pixels = rows * cols
    seg_count = lax.axis_size("seg")
    pre_spatial = spatial_forward(frames_in, spatial_weight)
    act_zero = jax.nn.silu(pre_spatial).astype(jnp.bfloat16).reshape(local_frames, pixels, chans)
    cot_local = cotangent.reshape(local_frames, pixels, chans)
    act_blocks = to_pixels(act_zero)
    cot_blocks = to_pixels(cot_local)
    acts = [act_blocks]
    block, total_frames = act_blocks.shape[0], act_blocks.shape[1]
    seg_frames = total_frames // seg_count
    pres = []
    for layer in range(LAYERS):
        pre, act = temporal_forward_k(acts[-1], temporal_weight[layer], dilation[layer])
        pres.append(pre)
        acts.append(act)
    feat = acts[-1]
    seg_shape = (block, seg_count, seg_frames, chans)
    feat_seg = feat.reshape(seg_shape)
    positions = jnp.arange(seg_frames, dtype=jnp.int32)
    onehot = positions[None, :] == key_index[:, None]
    keys = jnp.einsum(
        "ns,jnsc->jnc", onehot.astype(jnp.bfloat16), feat_seg, preferred_element_type=jnp.float32
    ).astype(jnp.bfloat16)
    key_full = jnp.broadcast_to(keys[:, :, None], seg_shape).reshape(-1, chans)
    feat_flat = feat.reshape(-1, chans)
    key_part = jnp.dot(
        keys.reshape(-1, chans), uniting_weight[1], preferred_element_type=jnp.float32
    ).reshape(block, seg_count, 1, chans)
    main_part = jnp.dot(feat_flat, uniting_weight[0], preferred_element_type=jnp.float32)
    united_blocks = (main_part.reshape(seg_shape) + key_part).astype(jnp.bfloat16)
    united = to_frames(united_blocks.reshape(block, total_frames, chans))
    cot_flat = cot_blocks.reshape(-1, chans)
    grad_feat = jnp.dot(cot_flat, uniting_weight[0].T, preferred_element_type=jnp.float32)
    seg_cot = jnp.sum(cot_blocks.reshape(seg_shape).astype(jnp.float32), axis=2)
    key_term = jnp.dot(
        seg_cot.reshape(-1, chans),
        uniting_weight[1].T.astype(jnp.float32),
        precision=lax.Precision.HIGHEST,
    ).reshape(block, seg_count, 1, chans)
    placed = onehot.astype(jnp.float32)[None, :, :, None] * key_term
    grad_feat = grad_feat.reshape(seg_shape) + placed
    grad_feat = grad_feat.reshape(block, total_frames, chans)
    grad_uniting = jnp.stack([inner(feat_flat, cot_flat), inner(key_full, cot_flat)])
    grad_pre = (grad_feat * silu_grad(pres[-1])).astype(jnp.bfloat16)
    tgrads = [None] * LAYERS
    for layer in range(LAYERS - 1, -1, -1):
        below = pres[layer - 1] if layer > 0 else None
        grad_pre, tgrads[layer] = temporal_backward_k(
            acts[layer], grad_pre, temporal_weight[layer], dilation[layer], below
        )
    grad_act0 = grad_pre
    grad_time = to_frames(grad_act0).reshape(frames_in.shape)
    grad_spre = (grad_time.astype(jnp.float32) * silu_grad(pre_spatial)).astype(jnp.bfloat16)
    grad_frames = spatial_back(grad_spre, spatial_weight).astype(jnp.bfloat16)
    grad_spatial = spatial_wgrad(frames_in, grad_spre)
    scale = 1.0 / jnp.sqrt(jnp.float32(total_frames * pixels))
    summed = all_sum((grad_spatial, jnp.stack(tgrads), grad_uniting), scale)
    return (
        united.reshape(frames_in.shape),
        grad_frames,
        summed[0],
        summed[1],
        summed[2],
    )


def solution(mesh):
    placed = (
        P(("seg", "grp"), None, None, None),
        P(),
        P(),
        P(),
        P(),
        P(),
        P(("seg", "grp"), None, None, None),
    )
    return jax.shard_map(
        local,
        mesh=mesh,
        in_specs=placed,
        out_specs=(
            P(("seg", "grp"), None, None, None),
            P(("seg", "grp"), None, None, None),
            P(),
            P(),
            P(),
        ),
        check_vma=False,
    )
```

```python
import functools

import jax
import jax.numpy as jnp
from jax import lax
from jax.sharding import PartitionSpec as P
from jax.experimental import pallas as pl
from jax.experimental.pallas import tpu as pltpu

LAYERS = 2
DMAX = 8


def from_root(value, axis, root):
    mine = lax.axis_index(axis) == root
    return lax.psum(jnp.where(mine, value, jnp.zeros_like(value)), axis)


def silu_grad(value):
    sigma = jax.nn.sigmoid(value)
    return sigma * (1.0 + value * (1.0 - sigma))


def inner(left, right):
    return lax.dot_general(
        left, right, (((0,), (0,)), ((), ())), preferred_element_type=jnp.float32
    )


def spatial_forward(frames, kernel):
    count, rows, cols, chans = frames.shape
    padded = jnp.pad(frames, ((0, 0), (1, 1), (1, 1), (0, 0)))
    total = jnp.zeros((count * rows * cols, chans), jnp.float32)
    for row_tap in range(3):
        for col_tap in range(3):
            piece = padded[:, row_tap : row_tap + rows, col_tap : col_tap + cols, :].reshape(
                -1, chans
            )
            total = total + jnp.dot(
                piece, kernel[3 * row_tap + col_tap], preferred_element_type=jnp.float32
            )
    return total.reshape(frames.shape)


def spatial_back(grads, kernel):
    count, rows, cols, chans = grads.shape
    padded = jnp.pad(grads, ((0, 0), (1, 1), (1, 1), (0, 0)))
    total = jnp.zeros((count * rows * cols, chans), jnp.float32)
    for row_tap in range(3):
        for col_tap in range(3):
            piece = padded[
                :, 2 - row_tap : 2 - row_tap + rows, 2 - col_tap : 2 - col_tap + cols, :
            ].reshape(-1, chans)
            total = total + jnp.dot(
                piece, kernel[3 * row_tap + col_tap].T, preferred_element_type=jnp.float32
            )
    return total.reshape(grads.shape)


def spatial_wgrad(frames, grads):
    count, rows, cols, chans = frames.shape
    padded = jnp.pad(frames, ((0, 0), (1, 1), (1, 1), (0, 0)))
    flat_grads = grads.reshape(-1, chans)
    result = []
    for row_tap in range(3):
        for col_tap in range(3):
            piece = padded[:, row_tap : row_tap + rows, col_tap : col_tap + cols, :].reshape(
                -1, chans
            )
            result.append(inner(piece, flat_grads))
    return jnp.stack(result)


def shifted(values, offset):
    padded = jnp.pad(values, ((2 * DMAX, 2 * DMAX), (0, 0), (0, 0)))
    start = 2 * DMAX + offset
    return lax.dynamic_slice_in_dim(padded, start, values.shape[0], 0)


def temporal_forward(acts, kernel, step_size):
    chans = acts.shape[2]
    total = jnp.zeros((acts.shape[0] * acts.shape[1], chans), jnp.float32)
    for tap in range(5):
        piece = shifted(acts, (tap - 2) * step_size).reshape(-1, chans)
        total = total + jnp.dot(piece, kernel[tap], preferred_element_type=jnp.float32)
    return total.reshape(acts.shape)


def temporal_back(grads, kernel, step_size):
    chans = grads.shape[2]
    total = jnp.zeros((grads.shape[0] * grads.shape[1], chans), jnp.float32)
    for tap in range(5):
        piece = shifted(grads, (2 - tap) * step_size).reshape(-1, chans)
        total = total + jnp.dot(piece, kernel[tap].T, preferred_element_type=jnp.float32)
    return total.reshape(grads.shape)


def temporal_wgrad(acts, grads, step_size):
    chans = acts.shape[2]
    flat_grads = grads.reshape(-1, chans)
    return jnp.stack(
        [
            inner(shifted(acts, (tap - 2) * step_size).reshape(-1, chans), flat_grads)
            for tap in range(5)
        ]
    )


def to_pixels(flat):
    count = lax.axis_size(("seg", "grp"))
    chans = flat.shape[-1]
    strided = flat.reshape(-1, count, chans)
    return lax.all_to_all(strided, ("seg", "grp"), split_axis=1, concat_axis=1, tiled=True)


def to_frames(blocks):
    out = lax.all_to_all(blocks, ("seg", "grp"), split_axis=1, concat_axis=1, tiled=True)
    return out.reshape(1, -1, blocks.shape[-1])


def shifted1(values, offset):
    padded = jnp.pad(values, ((0, 0), (2 * DMAX, 2 * DMAX), (0, 0)))
    start = 2 * DMAX + offset
    return lax.dynamic_slice_in_dim(padded, start, values.shape[1], 1)


def temporal_forward1(acts, kernel, step_size):
    chans = acts.shape[2]
    total = jnp.zeros((acts.shape[0] * acts.shape[1], chans), jnp.float32)
    for tap in range(5):
        piece = shifted1(acts, (tap - 2) * step_size).reshape(-1, chans)
        total = total + jnp.dot(piece, kernel[tap], preferred_element_type=jnp.float32)
    return total.reshape(acts.shape)


def temporal_back1(grads, kernel, step_size):
    chans = grads.shape[2]
    total = jnp.zeros((grads.shape[0] * grads.shape[1], chans), jnp.float32)
    for tap in range(5):
        piece = shifted1(grads, (2 - tap) * step_size).reshape(-1, chans)
        total = total + jnp.dot(piece, kernel[tap].T, preferred_element_type=jnp.float32)
    return total.reshape(grads.shape)


def temporal_wgrad1(acts, grads, step_size):
    chans = acts.shape[2]
    flat_grads = grads.reshape(-1, chans)
    return jnp.stack(
        [
            inner(shifted1(acts, (tap - 2) * step_size).reshape(-1, chans), flat_grads)
            for tap in range(5)
        ]
    )


JB = 10


def shift_matrix(offset, size):
    rows = lax.broadcasted_iota(jnp.int32, (size, size), 0)
    cols = lax.broadcasted_iota(jnp.int32, (size, size), 1)
    return (cols == rows + offset).astype(jnp.bfloat16)


def shifted_taps(x_ref, step, sign):
    blocks, frames, chans = x_ref.shape
    wide = jnp.concatenate([x_ref[j] for j in range(blocks)], axis=1)
    taps = []
    for tap in range(5):
        if tap == 2:
            taps.append(None)
            continue
        moved = jnp.dot(
            shift_matrix(sign * (tap - 2) * step, frames), wide,
            preferred_element_type=jnp.float32,
        ).astype(jnp.bfloat16)
        taps.append(moved)
    rows = []
    for j in range(blocks):
        parts = []
        for tap in range(5):
            if tap == 2:
                parts.append(x_ref[j])
            else:
                parts.append(taps[tap][:, j * chans : (j + 1) * chans])
        rows.append(jnp.concatenate(parts, axis=1))
    return jnp.concatenate(rows, axis=0)


def tfwd_kernel(dil_ref, act_ref, w_ref, pre_ref, out_ref):
    blocks, frames, chans = act_ref.shape
    stacked = shifted_taps(act_ref, dil_ref[0], 1)
    pre = jnp.dot(stacked, w_ref[...], preferred_element_type=jnp.float32)
    pre_ref[...] = pre.reshape(blocks, frames, chans)
    out_ref[...] = (pre / (1.0 + jnp.exp(-pre))).astype(jnp.bfloat16).reshape(blocks, frames, chans)


def temporal_forward_k(acts, kernel, step_size):
    count, frames, chans = acts.shape
    spec = pl.BlockSpec((JB, frames, chans), lambda j, d: (j, 0, 0))
    return pl.pallas_call(
        tfwd_kernel,
        grid_spec=pltpu.PrefetchScalarGridSpec(
            num_scalar_prefetch=1,
            grid=(count // JB,),
            in_specs=[spec, pl.BlockSpec((5 * chans, chans), lambda j, d: (0, 0))],
            out_specs=[spec, spec],
        ),
        out_shape=[
            jax.ShapeDtypeStruct(acts.shape, jnp.float32),
            jax.ShapeDtypeStruct(acts.shape, jnp.bfloat16),
        ],
    )(step_size.reshape(1), acts, kernel.reshape(5 * chans, chans))


def tbwd_kernel(with_pre, dil_ref, act_ref, grad_ref, wt_ref, *rest):
    if with_pre:
        pre_ref, out_ref, tg_ref = rest
    else:
        out_ref, tg_ref = rest
    blocks, frames, chans = act_ref.shape
    stacked = shifted_taps(grad_ref, dil_ref[0], -1)
    grad_act = jnp.dot(stacked, wt_ref[...], preferred_element_type=jnp.float32)
    flat_act = act_ref[...].reshape(blocks * frames, chans)
    part = lax.dot_general(
        flat_act, stacked, (((0,), (0,)), ((), ())), preferred_element_type=jnp.float32
    )

    @pl.when(pl.program_id(0) == 0)
    def _():
        tg_ref[...] = jnp.zeros_like(tg_ref)

    tg_ref[...] += part
    if with_pre:
        pre = pre_ref[...].reshape(blocks * frames, chans)
        sigma = 1.0 / (1.0 + jnp.exp(-pre))
        grad_act = grad_act * (sigma * (1.0 + pre * (1.0 - sigma)))
    out_ref[...] = grad_act.astype(jnp.bfloat16).reshape(blocks, frames, chans)


def temporal_backward_k(acts, grads, kernel, step_size, pre_below):
    count, frames, chans = acts.shape
    spec = pl.BlockSpec((JB, frames, chans), lambda j, d: (j, 0, 0))
    wt = jnp.concatenate([kernel[tap].T for tap in range(5)], axis=0)
    with_pre = pre_below is not None
    in_specs = [spec, spec, pl.BlockSpec((5 * chans, chans), lambda j, d: (0, 0))]
    operands = [step_size.reshape(1), acts, grads, wt]
    if with_pre:
        in_specs.append(spec)
        operands.append(pre_below)
    out, tg = pl.pallas_call(
        functools.partial(tbwd_kernel, with_pre),
        grid_spec=pltpu.PrefetchScalarGridSpec(
            num_scalar_prefetch=1,
            grid=(count // JB,),
            in_specs=in_specs,
            out_specs=[spec, pl.BlockSpec((chans, 5 * chans), lambda j, d: (0, 0))],
        ),
        out_shape=[
            jax.ShapeDtypeStruct(acts.shape, jnp.bfloat16),
            jax.ShapeDtypeStruct((chans, 5 * chans), jnp.float32),
        ],
        compiler_params=pltpu.CompilerParams(dimension_semantics=("arbitrary",)),
    )(*operands)
    tgrad = tg.reshape(chans, 5, chans).transpose(1, 0, 2)
    return out, tgrad


def all_sum(parts, scale):
    flat = jnp.concatenate([p.reshape(-1) for p in parts])
    count = lax.axis_size(("seg", "grp"))
    chunk = flat.shape[0] // count
    pieces = lax.all_to_all(
        flat.reshape(count, chunk), ("seg", "grp"), split_axis=0, concat_axis=0, tiled=True
    )
    mine = jnp.sum(pieces, axis=0) * scale
    spread = jnp.broadcast_to(mine[None], (count, chunk))
    whole = lax.all_to_all(spread, ("seg", "grp"), split_axis=0, concat_axis=0, tiled=True)
    whole = whole.reshape(-1)
    out = []
    offset = 0
    for p in parts:
        out.append(whole[offset : offset + p.size].reshape(p.shape))
        offset += p.size
    return out


def local(
    frames_in, spatial_weight, temporal_weight, uniting_weight, key_index, dilation, cotangent
):
    local_frames, rows, cols, chans = frames_in.shape
    pixels = rows * cols
    seg_count = lax.axis_size("seg")
    pre_spatial = spatial_forward(frames_in, spatial_weight)
    act_zero = jax.nn.silu(pre_spatial).astype(jnp.bfloat16).reshape(local_frames, pixels, chans)
    cot_local = cotangent.reshape(local_frames, pixels, chans)
    act_blocks = to_pixels(act_zero)
    cot_blocks = to_pixels(cot_local)
    acts = [act_blocks]
    block, total_frames = act_blocks.shape[0], act_blocks.shape[1]
    seg_frames = total_frames // seg_count
    pres = []
    for layer in range(LAYERS):
        pre, act = temporal_forward_k(acts[-1], temporal_weight[layer], dilation[layer])
        pres.append(pre)
        acts.append(act)
    feat = acts[-1]
    seg_shape = (block, seg_count, seg_frames, chans)
    feat_seg = feat.reshape(seg_shape)
    positions = jnp.arange(seg_frames, dtype=jnp.int32)
    onehot = positions[None, :] == key_index[:, None]
    keys = jnp.einsum(
        "ns,jnsc->jnc", onehot.astype(jnp.bfloat16), feat_seg, preferred_element_type=jnp.float32
    ).astype(jnp.bfloat16)
    key_full = jnp.broadcast_to(keys[:, :, None], seg_shape).reshape(-1, chans)
    feat_flat = feat.reshape(-1, chans)
    key_part = jnp.dot(
        keys.reshape(-1, chans), uniting_weight[1], preferred_element_type=jnp.float32
    ).reshape(block, seg_count, 1, chans)
    main_part = jnp.dot(feat_flat, uniting_weight[0], preferred_element_type=jnp.float32)
    united_blocks = (main_part.reshape(seg_shape) + key_part).astype(jnp.bfloat16)
    united = to_frames(united_blocks.reshape(block, total_frames, chans))
    cot_flat = cot_blocks.reshape(-1, chans)
    grad_feat = jnp.dot(cot_flat, uniting_weight[0].T, preferred_element_type=jnp.float32)
    seg_cot = jnp.sum(cot_blocks.reshape(seg_shape).astype(jnp.float32), axis=2)
    key_term = jnp.dot(
        seg_cot.reshape(-1, chans),
        uniting_weight[1].T.astype(jnp.float32),
        precision=lax.Precision.HIGHEST,
    ).reshape(block, seg_count, 1, chans)
    placed = onehot.astype(jnp.float32)[None, :, :, None] * key_term
    grad_feat = grad_feat.reshape(seg_shape) + placed
    grad_feat = grad_feat.reshape(block, total_frames, chans)
    grad_uniting = jnp.stack([inner(feat_flat, cot_flat), inner(key_full, cot_flat)])
    grad_pre = (grad_feat * silu_grad(pres[-1])).astype(jnp.bfloat16)
    tgrads = [None] * LAYERS
    for layer in range(LAYERS - 1, -1, -1):
        below = pres[layer - 1] if layer > 0 else None
        grad_pre, tgrads[layer] = temporal_backward_k(
            acts[layer], grad_pre, temporal_weight[layer], dilation[layer], below
        )
    grad_act0 = grad_pre
    scale = 1.0 / jnp.sqrt(jnp.float32(total_frames * pixels))
    early = lax.psum((jnp.stack(tgrads), grad_uniting), ("seg", "grp"))
    grad_time = to_frames(grad_act0).reshape(frames_in.shape)
    grad_spre = (grad_time.astype(jnp.float32) * silu_grad(pre_spatial)).astype(jnp.bfloat16)
    grad_frames = spatial_back(grad_spre, spatial_weight).astype(jnp.bfloat16)
    grad_spatial = spatial_wgrad(frames_in, grad_spre)
    (summed,) = all_sum((grad_spatial,), scale)
    return (
        united.reshape(frames_in.shape),
        grad_frames,
        summed,
        early[0] * scale,
        early[1] * scale,
    )


def solution(mesh):
    placed = (
        P(("seg", "grp"), None, None, None),
        P(),
        P(),
        P(),
        P(),
        P(),
        P(("seg", "grp"), None, None, None),
    )
    return jax.shard_map(
        local,
        mesh=mesh,
        in_specs=placed,
        out_specs=(
            P(("seg", "grp"), None, None, None),
            P(("seg", "grp"), None, None, None),
            P(),
            P(),
            P(),
        ),
        check_vma=False,
    )
```

```python
import functools

import jax
import jax.numpy as jnp
from jax import lax
from jax.sharding import PartitionSpec as P
from jax.experimental import pallas as pl
from jax.experimental.pallas import tpu as pltpu

LAYERS = 2
DMAX = 8


def from_root(value, axis, root):
    mine = lax.axis_index(axis) == root
    return lax.psum(jnp.where(mine, value, jnp.zeros_like(value)), axis)


def silu_grad(value):
    sigma = jax.nn.sigmoid(value)
    return sigma * (1.0 + value * (1.0 - sigma))


def inner(left, right):
    return lax.dot_general(
        left, right, (((0,), (0,)), ((), ())), preferred_element_type=jnp.float32
    )


def spatial_forward(frames, kernel):
    count, rows, cols, chans = frames.shape
    padded = jnp.pad(frames, ((0, 0), (1, 1), (1, 1), (0, 0)))
    total = jnp.zeros((count * rows * cols, chans), jnp.float32)
    for row_tap in range(3):
        for col_tap in range(3):
            piece = padded[:, row_tap : row_tap + rows, col_tap : col_tap + cols, :].reshape(
                -1, chans
            )
            total = total + jnp.dot(
                piece, kernel[3 * row_tap + col_tap], preferred_element_type=jnp.float32
            )
    return total.reshape(frames.shape)


def spatial_back(grads, kernel):
    count, rows, cols, chans = grads.shape
    padded = jnp.pad(grads, ((0, 0), (1, 1), (1, 1), (0, 0)))
    total = jnp.zeros((count * rows * cols, chans), jnp.float32)
    for row_tap in range(3):
        for col_tap in range(3):
            piece = padded[
                :, 2 - row_tap : 2 - row_tap + rows, 2 - col_tap : 2 - col_tap + cols, :
            ].reshape(-1, chans)
            total = total + jnp.dot(
                piece, kernel[3 * row_tap + col_tap].T, preferred_element_type=jnp.float32
            )
    return total.reshape(grads.shape)


def spatial_wgrad(frames, grads):
    count, rows, cols, chans = frames.shape
    padded = jnp.pad(frames, ((0, 0), (1, 1), (1, 1), (0, 0)))
    flat_grads = grads.reshape(-1, chans)
    result = []
    for row_tap in range(3):
        for col_tap in range(3):
            piece = padded[:, row_tap : row_tap + rows, col_tap : col_tap + cols, :].reshape(
                -1, chans
            )
            result.append(inner(piece, flat_grads))
    return jnp.stack(result)


def shifted(values, offset):
    padded = jnp.pad(values, ((2 * DMAX, 2 * DMAX), (0, 0), (0, 0)))
    start = 2 * DMAX + offset
    return lax.dynamic_slice_in_dim(padded, start, values.shape[0], 0)


def temporal_forward(acts, kernel, step_size):
    chans = acts.shape[2]
    total = jnp.zeros((acts.shape[0] * acts.shape[1], chans), jnp.float32)
    for tap in range(5):
        piece = shifted(acts, (tap - 2) * step_size).reshape(-1, chans)
        total = total + jnp.dot(piece, kernel[tap], preferred_element_type=jnp.float32)
    return total.reshape(acts.shape)


def temporal_back(grads, kernel, step_size):
    chans = grads.shape[2]
    total = jnp.zeros((grads.shape[0] * grads.shape[1], chans), jnp.float32)
    for tap in range(5):
        piece = shifted(grads, (2 - tap) * step_size).reshape(-1, chans)
        total = total + jnp.dot(piece, kernel[tap].T, preferred_element_type=jnp.float32)
    return total.reshape(grads.shape)


def temporal_wgrad(acts, grads, step_size):
    chans = acts.shape[2]
    flat_grads = grads.reshape(-1, chans)
    return jnp.stack(
        [
            inner(shifted(acts, (tap - 2) * step_size).reshape(-1, chans), flat_grads)
            for tap in range(5)
        ]
    )


def to_pixels(flat):
    count = lax.axis_size(("seg", "grp"))
    chans = flat.shape[-1]
    strided = flat.reshape(-1, count, chans)
    return lax.all_to_all(strided, ("seg", "grp"), split_axis=1, concat_axis=1, tiled=True)


def to_frames(blocks):
    out = lax.all_to_all(blocks, ("seg", "grp"), split_axis=1, concat_axis=1, tiled=True)
    return out.reshape(1, -1, blocks.shape[-1])


def shifted1(values, offset):
    padded = jnp.pad(values, ((0, 0), (2 * DMAX, 2 * DMAX), (0, 0)))
    start = 2 * DMAX + offset
    return lax.dynamic_slice_in_dim(padded, start, values.shape[1], 1)


def temporal_forward1(acts, kernel, step_size):
    chans = acts.shape[2]
    total = jnp.zeros((acts.shape[0] * acts.shape[1], chans), jnp.float32)
    for tap in range(5):
        piece = shifted1(acts, (tap - 2) * step_size).reshape(-1, chans)
        total = total + jnp.dot(piece, kernel[tap], preferred_element_type=jnp.float32)
    return total.reshape(acts.shape)


def temporal_back1(grads, kernel, step_size):
    chans = grads.shape[2]
    total = jnp.zeros((grads.shape[0] * grads.shape[1], chans), jnp.float32)
    for tap in range(5):
        piece = shifted1(grads, (2 - tap) * step_size).reshape(-1, chans)
        total = total + jnp.dot(piece, kernel[tap].T, preferred_element_type=jnp.float32)
    return total.reshape(grads.shape)


def temporal_wgrad1(acts, grads, step_size):
    chans = acts.shape[2]
    flat_grads = grads.reshape(-1, chans)
    return jnp.stack(
        [
            inner(shifted1(acts, (tap - 2) * step_size).reshape(-1, chans), flat_grads)
            for tap in range(5)
        ]
    )


JB = 15


def shift_matrix(offset, size):
    rows = lax.broadcasted_iota(jnp.int32, (size, size), 0)
    cols = lax.broadcasted_iota(jnp.int32, (size, size), 1)
    return (cols == rows + offset).astype(jnp.bfloat16)


def shifted_taps(x_ref, step, sign):
    blocks, frames, chans = x_ref.shape
    wide = jnp.concatenate([x_ref[j] for j in range(blocks)], axis=1)
    taps = []
    for tap in range(5):
        if tap == 2:
            taps.append(None)
            continue
        moved = jnp.dot(
            shift_matrix(sign * (tap - 2) * step, frames), wide,
            preferred_element_type=jnp.float32,
        ).astype(jnp.bfloat16)
        taps.append(moved)
    rows = []
    for j in range(blocks):
        parts = []
        for tap in range(5):
            if tap == 2:
                parts.append(x_ref[j])
            else:
                parts.append(taps[tap][:, j * chans : (j + 1) * chans])
        rows.append(jnp.concatenate(parts, axis=1))
    return jnp.concatenate(rows, axis=0)


def tfwd_kernel(dil_ref, act_ref, w_ref, pre_ref, out_ref):
    blocks, frames, chans = act_ref.shape
    stacked = shifted_taps(act_ref, dil_ref[0], 1)
    pre = jnp.dot(stacked, w_ref[...], preferred_element_type=jnp.float32)
    pre_ref[...] = pre.reshape(blocks, frames, chans)
    out_ref[...] = (pre / (1.0 + jnp.exp(-pre))).astype(jnp.bfloat16).reshape(blocks, frames, chans)


def temporal_forward_k(acts, kernel, step_size):
    count, frames, chans = acts.shape
    spec = pl.BlockSpec((JB, frames, chans), lambda j, d: (j, 0, 0))
    return pl.pallas_call(
        tfwd_kernel,
        grid_spec=pltpu.PrefetchScalarGridSpec(
            num_scalar_prefetch=1,
            grid=(count // JB,),
            in_specs=[spec, pl.BlockSpec((5 * chans, chans), lambda j, d: (0, 0))],
            out_specs=[spec, spec],
        ),
        out_shape=[
            jax.ShapeDtypeStruct(acts.shape, jnp.float32),
            jax.ShapeDtypeStruct(acts.shape, jnp.bfloat16),
        ],
    )(step_size.reshape(1), acts, kernel.reshape(5 * chans, chans))


def tbwd_kernel(with_pre, dil_ref, act_ref, grad_ref, wt_ref, *rest):
    if with_pre:
        pre_ref, out_ref, tg_ref = rest
    else:
        out_ref, tg_ref = rest
    blocks, frames, chans = act_ref.shape
    stacked = shifted_taps(grad_ref, dil_ref[0], -1)
    grad_act = jnp.dot(stacked, wt_ref[...], preferred_element_type=jnp.float32)
    flat_act = act_ref[...].reshape(blocks * frames, chans)
    part = lax.dot_general(
        flat_act, stacked, (((0,), (0,)), ((), ())), preferred_element_type=jnp.float32
    )

    @pl.when(pl.program_id(0) == 0)
    def _():
        tg_ref[...] = jnp.zeros_like(tg_ref)

    tg_ref[...] += part
    if with_pre:
        pre = pre_ref[...].reshape(blocks * frames, chans)
        sigma = 1.0 / (1.0 + jnp.exp(-pre))
        grad_act = grad_act * (sigma * (1.0 + pre * (1.0 - sigma)))
    out_ref[...] = grad_act.astype(jnp.bfloat16).reshape(blocks, frames, chans)


def temporal_backward_k(acts, grads, kernel, step_size, pre_below):
    count, frames, chans = acts.shape
    spec = pl.BlockSpec((JB, frames, chans), lambda j, d: (j, 0, 0))
    wt = jnp.concatenate([kernel[tap].T for tap in range(5)], axis=0)
    with_pre = pre_below is not None
    in_specs = [spec, spec, pl.BlockSpec((5 * chans, chans), lambda j, d: (0, 0))]
    operands = [step_size.reshape(1), acts, grads, wt]
    if with_pre:
        in_specs.append(spec)
        operands.append(pre_below)
    out, tg = pl.pallas_call(
        functools.partial(tbwd_kernel, with_pre),
        grid_spec=pltpu.PrefetchScalarGridSpec(
            num_scalar_prefetch=1,
            grid=(count // JB,),
            in_specs=in_specs,
            out_specs=[spec, pl.BlockSpec((chans, 5 * chans), lambda j, d: (0, 0))],
        ),
        out_shape=[
            jax.ShapeDtypeStruct(acts.shape, jnp.bfloat16),
            jax.ShapeDtypeStruct((chans, 5 * chans), jnp.float32),
        ],
        compiler_params=pltpu.CompilerParams(dimension_semantics=("arbitrary",)),
    )(*operands)
    tgrad = tg.reshape(chans, 5, chans).transpose(1, 0, 2)
    return out, tgrad


def all_sum(parts, scale):
    flat = jnp.concatenate([p.reshape(-1) for p in parts])
    count = lax.axis_size(("seg", "grp"))
    chunk = flat.shape[0] // count
    pieces = lax.all_to_all(
        flat.reshape(count, chunk), ("seg", "grp"), split_axis=0, concat_axis=0, tiled=True
    )
    mine = (jnp.sum(pieces, axis=0) * scale).astype(jnp.bfloat16)
    spread = jnp.broadcast_to(mine[None], (count, chunk))
    whole = lax.all_to_all(spread, ("seg", "grp"), split_axis=0, concat_axis=0, tiled=True)
    whole = whole.reshape(-1).astype(jnp.float32)
    out = []
    offset = 0
    for p in parts:
        out.append(whole[offset : offset + p.size].reshape(p.shape))
        offset += p.size
    return out


def local(
    frames_in, spatial_weight, temporal_weight, uniting_weight, key_index, dilation, cotangent
):
    local_frames, rows, cols, chans = frames_in.shape
    pixels = rows * cols
    seg_count = lax.axis_size("seg")
    pre_spatial = spatial_forward(frames_in, spatial_weight)
    act_zero = jax.nn.silu(pre_spatial).astype(jnp.bfloat16).reshape(local_frames, pixels, chans)
    cot_local = cotangent.reshape(local_frames, pixels, chans)
    act_blocks = to_pixels(act_zero)
    cot_blocks = to_pixels(cot_local)
    acts = [act_blocks]
    block, total_frames = act_blocks.shape[0], act_blocks.shape[1]
    seg_frames = total_frames // seg_count
    pres = []
    for layer in range(LAYERS):
        pre, act = temporal_forward_k(acts[-1], temporal_weight[layer], dilation[layer])
        pres.append(pre)
        acts.append(act)
    feat = acts[-1]
    seg_shape = (block, seg_count, seg_frames, chans)
    feat_seg = feat.reshape(seg_shape)
    positions = jnp.arange(seg_frames, dtype=jnp.int32)
    onehot = positions[None, :] == key_index[:, None]
    keys = jnp.einsum(
        "ns,jnsc->jnc", onehot.astype(jnp.bfloat16), feat_seg, preferred_element_type=jnp.float32
    ).astype(jnp.bfloat16)
    key_full = jnp.broadcast_to(keys[:, :, None], seg_shape).reshape(-1, chans)
    feat_flat = feat.reshape(-1, chans)
    key_part = jnp.dot(
        keys.reshape(-1, chans), uniting_weight[1], preferred_element_type=jnp.float32
    ).reshape(block, seg_count, 1, chans)
    main_part = jnp.dot(feat_flat, uniting_weight[0], preferred_element_type=jnp.float32)
    united_blocks = (main_part.reshape(seg_shape) + key_part).astype(jnp.bfloat16)
    united = to_frames(united_blocks.reshape(block, total_frames, chans))
    cot_flat = cot_blocks.reshape(-1, chans)
    grad_feat = jnp.dot(cot_flat, uniting_weight[0].T, preferred_element_type=jnp.float32)
    seg_cot = jnp.sum(cot_blocks.reshape(seg_shape).astype(jnp.float32), axis=2)
    key_term = jnp.dot(
        seg_cot.reshape(-1, chans),
        uniting_weight[1].T.astype(jnp.float32),
        precision=lax.Precision.HIGHEST,
    ).reshape(block, seg_count, 1, chans)
    placed = onehot.astype(jnp.float32)[None, :, :, None] * key_term
    grad_feat = grad_feat.reshape(seg_shape) + placed
    grad_feat = grad_feat.reshape(block, total_frames, chans)
    grad_uniting = jnp.stack([inner(feat_flat, cot_flat), inner(key_full, cot_flat)])
    grad_pre = (grad_feat * silu_grad(pres[-1])).astype(jnp.bfloat16)
    tgrads = [None] * LAYERS
    for layer in range(LAYERS - 1, -1, -1):
        below = pres[layer - 1] if layer > 0 else None
        grad_pre, tgrads[layer] = temporal_backward_k(
            acts[layer], grad_pre, temporal_weight[layer], dilation[layer], below
        )
    grad_act0 = grad_pre
    grad_time = to_frames(grad_act0).reshape(frames_in.shape)
    grad_spre = (grad_time.astype(jnp.float32) * silu_grad(pre_spatial)).astype(jnp.bfloat16)
    grad_frames = spatial_back(grad_spre, spatial_weight).astype(jnp.bfloat16)
    grad_spatial = spatial_wgrad(frames_in, grad_spre)
    scale = 1.0 / jnp.sqrt(jnp.float32(total_frames * pixels))
    summed = all_sum((grad_spatial, jnp.stack(tgrads), grad_uniting), scale)
    return (
        united.reshape(frames_in.shape),
        grad_frames,
        summed[0],
        summed[1],
        summed[2],
    )


def solution(mesh):
    placed = (
        P(("seg", "grp"), None, None, None),
        P(),
        P(),
        P(),
        P(),
        P(),
        P(("seg", "grp"), None, None, None),
    )
    return jax.shard_map(
        local,
        mesh=mesh,
        in_specs=placed,
        out_specs=(
            P(("seg", "grp"), None, None, None),
            P(("seg", "grp"), None, None, None),
            P(),
            P(),
            P(),
        ),
        check_vma=False,
    )
```

```python
import functools

import jax
import jax.numpy as jnp
from jax import lax
from jax.sharding import PartitionSpec as P
from jax.experimental import pallas as pl
from jax.experimental.pallas import tpu as pltpu

LAYERS = 2
DMAX = 8


def from_root(value, axis, root):
    mine = lax.axis_index(axis) == root
    return lax.psum(jnp.where(mine, value, jnp.zeros_like(value)), axis)


def silu_grad(value):
    sigma = jax.nn.sigmoid(value)
    return sigma * (1.0 + value * (1.0 - sigma))


def inner(left, right):
    return lax.dot_general(
        left, right, (((0,), (0,)), ((), ())), preferred_element_type=jnp.float32
    )


def spatial_forward(frames, kernel):
    count, rows, cols, chans = frames.shape
    padded = jnp.pad(frames, ((0, 0), (1, 1), (1, 1), (0, 0)))
    total = jnp.zeros((count * rows * cols, chans), jnp.float32)
    for row_tap in range(3):
        for col_tap in range(3):
            piece = padded[:, row_tap : row_tap + rows, col_tap : col_tap + cols, :].reshape(
                -1, chans
            )
            total = total + jnp.dot(
                piece, kernel[3 * row_tap + col_tap], preferred_element_type=jnp.float32
            )
    return total.reshape(frames.shape)


def spatial_back(grads, kernel):
    count, rows, cols, chans = grads.shape
    padded = jnp.pad(grads, ((0, 0), (1, 1), (1, 1), (0, 0)))
    total = jnp.zeros((count * rows * cols, chans), jnp.float32)
    for row_tap in range(3):
        for col_tap in range(3):
            piece = padded[
                :, 2 - row_tap : 2 - row_tap + rows, 2 - col_tap : 2 - col_tap + cols, :
            ].reshape(-1, chans)
            total = total + jnp.dot(
                piece, kernel[3 * row_tap + col_tap].T, preferred_element_type=jnp.float32
            )
    return total.reshape(grads.shape)


def spatial_wgrad(frames, grads):
    count, rows, cols, chans = frames.shape
    padded = jnp.pad(frames, ((0, 0), (1, 1), (1, 1), (0, 0)))
    flat_grads = grads.reshape(-1, chans)
    result = []
    for row_tap in range(3):
        for col_tap in range(3):
            piece = padded[:, row_tap : row_tap + rows, col_tap : col_tap + cols, :].reshape(
                -1, chans
            )
            result.append(inner(piece, flat_grads))
    return jnp.stack(result)


def shifted(values, offset):
    padded = jnp.pad(values, ((2 * DMAX, 2 * DMAX), (0, 0), (0, 0)))
    start = 2 * DMAX + offset
    return lax.dynamic_slice_in_dim(padded, start, values.shape[0], 0)


def temporal_forward(acts, kernel, step_size):
    chans = acts.shape[2]
    total = jnp.zeros((acts.shape[0] * acts.shape[1], chans), jnp.float32)
    for tap in range(5):
        piece = shifted(acts, (tap - 2) * step_size).reshape(-1, chans)
        total = total + jnp.dot(piece, kernel[tap], preferred_element_type=jnp.float32)
    return total.reshape(acts.shape)


def temporal_back(grads, kernel, step_size):
    chans = grads.shape[2]
    total = jnp.zeros((grads.shape[0] * grads.shape[1], chans), jnp.float32)
    for tap in range(5):
        piece = shifted(grads, (2 - tap) * step_size).reshape(-1, chans)
        total = total + jnp.dot(piece, kernel[tap].T, preferred_element_type=jnp.float32)
    return total.reshape(grads.shape)


def temporal_wgrad(acts, grads, step_size):
    chans = acts.shape[2]
    flat_grads = grads.reshape(-1, chans)
    return jnp.stack(
        [
            inner(shifted(acts, (tap - 2) * step_size).reshape(-1, chans), flat_grads)
            for tap in range(5)
        ]
    )


def to_pixels(flat):
    count = lax.axis_size(("seg", "grp"))
    chans = flat.shape[-1]
    strided = flat.reshape(-1, count, chans)
    return lax.all_to_all(strided, ("seg", "grp"), split_axis=1, concat_axis=1, tiled=True)


def to_frames(blocks):
    out = lax.all_to_all(blocks, ("seg", "grp"), split_axis=1, concat_axis=1, tiled=True)
    return out.reshape(1, -1, blocks.shape[-1])


def shifted1(values, offset):
    padded = jnp.pad(values, ((0, 0), (2 * DMAX, 2 * DMAX), (0, 0)))
    start = 2 * DMAX + offset
    return lax.dynamic_slice_in_dim(padded, start, values.shape[1], 1)


def temporal_forward1(acts, kernel, step_size):
    chans = acts.shape[2]
    total = jnp.zeros((acts.shape[0] * acts.shape[1], chans), jnp.float32)
    for tap in range(5):
        piece = shifted1(acts, (tap - 2) * step_size).reshape(-1, chans)
        total = total + jnp.dot(piece, kernel[tap], preferred_element_type=jnp.float32)
    return total.reshape(acts.shape)


def temporal_back1(grads, kernel, step_size):
    chans = grads.shape[2]
    total = jnp.zeros((grads.shape[0] * grads.shape[1], chans), jnp.float32)
    for tap in range(5):
        piece = shifted1(grads, (2 - tap) * step_size).reshape(-1, chans)
        total = total + jnp.dot(piece, kernel[tap].T, preferred_element_type=jnp.float32)
    return total.reshape(grads.shape)


def temporal_wgrad1(acts, grads, step_size):
    chans = acts.shape[2]
    flat_grads = grads.reshape(-1, chans)
    return jnp.stack(
        [
            inner(shifted1(acts, (tap - 2) * step_size).reshape(-1, chans), flat_grads)
            for tap in range(5)
        ]
    )


JB = 10


def shift_matrix(offset, size):
    rows = lax.broadcasted_iota(jnp.int32, (size, size), 0)
    cols = lax.broadcasted_iota(jnp.int32, (size, size), 1)
    return (cols == rows + offset).astype(jnp.bfloat16)


def shifted_taps(x_ref, step, sign):
    blocks, frames, chans = x_ref.shape
    wide = jnp.concatenate([x_ref[j] for j in range(blocks)], axis=1)
    taps = []
    for tap in range(5):
        if tap == 2:
            taps.append(None)
            continue
        moved = jnp.dot(
            shift_matrix(sign * (tap - 2) * step, frames), wide,
            preferred_element_type=jnp.float32,
        ).astype(jnp.bfloat16)
        taps.append(moved)
    rows = []
    for j in range(blocks):
        parts = []
        for tap in range(5):
            if tap == 2:
                parts.append(x_ref[j])
            else:
                parts.append(taps[tap][:, j * chans : (j + 1) * chans])
        rows.append(jnp.concatenate(parts, axis=1))
    return jnp.concatenate(rows, axis=0)


def tfwd_kernel(dil_ref, act_ref, w_ref, pre_ref, out_ref):
    blocks, frames, chans = act_ref.shape
    stacked = shifted_taps(act_ref, dil_ref[0], 1)
    pre = jnp.dot(stacked, w_ref[...], preferred_element_type=jnp.float32)
    pre_ref[...] = pre.reshape(blocks, frames, chans)
    out_ref[...] = (pre / (1.0 + jnp.exp(-pre))).astype(jnp.bfloat16).reshape(blocks, frames, chans)


def temporal_forward_k(acts, kernel, step_size):
    count, frames, chans = acts.shape
    spec = pl.BlockSpec((JB, frames, chans), lambda j, d: (j, 0, 0))
    return pl.pallas_call(
        tfwd_kernel,
        grid_spec=pltpu.PrefetchScalarGridSpec(
            num_scalar_prefetch=1,
            grid=(count // JB,),
            in_specs=[spec, pl.BlockSpec((5 * chans, chans), lambda j, d: (0, 0))],
            out_specs=[spec, spec],
        ),
        out_shape=[
            jax.ShapeDtypeStruct(acts.shape, jnp.float32),
            jax.ShapeDtypeStruct(acts.shape, jnp.bfloat16),
        ],
    )(step_size.reshape(1), acts, kernel.reshape(5 * chans, chans))


def tbwd_kernel(with_pre, dil_ref, act_ref, grad_ref, wt_ref, *rest):
    if with_pre:
        pre_ref, out_ref, tg_ref = rest
    else:
        out_ref, tg_ref = rest
    blocks, frames, chans = act_ref.shape
    stacked = shifted_taps(grad_ref, dil_ref[0], -1)
    grad_act = None
    for tap in range(5):
        term = lax.dot_general(
            stacked[:, tap * chans : (tap + 1) * chans],
            wt_ref[tap * chans : (tap + 1) * chans, :],
            (((1,), (1,)), ((), ())),
            preferred_element_type=jnp.float32,
        )
        grad_act = term if grad_act is None else grad_act + term
    flat_act = act_ref[...].reshape(blocks * frames, chans)
    part = lax.dot_general(
        flat_act, stacked, (((0,), (0,)), ((), ())), preferred_element_type=jnp.float32
    )

    @pl.when(pl.program_id(0) == 0)
    def _():
        tg_ref[...] = jnp.zeros_like(tg_ref)

    for tap in range(5):
        tg_ref[tap] += part[:, tap * chans : (tap + 1) * chans]
    if with_pre:
        pre = pre_ref[...].reshape(blocks * frames, chans)
        sigma = 1.0 / (1.0 + jnp.exp(-pre))
        grad_act = grad_act * (sigma * (1.0 + pre * (1.0 - sigma)))
    out_ref[...] = grad_act.astype(jnp.bfloat16).reshape(blocks, frames, chans)


def temporal_backward_k(acts, grads, kernel, step_size, pre_below):
    count, frames, chans = acts.shape
    spec = pl.BlockSpec((JB, frames, chans), lambda j, d: (j, 0, 0))
    wt = kernel.reshape(5 * chans, chans)
    with_pre = pre_below is not None
    in_specs = [spec, spec, pl.BlockSpec((5 * chans, chans), lambda j, d: (0, 0))]
    operands = [step_size.reshape(1), acts, grads, wt]
    if with_pre:
        in_specs.append(spec)
        operands.append(pre_below)
    out, tg = pl.pallas_call(
        functools.partial(tbwd_kernel, with_pre),
        grid_spec=pltpu.PrefetchScalarGridSpec(
            num_scalar_prefetch=1,
            grid=(count // JB,),
            in_specs=in_specs,
            out_specs=[spec, pl.BlockSpec((5, chans, chans), lambda j, d: (0, 0, 0))],
        ),
        out_shape=[
            jax.ShapeDtypeStruct(acts.shape, jnp.bfloat16),
            jax.ShapeDtypeStruct((5, chans, chans), jnp.float32),
        ],
        compiler_params=pltpu.CompilerParams(dimension_semantics=("arbitrary",)),
    )(*operands)
    return out, tg


def all_sum(parts, scale):
    chans = parts[0].shape[-1]
    count = lax.axis_size(("seg", "grp"))
    rows = [p.reshape(-1, chans) for p in parts]
    used = sum(r.shape[0] for r in rows)
    per = -(-used // (count * 8)) * 8
    rows.append(jnp.zeros((per * count - used, chans), jnp.float32))
    stack = jnp.concatenate(rows, axis=0).reshape(count, per, chans)
    pieces = lax.all_to_all(stack, ("seg", "grp"), split_axis=0, concat_axis=0, tiled=True)
    mine = jnp.sum(pieces, axis=0, keepdims=True) * scale
    spread = jnp.broadcast_to(mine, stack.shape)
    whole = lax.all_to_all(spread, ("seg", "grp"), split_axis=0, concat_axis=0, tiled=True)
    whole = whole.reshape(-1, chans)
    out = []
    offset = 0
    for p in parts:
        size = p.size // chans
        out.append(whole[offset : offset + size].reshape(p.shape))
        offset += size
    return out


def local(
    frames_in, spatial_weight, temporal_weight, uniting_weight, key_index, dilation, cotangent
):
    local_frames, rows, cols, chans = frames_in.shape
    pixels = rows * cols
    seg_count = lax.axis_size("seg")
    pre_spatial = spatial_forward(frames_in, spatial_weight)
    act_zero = jax.nn.silu(pre_spatial).astype(jnp.bfloat16).reshape(local_frames, pixels, chans)
    cot_local = cotangent.reshape(local_frames, pixels, chans)
    act_blocks = to_pixels(act_zero)
    cot_blocks = to_pixels(cot_local)
    acts = [act_blocks]
    block, total_frames = act_blocks.shape[0], act_blocks.shape[1]
    seg_frames = total_frames // seg_count
    pres = []
    for layer in range(LAYERS):
        pre, act = temporal_forward_k(acts[-1], temporal_weight[layer], dilation[layer])
        pres.append(pre)
        acts.append(act)
    feat = acts[-1]
    seg_shape = (block, seg_count, seg_frames, chans)
    feat_seg = feat.reshape(seg_shape)
    positions = jnp.arange(seg_frames, dtype=jnp.int32)
    onehot = positions[None, :] == key_index[:, None]
    keys = jnp.einsum(
        "ns,jnsc->jnc", onehot.astype(jnp.bfloat16), feat_seg, preferred_element_type=jnp.float32
    ).astype(jnp.bfloat16)
    key_full = jnp.broadcast_to(keys[:, :, None], seg_shape).reshape(-1, chans)
    feat_flat = feat.reshape(-1, chans)
    key_part = jnp.dot(
        keys.reshape(-1, chans), uniting_weight[1], preferred_element_type=jnp.float32
    ).reshape(block, seg_count, 1, chans)
    main_part = jnp.dot(feat_flat, uniting_weight[0], preferred_element_type=jnp.float32)
    united_blocks = (main_part.reshape(seg_shape) + key_part).astype(jnp.bfloat16)
    united = to_frames(united_blocks.reshape(block, total_frames, chans))
    cot_flat = cot_blocks.reshape(-1, chans)
    grad_feat = jnp.dot(cot_flat, uniting_weight[0].T, preferred_element_type=jnp.float32)
    seg_cot = jnp.sum(cot_blocks.reshape(seg_shape).astype(jnp.float32), axis=2)
    key_term = jnp.dot(
        seg_cot.reshape(-1, chans),
        uniting_weight[1].T.astype(jnp.float32),
        precision=lax.Precision.HIGHEST,
    ).reshape(block, seg_count, 1, chans)
    placed = onehot.astype(jnp.float32)[None, :, :, None] * key_term
    grad_feat = grad_feat.reshape(seg_shape) + placed
    grad_feat = grad_feat.reshape(block, total_frames, chans)
    grad_uniting = jnp.stack([inner(feat_flat, cot_flat), inner(key_full, cot_flat)])
    grad_pre = (grad_feat * silu_grad(pres[-1])).astype(jnp.bfloat16)
    tgrads = [None] * LAYERS
    for layer in range(LAYERS - 1, -1, -1):
        below = pres[layer - 1] if layer > 0 else None
        grad_pre, tgrads[layer] = temporal_backward_k(
            acts[layer], grad_pre, temporal_weight[layer], dilation[layer], below
        )
    grad_act0 = grad_pre
    grad_time = to_frames(grad_act0).reshape(frames_in.shape)
    grad_spre = (grad_time.astype(jnp.float32) * silu_grad(pre_spatial)).astype(jnp.bfloat16)
    grad_frames = spatial_back(grad_spre, spatial_weight).astype(jnp.bfloat16)
    grad_spatial = spatial_wgrad(frames_in, grad_spre)
    scale = 1.0 / jnp.sqrt(jnp.float32(total_frames * pixels))
    summed = all_sum((grad_spatial, jnp.stack(tgrads), grad_uniting), scale)
    return (
        united.reshape(frames_in.shape),
        grad_frames,
        summed[0],
        summed[1],
        summed[2],
    )


def solution(mesh):
    placed = (
        P(("seg", "grp"), None, None, None),
        P(),
        P(),
        P(),
        P(),
        P(),
        P(("seg", "grp"), None, None, None),
    )
    return jax.shard_map(
        local,
        mesh=mesh,
        in_specs=placed,
        out_specs=(
            P(("seg", "grp"), None, None, None),
            P(("seg", "grp"), None, None, None),
            P(),
            P(),
            P(),
        ),
        check_vma=False,
    )
```

```python
import functools

import jax
import jax.numpy as jnp
from jax import lax
from jax.sharding import PartitionSpec as P
from jax.experimental import pallas as pl
from jax.experimental.pallas import tpu as pltpu

LAYERS = 2
DMAX = 8


def from_root(value, axis, root):
    mine = lax.axis_index(axis) == root
    return lax.psum(jnp.where(mine, value, jnp.zeros_like(value)), axis)


def silu_grad(value):
    sigma = jax.nn.sigmoid(value)
    return sigma * (1.0 + value * (1.0 - sigma))


def inner(left, right):
    return lax.dot_general(
        left, right, (((0,), (0,)), ((), ())), preferred_element_type=jnp.float32
    )


def spatial_forward(frames, kernel):
    count, rows, cols, chans = frames.shape
    padded = jnp.pad(frames, ((0, 0), (1, 1), (1, 1), (0, 0)))
    total = jnp.zeros((count * rows * cols, chans), jnp.float32)
    for row_tap in range(3):
        for col_tap in range(3):
            piece = padded[:, row_tap : row_tap + rows, col_tap : col_tap + cols, :].reshape(
                -1, chans
            )
            total = total + jnp.dot(
                piece, kernel[3 * row_tap + col_tap], preferred_element_type=jnp.float32
            )
    return total.reshape(frames.shape)


def spatial_back(grads, kernel):
    count, rows, cols, chans = grads.shape
    padded = jnp.pad(grads, ((0, 0), (1, 1), (1, 1), (0, 0)))
    total = jnp.zeros((count * rows * cols, chans), jnp.float32)
    for row_tap in range(3):
        for col_tap in range(3):
            piece = padded[
                :, 2 - row_tap : 2 - row_tap + rows, 2 - col_tap : 2 - col_tap + cols, :
            ].reshape(-1, chans)
            total = total + jnp.dot(
                piece, kernel[3 * row_tap + col_tap].T, preferred_element_type=jnp.float32
            )
    return total.reshape(grads.shape)


def spatial_wgrad(frames, grads):
    count, rows, cols, chans = frames.shape
    padded = jnp.pad(frames, ((0, 0), (1, 1), (1, 1), (0, 0)))
    flat_grads = grads.reshape(-1, chans)
    result = []
    for row_tap in range(3):
        for col_tap in range(3):
            piece = padded[:, row_tap : row_tap + rows, col_tap : col_tap + cols, :].reshape(
                -1, chans
            )
            result.append(inner(piece, flat_grads))
    return jnp.stack(result)


def shifted(values, offset):
    padded = jnp.pad(values, ((2 * DMAX, 2 * DMAX), (0, 0), (0, 0)))
    start = 2 * DMAX + offset
    return lax.dynamic_slice_in_dim(padded, start, values.shape[0], 0)


def temporal_forward(acts, kernel, step_size):
    chans = acts.shape[2]
    total = jnp.zeros((acts.shape[0] * acts.shape[1], chans), jnp.float32)
    for tap in range(5):
        piece = shifted(acts, (tap - 2) * step_size).reshape(-1, chans)
        total = total + jnp.dot(piece, kernel[tap], preferred_element_type=jnp.float32)
    return total.reshape(acts.shape)


def temporal_back(grads, kernel, step_size):
    chans = grads.shape[2]
    total = jnp.zeros((grads.shape[0] * grads.shape[1], chans), jnp.float32)
    for tap in range(5):
        piece = shifted(grads, (2 - tap) * step_size).reshape(-1, chans)
        total = total + jnp.dot(piece, kernel[tap].T, preferred_element_type=jnp.float32)
    return total.reshape(grads.shape)


def temporal_wgrad(acts, grads, step_size):
    chans = acts.shape[2]
    flat_grads = grads.reshape(-1, chans)
    return jnp.stack(
        [
            inner(shifted(acts, (tap - 2) * step_size).reshape(-1, chans), flat_grads)
            for tap in range(5)
        ]
    )


def to_pixels(flat):
    count = lax.axis_size(("seg", "grp"))
    chans = flat.shape[-1]
    strided = flat.reshape(-1, count, chans)
    return lax.all_to_all(strided, ("seg", "grp"), split_axis=1, concat_axis=1, tiled=True)


def to_frames(blocks):
    out = lax.all_to_all(blocks, ("seg", "grp"), split_axis=1, concat_axis=1, tiled=True)
    return out.reshape(1, -1, blocks.shape[-1])


def shifted1(values, offset):
    padded = jnp.pad(values, ((0, 0), (2 * DMAX, 2 * DMAX), (0, 0)))
    start = 2 * DMAX + offset
    return lax.dynamic_slice_in_dim(padded, start, values.shape[1], 1)


def temporal_forward1(acts, kernel, step_size):
    chans = acts.shape[2]
    total = jnp.zeros((acts.shape[0] * acts.shape[1], chans), jnp.float32)
    for tap in range(5):
        piece = shifted1(acts, (tap - 2) * step_size).reshape(-1, chans)
        total = total + jnp.dot(piece, kernel[tap], preferred_element_type=jnp.float32)
    return total.reshape(acts.shape)


def temporal_back1(grads, kernel, step_size):
    chans = grads.shape[2]
    total = jnp.zeros((grads.shape[0] * grads.shape[1], chans), jnp.float32)
    for tap in range(5):
        piece = shifted1(grads, (2 - tap) * step_size).reshape(-1, chans)
        total = total + jnp.dot(piece, kernel[tap].T, preferred_element_type=jnp.float32)
    return total.reshape(grads.shape)


def temporal_wgrad1(acts, grads, step_size):
    chans = acts.shape[2]
    flat_grads = grads.reshape(-1, chans)
    return jnp.stack(
        [
            inner(shifted1(acts, (tap - 2) * step_size).reshape(-1, chans), flat_grads)
            for tap in range(5)
        ]
    )


JB = 10


def shift_matrix(offset, size):
    rows = lax.broadcasted_iota(jnp.int32, (size, size), 0)
    cols = lax.broadcasted_iota(jnp.int32, (size, size), 1)
    return (cols == rows + offset).astype(jnp.bfloat16)


def shifted_taps(x_ref, step, sign):
    blocks, frames, chans = x_ref.shape
    wide = jnp.concatenate([x_ref[j] for j in range(blocks)], axis=1)
    taps = []
    for tap in range(5):
        if tap == 2:
            taps.append(None)
            continue
        moved = jnp.dot(
            shift_matrix(sign * (tap - 2) * step, frames), wide,
            preferred_element_type=jnp.float32,
        ).astype(jnp.bfloat16)
        taps.append(moved)
    rows = []
    for j in range(blocks):
        parts = []
        for tap in range(5):
            if tap == 2:
                parts.append(x_ref[j])
            else:
                parts.append(taps[tap][:, j * chans : (j + 1) * chans])
        rows.append(jnp.concatenate(parts, axis=1))
    return jnp.concatenate(rows, axis=0)


def tfwd_kernel(dil_ref, act_ref, w_ref, pre_ref, out_ref):
    blocks, frames, chans = act_ref.shape
    stacked = shifted_taps(act_ref, dil_ref[0], 1)
    pre = jnp.dot(stacked, w_ref[...], preferred_element_type=jnp.float32)
    pre_ref[...] = pre.reshape(blocks, frames, chans)
    out_ref[...] = (pre / (1.0 + jnp.exp(-pre))).astype(jnp.bfloat16).reshape(blocks, frames, chans)


def temporal_forward_k(acts, kernel, step_size):
    count, frames, chans = acts.shape
    spec = pl.BlockSpec((JB, frames, chans), lambda j, d: (j, 0, 0))
    return pl.pallas_call(
        tfwd_kernel,
        grid_spec=pltpu.PrefetchScalarGridSpec(
            num_scalar_prefetch=1,
            grid=(count // JB,),
            in_specs=[spec, pl.BlockSpec((5 * chans, chans), lambda j, d: (0, 0))],
            out_specs=[spec, spec],
        ),
        out_shape=[
            jax.ShapeDtypeStruct(acts.shape, jnp.float32),
            jax.ShapeDtypeStruct(acts.shape, jnp.bfloat16),
        ],
        cost_estimate=pl.CostEstimate(
            flops=2 * count * frames * chans * chans * 9,
            transcendentals=count * frames * chans,
            bytes_accessed=count * frames * chans * 8,
        ),
    )(step_size.reshape(1), acts, kernel.reshape(5 * chans, chans))


def tbwd_kernel(with_pre, dil_ref, act_ref, grad_ref, wt_ref, *rest):
    if with_pre:
        pre_ref, out_ref, tg_ref = rest
    else:
        out_ref, tg_ref = rest
    blocks, frames, chans = act_ref.shape
    stacked = shifted_taps(grad_ref, dil_ref[0], -1)
    grad_act = None
    for tap in range(5):
        term = lax.dot_general(
            stacked[:, tap * chans : (tap + 1) * chans],
            wt_ref[tap * chans : (tap + 1) * chans, :],
            (((1,), (1,)), ((), ())),
            preferred_element_type=jnp.float32,
        )
        grad_act = term if grad_act is None else grad_act + term
    flat_act = act_ref[...].reshape(blocks * frames, chans)
    part = lax.dot_general(
        flat_act, stacked, (((0,), (0,)), ((), ())), preferred_element_type=jnp.float32
    )

    @pl.when(pl.program_id(0) == 0)
    def _():
        tg_ref[...] = jnp.zeros_like(tg_ref)

    for tap in range(5):
        tg_ref[tap] += part[:, tap * chans : (tap + 1) * chans]
    if with_pre:
        pre = pre_ref[...].reshape(blocks * frames, chans)
        sigma = 1.0 / (1.0 + jnp.exp(-pre))
        grad_act = grad_act * (sigma * (1.0 + pre * (1.0 - sigma)))
    out_ref[...] = grad_act.astype(jnp.bfloat16).reshape(blocks, frames, chans)


def temporal_backward_k(acts, grads, kernel, step_size, pre_below):
    count, frames, chans = acts.shape
    spec = pl.BlockSpec((JB, frames, chans), lambda j, d: (j, 0, 0))
    wt = kernel.reshape(5 * chans, chans)
    with_pre = pre_below is not None
    in_specs = [spec, spec, pl.BlockSpec((5 * chans, chans), lambda j, d: (0, 0))]
    operands = [step_size.reshape(1), acts, grads, wt]
    if with_pre:
        in_specs.append(spec)
        operands.append(pre_below)
    out, tg = pl.pallas_call(
        functools.partial(tbwd_kernel, with_pre),
        grid_spec=pltpu.PrefetchScalarGridSpec(
            num_scalar_prefetch=1,
            grid=(count // JB,),
            in_specs=in_specs,
            out_specs=[spec, pl.BlockSpec((5, chans, chans), lambda j, d: (0, 0, 0))],
        ),
        out_shape=[
            jax.ShapeDtypeStruct(acts.shape, jnp.bfloat16),
            jax.ShapeDtypeStruct((5, chans, chans), jnp.float32),
        ],
        compiler_params=pltpu.CompilerParams(dimension_semantics=("arbitrary",)),
        cost_estimate=pl.CostEstimate(
            flops=2 * count * frames * chans * chans * 14,
            transcendentals=count * frames * chans,
            bytes_accessed=count * frames * chans * 10,
        ),
    )(*operands)
    return out, tg


def all_sum(parts, scale):
    chans = parts[0].shape[-1]
    count = lax.axis_size(("seg", "grp"))
    rows = [p.reshape(-1, chans) for p in parts]
    used = sum(r.shape[0] for r in rows)
    per = -(-used // (count * 8)) * 8
    rows.append(jnp.zeros((per * count - used, chans), jnp.float32))
    stack = jnp.concatenate(rows, axis=0).reshape(count, per, chans)
    pieces = lax.all_to_all(stack, ("seg", "grp"), split_axis=0, concat_axis=0, tiled=True)
    mine = jnp.sum(pieces, axis=0, keepdims=True) * scale
    spread = jnp.broadcast_to(mine, stack.shape)
    whole = lax.all_to_all(spread, ("seg", "grp"), split_axis=0, concat_axis=0, tiled=True)
    whole = whole.reshape(-1, chans)
    out = []
    offset = 0
    for p in parts:
        size = p.size // chans
        out.append(whole[offset : offset + size].reshape(p.shape))
        offset += size
    return out


def local(
    frames_in, spatial_weight, temporal_weight, uniting_weight, key_index, dilation, cotangent
):
    local_frames, rows, cols, chans = frames_in.shape
    pixels = rows * cols
    seg_count = lax.axis_size("seg")
    pre_spatial = spatial_forward(frames_in, spatial_weight)
    act_zero = jax.nn.silu(pre_spatial).astype(jnp.bfloat16).reshape(local_frames, pixels, chans)
    cot_local = cotangent.reshape(local_frames, pixels, chans)
    act_blocks = to_pixels(act_zero)
    act_blocks, cot_local = lax.optimization_barrier((act_blocks, cot_local))
    cot_blocks = to_pixels(cot_local)
    acts = [act_blocks]
    block, total_frames = act_blocks.shape[0], act_blocks.shape[1]
    seg_frames = total_frames // seg_count
    pres = []
    for layer in range(LAYERS):
        pre, act = temporal_forward_k(acts[-1], temporal_weight[layer], dilation[layer])
        pres.append(pre)
        acts.append(act)
    feat = acts[-1]
    seg_shape = (block, seg_count, seg_frames, chans)
    feat_seg = feat.reshape(seg_shape)
    positions = jnp.arange(seg_frames, dtype=jnp.int32)
    onehot = positions[None, :] == key_index[:, None]
    keys = jnp.einsum(
        "ns,jnsc->jnc", onehot.astype(jnp.bfloat16), feat_seg, preferred_element_type=jnp.float32
    ).astype(jnp.bfloat16)
    key_full = jnp.broadcast_to(keys[:, :, None], seg_shape).reshape(-1, chans)
    feat_flat = feat.reshape(-1, chans)
    key_part = jnp.dot(
        keys.reshape(-1, chans), uniting_weight[1], preferred_element_type=jnp.float32
    ).reshape(block, seg_count, 1, chans)
    main_part = jnp.dot(feat_flat, uniting_weight[0], preferred_element_type=jnp.float32)
    united_blocks = (main_part.reshape(seg_shape) + key_part).astype(jnp.bfloat16)
    united = to_frames(united_blocks.reshape(block, total_frames, chans))
    cot_flat = cot_blocks.reshape(-1, chans)
    grad_feat = jnp.dot(cot_flat, uniting_weight[0].T, preferred_element_type=jnp.float32)
    seg_cot = jnp.sum(cot_blocks.reshape(seg_shape).astype(jnp.float32), axis=2)
    key_term = jnp.dot(
        seg_cot.reshape(-1, chans),
        uniting_weight[1].T.astype(jnp.float32),
        precision=lax.Precision.HIGHEST,
    ).reshape(block, seg_count, 1, chans)
    placed = onehot.astype(jnp.float32)[None, :, :, None] * key_term
    grad_feat = grad_feat.reshape(seg_shape) + placed
    grad_feat = grad_feat.reshape(block, total_frames, chans)
    grad_uniting = jnp.stack([inner(feat_flat, cot_flat), inner(key_full, cot_flat)])
    grad_pre = (grad_feat * silu_grad(pres[-1])).astype(jnp.bfloat16)
    tgrads = [None] * LAYERS
    for layer in range(LAYERS - 1, -1, -1):
        below = pres[layer - 1] if layer > 0 else None
        grad_pre, tgrads[layer] = temporal_backward_k(
            acts[layer], grad_pre, temporal_weight[layer], dilation[layer], below
        )
    grad_act0 = grad_pre
    grad_time = to_frames(grad_act0).reshape(frames_in.shape)
    grad_spre = (grad_time.astype(jnp.float32) * silu_grad(pre_spatial)).astype(jnp.bfloat16)
    grad_frames = spatial_back(grad_spre, spatial_weight).astype(jnp.bfloat16)
    grad_spatial = spatial_wgrad(frames_in, grad_spre)
    scale = 1.0 / jnp.sqrt(jnp.float32(total_frames * pixels))
    summed = all_sum((grad_spatial, jnp.stack(tgrads), grad_uniting), scale)
    return (
        united.reshape(frames_in.shape),
        grad_frames,
        summed[0],
        summed[1],
        summed[2],
    )


def solution(mesh):
    placed = (
        P(("seg", "grp"), None, None, None),
        P(),
        P(),
        P(),
        P(),
        P(),
        P(("seg", "grp"), None, None, None),
    )
    return jax.shard_map(
        local,
        mesh=mesh,
        in_specs=placed,
        out_specs=(
            P(("seg", "grp"), None, None, None),
            P(("seg", "grp"), None, None, None),
            P(),
            P(),
            P(),
        ),
        check_vma=False,
    )
```

```python
import functools

import jax
import jax.numpy as jnp
from jax import lax
from jax.sharding import PartitionSpec as P
from jax.experimental import pallas as pl
from jax.experimental.pallas import tpu as pltpu

LAYERS = 2
DMAX = 8


def from_root(value, axis, root):
    mine = lax.axis_index(axis) == root
    return lax.psum(jnp.where(mine, value, jnp.zeros_like(value)), axis)


def silu_grad(value):
    sigma = jax.nn.sigmoid(value)
    return sigma * (1.0 + value * (1.0 - sigma))


def inner(left, right):
    return lax.dot_general(
        left, right, (((0,), (0,)), ((), ())), preferred_element_type=jnp.float32
    )


def spatial_forward(frames, kernel):
    count, rows, cols, chans = frames.shape
    padded = jnp.pad(frames, ((0, 0), (1, 1), (1, 1), (0, 0)))
    total = jnp.zeros((count * rows * cols, chans), jnp.float32)
    for row_tap in range(3):
        for col_tap in range(3):
            piece = padded[:, row_tap : row_tap + rows, col_tap : col_tap + cols, :].reshape(
                -1, chans
            )
            total = total + jnp.dot(
                piece, kernel[3 * row_tap + col_tap], preferred_element_type=jnp.float32
            )
    return total.reshape(frames.shape)


def spatial_back(grads, kernel):
    count, rows, cols, chans = grads.shape
    padded = jnp.pad(grads, ((0, 0), (1, 1), (1, 1), (0, 0)))
    total = jnp.zeros((count * rows * cols, chans), jnp.float32)
    for row_tap in range(3):
        for col_tap in range(3):
            piece = padded[
                :, 2 - row_tap : 2 - row_tap + rows, 2 - col_tap : 2 - col_tap + cols, :
            ].reshape(-1, chans)
            total = total + jnp.dot(
                piece, kernel[3 * row_tap + col_tap].T, preferred_element_type=jnp.float32
            )
    return total.reshape(grads.shape)


def spatial_wgrad(frames, grads):
    count, rows, cols, chans = frames.shape
    padded = jnp.pad(frames, ((0, 0), (1, 1), (1, 1), (0, 0)))
    flat_grads = grads.reshape(-1, chans)
    result = []
    for row_tap in range(3):
        for col_tap in range(3):
            piece = padded[:, row_tap : row_tap + rows, col_tap : col_tap + cols, :].reshape(
                -1, chans
            )
            result.append(inner(piece, flat_grads))
    return jnp.stack(result)


def shifted(values, offset):
    padded = jnp.pad(values, ((2 * DMAX, 2 * DMAX), (0, 0), (0, 0)))
    start = 2 * DMAX + offset
    return lax.dynamic_slice_in_dim(padded, start, values.shape[0], 0)


def temporal_forward(acts, kernel, step_size):
    chans = acts.shape[2]
    total = jnp.zeros((acts.shape[0] * acts.shape[1], chans), jnp.float32)
    for tap in range(5):
        piece = shifted(acts, (tap - 2) * step_size).reshape(-1, chans)
        total = total + jnp.dot(piece, kernel[tap], preferred_element_type=jnp.float32)
    return total.reshape(acts.shape)


def temporal_back(grads, kernel, step_size):
    chans = grads.shape[2]
    total = jnp.zeros((grads.shape[0] * grads.shape[1], chans), jnp.float32)
    for tap in range(5):
        piece = shifted(grads, (2 - tap) * step_size).reshape(-1, chans)
        total = total + jnp.dot(piece, kernel[tap].T, preferred_element_type=jnp.float32)
    return total.reshape(grads.shape)


def temporal_wgrad(acts, grads, step_size):
    chans = acts.shape[2]
    flat_grads = grads.reshape(-1, chans)
    return jnp.stack(
        [
            inner(shifted(acts, (tap - 2) * step_size).reshape(-1, chans), flat_grads)
            for tap in range(5)
        ]
    )


def to_pixels(flat):
    count = lax.axis_size(("seg", "grp"))
    chans = flat.shape[-1]
    strided = flat.reshape(-1, count, chans)
    return lax.all_to_all(strided, ("seg", "grp"), split_axis=1, concat_axis=1, tiled=True)


def to_frames(blocks):
    out = lax.all_to_all(blocks, ("seg", "grp"), split_axis=1, concat_axis=1, tiled=True)
    return out.reshape(1, -1, blocks.shape[-1])


def shifted1(values, offset):
    padded = jnp.pad(values, ((0, 0), (2 * DMAX, 2 * DMAX), (0, 0)))
    start = 2 * DMAX + offset
    return lax.dynamic_slice_in_dim(padded, start, values.shape[1], 1)


def temporal_forward1(acts, kernel, step_size):
    chans = acts.shape[2]
    total = jnp.zeros((acts.shape[0] * acts.shape[1], chans), jnp.float32)
    for tap in range(5):
        piece = shifted1(acts, (tap - 2) * step_size).reshape(-1, chans)
        total = total + jnp.dot(piece, kernel[tap], preferred_element_type=jnp.float32)
    return total.reshape(acts.shape)


def temporal_back1(grads, kernel, step_size):
    chans = grads.shape[2]
    total = jnp.zeros((grads.shape[0] * grads.shape[1], chans), jnp.float32)
    for tap in range(5):
        piece = shifted1(grads, (2 - tap) * step_size).reshape(-1, chans)
        total = total + jnp.dot(piece, kernel[tap].T, preferred_element_type=jnp.float32)
    return total.reshape(grads.shape)


def temporal_wgrad1(acts, grads, step_size):
    chans = acts.shape[2]
    flat_grads = grads.reshape(-1, chans)
    return jnp.stack(
        [
            inner(shifted1(acts, (tap - 2) * step_size).reshape(-1, chans), flat_grads)
            for tap in range(5)
        ]
    )


JB = 10


def shift_matrix(offset, size):
    rows = lax.broadcasted_iota(jnp.int32, (size, size), 0)
    cols = lax.broadcasted_iota(jnp.int32, (size, size), 1)
    return (cols == rows + offset).astype(jnp.bfloat16)


def shifted_taps(x_ref, step, sign):
    blocks, frames, chans = x_ref.shape
    wide = jnp.concatenate([x_ref[j] for j in range(blocks)], axis=1).astype(jnp.float32)
    rows = lax.broadcasted_iota(jnp.int32, wide.shape, 0)
    taps = []
    for tap in range(5):
        if tap == 2:
            taps.append(None)
            continue
        offset = sign * (tap - 2) * step
        rolled = pltpu.roll(wide, (frames - offset) % frames, 0)
        inside = (rows + offset >= 0) & (rows + offset < frames)
        taps.append(jnp.where(inside, rolled, 0.0).astype(jnp.bfloat16))
    rows = []
    for j in range(blocks):
        parts = []
        for tap in range(5):
            if tap == 2:
                parts.append(x_ref[j])
            else:
                parts.append(taps[tap][:, j * chans : (j + 1) * chans])
        rows.append(jnp.concatenate(parts, axis=1))
    return jnp.concatenate(rows, axis=0)


def tfwd_kernel(dil_ref, act_ref, w_ref, pre_ref, out_ref):
    blocks, frames, chans = act_ref.shape
    stacked = shifted_taps(act_ref, dil_ref[0], 1)
    pre = jnp.dot(stacked, w_ref[...], preferred_element_type=jnp.float32)
    pre_ref[...] = pre.reshape(blocks, frames, chans)
    out_ref[...] = (pre / (1.0 + jnp.exp(-pre))).astype(jnp.bfloat16).reshape(blocks, frames, chans)


def temporal_forward_k(acts, kernel, step_size):
    count, frames, chans = acts.shape
    spec = pl.BlockSpec((JB, frames, chans), lambda j, d: (j, 0, 0))
    return pl.pallas_call(
        tfwd_kernel,
        grid_spec=pltpu.PrefetchScalarGridSpec(
            num_scalar_prefetch=1,
            grid=(count // JB,),
            in_specs=[spec, pl.BlockSpec((5 * chans, chans), lambda j, d: (0, 0))],
            out_specs=[spec, spec],
        ),
        out_shape=[
            jax.ShapeDtypeStruct(acts.shape, jnp.float32),
            jax.ShapeDtypeStruct(acts.shape, jnp.bfloat16),
        ],
        cost_estimate=pl.CostEstimate(
            flops=2 * count * frames * chans * chans * 9,
            transcendentals=count * frames * chans,
            bytes_accessed=count * frames * chans * 8,
        ),
    )(step_size.reshape(1), acts, kernel.reshape(5 * chans, chans))


def tbwd_kernel(with_pre, dil_ref, act_ref, grad_ref, wt_ref, *rest):
    if with_pre:
        pre_ref, out_ref, tg_ref = rest
    else:
        out_ref, tg_ref = rest
    blocks, frames, chans = act_ref.shape
    stacked = shifted_taps(grad_ref, dil_ref[0], -1)
    grad_act = None
    for tap in range(5):
        term = lax.dot_general(
            stacked[:, tap * chans : (tap + 1) * chans],
            wt_ref[tap * chans : (tap + 1) * chans, :],
            (((1,), (1,)), ((), ())),
            preferred_element_type=jnp.float32,
        )
        grad_act = term if grad_act is None else grad_act + term
    flat_act = act_ref[...].reshape(blocks * frames, chans)
    part = lax.dot_general(
        flat_act, stacked, (((0,), (0,)), ((), ())), preferred_element_type=jnp.float32
    )

    @pl.when(pl.program_id(0) == 0)
    def _():
        tg_ref[...] = jnp.zeros_like(tg_ref)

    for tap in range(5):
        tg_ref[tap] += part[:, tap * chans : (tap + 1) * chans]
    if with_pre:
        pre = pre_ref[...].reshape(blocks * frames, chans)
        sigma = 1.0 / (1.0 + jnp.exp(-pre))
        grad_act = grad_act * (sigma * (1.0 + pre * (1.0 - sigma)))
    out_ref[...] = grad_act.astype(jnp.bfloat16).reshape(blocks, frames, chans)


def temporal_backward_k(acts, grads, kernel, step_size, pre_below):
    count, frames, chans = acts.shape
    spec = pl.BlockSpec((JB, frames, chans), lambda j, d: (j, 0, 0))
    wt = kernel.reshape(5 * chans, chans)
    with_pre = pre_below is not None
    in_specs = [spec, spec, pl.BlockSpec((5 * chans, chans), lambda j, d: (0, 0))]
    operands = [step_size.reshape(1), acts, grads, wt]
    if with_pre:
        in_specs.append(spec)
        operands.append(pre_below)
    out, tg = pl.pallas_call(
        functools.partial(tbwd_kernel, with_pre),
        grid_spec=pltpu.PrefetchScalarGridSpec(
            num_scalar_prefetch=1,
            grid=(count // JB,),
            in_specs=in_specs,
            out_specs=[spec, pl.BlockSpec((5, chans, chans), lambda j, d: (0, 0, 0))],
        ),
        out_shape=[
            jax.ShapeDtypeStruct(acts.shape, jnp.bfloat16),
            jax.ShapeDtypeStruct((5, chans, chans), jnp.float32),
        ],
        compiler_params=pltpu.CompilerParams(dimension_semantics=("arbitrary",)),
        cost_estimate=pl.CostEstimate(
            flops=2 * count * frames * chans * chans * 14,
            transcendentals=count * frames * chans,
            bytes_accessed=count * frames * chans * 10,
        ),
    )(*operands)
    return out, tg


def all_sum(parts, scale):
    chans = parts[0].shape[-1]
    count = lax.axis_size(("seg", "grp"))
    rows = [p.reshape(-1, chans) for p in parts]
    used = sum(r.shape[0] for r in rows)
    per = -(-used // (count * 8)) * 8
    rows.append(jnp.zeros((per * count - used, chans), jnp.float32))
    stack = jnp.concatenate(rows, axis=0).reshape(count, per, chans)
    pieces = lax.all_to_all(stack, ("seg", "grp"), split_axis=0, concat_axis=0, tiled=True)
    mine = jnp.sum(pieces, axis=0, keepdims=True) * scale
    spread = jnp.broadcast_to(mine, stack.shape)
    whole = lax.all_to_all(spread, ("seg", "grp"), split_axis=0, concat_axis=0, tiled=True)
    whole = whole.reshape(-1, chans)
    out = []
    offset = 0
    for p in parts:
        size = p.size // chans
        out.append(whole[offset : offset + size].reshape(p.shape))
        offset += size
    return out


def local(
    frames_in, spatial_weight, temporal_weight, uniting_weight, key_index, dilation, cotangent
):
    local_frames, rows, cols, chans = frames_in.shape
    pixels = rows * cols
    seg_count = lax.axis_size("seg")
    pre_spatial = spatial_forward(frames_in, spatial_weight)
    act_zero = jax.nn.silu(pre_spatial).astype(jnp.bfloat16).reshape(local_frames, pixels, chans)
    cot_local = cotangent.reshape(local_frames, pixels, chans)
    act_blocks = to_pixels(act_zero)
    act_blocks, cot_local = lax.optimization_barrier((act_blocks, cot_local))
    cot_blocks = to_pixels(cot_local)
    acts = [act_blocks]
    block, total_frames = act_blocks.shape[0], act_blocks.shape[1]
    seg_frames = total_frames // seg_count
    pres = []
    for layer in range(LAYERS):
        pre, act = temporal_forward_k(acts[-1], temporal_weight[layer], dilation[layer])
        pres.append(pre)
        acts.append(act)
    feat = acts[-1]
    seg_shape = (block, seg_count, seg_frames, chans)
    feat_seg = feat.reshape(seg_shape)
    positions = jnp.arange(seg_frames, dtype=jnp.int32)
    onehot = positions[None, :] == key_index[:, None]
    keys = jnp.einsum(
        "ns,jnsc->jnc", onehot.astype(jnp.bfloat16), feat_seg, preferred_element_type=jnp.float32
    ).astype(jnp.bfloat16)
    key_full = jnp.broadcast_to(keys[:, :, None], seg_shape).reshape(-1, chans)
    feat_flat = feat.reshape(-1, chans)
    key_part = jnp.dot(
        keys.reshape(-1, chans), uniting_weight[1], preferred_element_type=jnp.float32
    ).reshape(block, seg_count, 1, chans)
    main_part = jnp.dot(feat_flat, uniting_weight[0], preferred_element_type=jnp.float32)
    united_blocks = (main_part.reshape(seg_shape) + key_part).astype(jnp.bfloat16)
    united = to_frames(united_blocks.reshape(block, total_frames, chans))
    cot_flat = cot_blocks.reshape(-1, chans)
    grad_feat = jnp.dot(cot_flat, uniting_weight[0].T, preferred_element_type=jnp.float32)
    seg_cot = jnp.sum(cot_blocks.reshape(seg_shape).astype(jnp.float32), axis=2)
    key_term = jnp.dot(
        seg_cot.reshape(-1, chans),
        uniting_weight[1].T.astype(jnp.float32),
        precision=lax.Precision.HIGHEST,
    ).reshape(block, seg_count, 1, chans)
    placed = onehot.astype(jnp.float32)[None, :, :, None] * key_term
    grad_feat = grad_feat.reshape(seg_shape) + placed
    grad_feat = grad_feat.reshape(block, total_frames, chans)
    grad_uniting = jnp.stack([inner(feat_flat, cot_flat), inner(key_full, cot_flat)])
    grad_pre = (grad_feat * silu_grad(pres[-1])).astype(jnp.bfloat16)
    tgrads = [None] * LAYERS
    for layer in range(LAYERS - 1, -1, -1):
        below = pres[layer - 1] if layer > 0 else None
        grad_pre, tgrads[layer] = temporal_backward_k(
            acts[layer], grad_pre, temporal_weight[layer], dilation[layer], below
        )
    grad_act0 = grad_pre
    grad_time = to_frames(grad_act0).reshape(frames_in.shape)
    grad_spre = (grad_time.astype(jnp.float32) * silu_grad(pre_spatial)).astype(jnp.bfloat16)
    grad_frames = spatial_back(grad_spre, spatial_weight).astype(jnp.bfloat16)
    grad_spatial = spatial_wgrad(frames_in, grad_spre)
    scale = 1.0 / jnp.sqrt(jnp.float32(total_frames * pixels))
    summed = all_sum((grad_spatial, jnp.stack(tgrads), grad_uniting), scale)
    return (
        united.reshape(frames_in.shape),
        grad_frames,
        summed[0],
        summed[1],
        summed[2],
    )


def solution(mesh):
    placed = (
        P(("seg", "grp"), None, None, None),
        P(),
        P(),
        P(),
        P(),
        P(),
        P(("seg", "grp"), None, None, None),
    )
    return jax.shard_map(
        local,
        mesh=mesh,
        in_specs=placed,
        out_specs=(
            P(("seg", "grp"), None, None, None),
            P(("seg", "grp"), None, None, None),
            P(),
            P(),
            P(),
        ),
        check_vma=False,
    )
```

```python
import functools

import jax
import jax.numpy as jnp
from jax import lax
from jax.sharding import PartitionSpec as P
from jax.experimental import pallas as pl
from jax.experimental.pallas import tpu as pltpu

LAYERS = 2
DMAX = 8


def from_root(value, axis, root):
    mine = lax.axis_index(axis) == root
    return lax.psum(jnp.where(mine, value, jnp.zeros_like(value)), axis)


def silu_grad(value):
    sigma = jax.nn.sigmoid(value)
    return sigma * (1.0 + value * (1.0 - sigma))


def inner(left, right):
    return lax.dot_general(
        left, right, (((0,), (0,)), ((), ())), preferred_element_type=jnp.float32
    )


def spatial_forward(frames, kernel):
    count, rows, cols, chans = frames.shape
    padded = jnp.pad(frames, ((0, 0), (1, 1), (1, 1), (0, 0)))
    total = jnp.zeros((count * rows * cols, chans), jnp.float32)
    for row_tap in range(3):
        for col_tap in range(3):
            piece = padded[:, row_tap : row_tap + rows, col_tap : col_tap + cols, :].reshape(
                -1, chans
            )
            total = total + jnp.dot(
                piece, kernel[3 * row_tap + col_tap], preferred_element_type=jnp.float32
            )
    return total.reshape(frames.shape)


def spatial_back(grads, kernel):
    count, rows, cols, chans = grads.shape
    padded = jnp.pad(grads, ((0, 0), (1, 1), (1, 1), (0, 0)))
    total = jnp.zeros((count * rows * cols, chans), jnp.float32)
    for row_tap in range(3):
        for col_tap in range(3):
            piece = padded[
                :, 2 - row_tap : 2 - row_tap + rows, 2 - col_tap : 2 - col_tap + cols, :
            ].reshape(-1, chans)
            total = total + jnp.dot(
                piece, kernel[3 * row_tap + col_tap].T, preferred_element_type=jnp.float32
            )
    return total.reshape(grads.shape)


def spatial_wgrad(frames, grads):
    count, rows, cols, chans = frames.shape
    padded = jnp.pad(frames, ((0, 0), (1, 1), (1, 1), (0, 0)))
    flat_grads = grads.reshape(-1, chans)
    result = []
    for row_tap in range(3):
        for col_tap in range(3):
            piece = padded[:, row_tap : row_tap + rows, col_tap : col_tap + cols, :].reshape(
                -1, chans
            )
            result.append(inner(piece, flat_grads))
    return jnp.stack(result)


def shifted(values, offset):
    padded = jnp.pad(values, ((2 * DMAX, 2 * DMAX), (0, 0), (0, 0)))
    start = 2 * DMAX + offset
    return lax.dynamic_slice_in_dim(padded, start, values.shape[0], 0)


def temporal_forward(acts, kernel, step_size):
    chans = acts.shape[2]
    total = jnp.zeros((acts.shape[0] * acts.shape[1], chans), jnp.float32)
    for tap in range(5):
        piece = shifted(acts, (tap - 2) * step_size).reshape(-1, chans)
        total = total + jnp.dot(piece, kernel[tap], preferred_element_type=jnp.float32)
    return total.reshape(acts.shape)


def temporal_back(grads, kernel, step_size):
    chans = grads.shape[2]
    total = jnp.zeros((grads.shape[0] * grads.shape[1], chans), jnp.float32)
    for tap in range(5):
        piece = shifted(grads, (2 - tap) * step_size).reshape(-1, chans)
        total = total + jnp.dot(piece, kernel[tap].T, preferred_element_type=jnp.float32)
    return total.reshape(grads.shape)


def temporal_wgrad(acts, grads, step_size):
    chans = acts.shape[2]
    flat_grads = grads.reshape(-1, chans)
    return jnp.stack(
        [
            inner(shifted(acts, (tap - 2) * step_size).reshape(-1, chans), flat_grads)
            for tap in range(5)
        ]
    )


def to_pixels(flat):
    count = lax.axis_size(("seg", "grp"))
    chans = flat.shape[-1]
    strided = flat.reshape(-1, count, chans)
    return lax.all_to_all(strided, ("seg", "grp"), split_axis=1, concat_axis=1, tiled=True)


def to_frames(blocks):
    out = lax.all_to_all(blocks, ("seg", "grp"), split_axis=1, concat_axis=1, tiled=True)
    return out.reshape(1, -1, blocks.shape[-1])


def shifted1(values, offset):
    padded = jnp.pad(values, ((0, 0), (2 * DMAX, 2 * DMAX), (0, 0)))
    start = 2 * DMAX + offset
    return lax.dynamic_slice_in_dim(padded, start, values.shape[1], 1)


def temporal_forward1(acts, kernel, step_size):
    chans = acts.shape[2]
    total = jnp.zeros((acts.shape[0] * acts.shape[1], chans), jnp.float32)
    for tap in range(5):
        piece = shifted1(acts, (tap - 2) * step_size).reshape(-1, chans)
        total = total + jnp.dot(piece, kernel[tap], preferred_element_type=jnp.float32)
    return total.reshape(acts.shape)


def temporal_back1(grads, kernel, step_size):
    chans = grads.shape[2]
    total = jnp.zeros((grads.shape[0] * grads.shape[1], chans), jnp.float32)
    for tap in range(5):
        piece = shifted1(grads, (2 - tap) * step_size).reshape(-1, chans)
        total = total + jnp.dot(piece, kernel[tap].T, preferred_element_type=jnp.float32)
    return total.reshape(grads.shape)


def temporal_wgrad1(acts, grads, step_size):
    chans = acts.shape[2]
    flat_grads = grads.reshape(-1, chans)
    return jnp.stack(
        [
            inner(shifted1(acts, (tap - 2) * step_size).reshape(-1, chans), flat_grads)
            for tap in range(5)
        ]
    )


JB = 10


def shift_matrix(offset, size):
    rows = lax.broadcasted_iota(jnp.int32, (size, size), 0)
    cols = lax.broadcasted_iota(jnp.int32, (size, size), 1)
    return (cols == rows + offset).astype(jnp.bfloat16)


def shifted_taps(x_ref, step, sign):
    blocks, frames, chans = x_ref.shape
    wide = jnp.concatenate([x_ref[j] for j in range(blocks)], axis=1)
    taps = []
    for tap in range(5):
        if tap == 2:
            taps.append(None)
            continue
        moved = jnp.dot(
            shift_matrix(sign * (tap - 2) * step, frames), wide,
            preferred_element_type=jnp.float32,
        ).astype(jnp.bfloat16)
        taps.append(moved)
    rows = []
    for j in range(blocks):
        parts = []
        for tap in range(5):
            if tap == 2:
                parts.append(x_ref[j])
            else:
                parts.append(taps[tap][:, j * chans : (j + 1) * chans])
        rows.append(jnp.concatenate(parts, axis=1))
    return jnp.concatenate(rows, axis=0)


def tfwd_kernel(dil_ref, act_ref, w_ref, pre_ref, out_ref):
    blocks, frames, chans = act_ref.shape
    stacked = shifted_taps(act_ref, dil_ref[0], 1)
    pre = jnp.dot(stacked, w_ref[...], preferred_element_type=jnp.float32)
    pre_ref[...] = pre.reshape(blocks, frames, chans)
    out_ref[...] = (pre / (1.0 + jnp.exp(-pre))).astype(jnp.bfloat16).reshape(blocks, frames, chans)


def temporal_forward_k(acts, kernel, step_size):
    count, frames, chans = acts.shape
    spec = pl.BlockSpec((JB, frames, chans), lambda j, d: (j, 0, 0))
    return pl.pallas_call(
        tfwd_kernel,
        grid_spec=pltpu.PrefetchScalarGridSpec(
            num_scalar_prefetch=1,
            grid=(count // JB,),
            in_specs=[spec, pl.BlockSpec((5 * chans, chans), lambda j, d: (0, 0))],
            out_specs=[spec, spec],
        ),
        out_shape=[
            jax.ShapeDtypeStruct(acts.shape, jnp.float32),
            jax.ShapeDtypeStruct(acts.shape, jnp.bfloat16),
        ],
        cost_estimate=pl.CostEstimate(
            flops=2 * count * frames * chans * chans * 9,
            transcendentals=count * frames * chans,
            bytes_accessed=count * frames * chans * 8,
        ),
    )(step_size.reshape(1), acts, kernel.reshape(5 * chans, chans))


def tbwd_kernel(with_pre, dil_ref, act_ref, grad_ref, wt_ref, *rest):
    if with_pre:
        pre_ref, out_ref, tg_ref = rest
    else:
        out_ref, tg_ref = rest
    blocks, frames, chans = act_ref.shape
    stacked = shifted_taps(grad_ref, dil_ref[0], -1)
    grad_act = None
    for tap in range(5):
        term = lax.dot_general(
            stacked[:, tap * chans : (tap + 1) * chans],
            wt_ref[tap * chans : (tap + 1) * chans, :],
            (((1,), (1,)), ((), ())),
            preferred_element_type=jnp.float32,
        )
        grad_act = term if grad_act is None else grad_act + term
    flat_act = act_ref[...].reshape(blocks * frames, chans)
    part = lax.dot_general(
        flat_act, stacked, (((0,), (0,)), ((), ())), preferred_element_type=jnp.float32
    )

    @pl.when(pl.program_id(0) == 0)
    def _():
        tg_ref[...] = jnp.zeros_like(tg_ref)

    for tap in range(5):
        tg_ref[tap] += part[:, tap * chans : (tap + 1) * chans]
    if with_pre:
        pre = pre_ref[...].reshape(blocks * frames, chans)
        sigma = 1.0 / (1.0 + jnp.exp(-pre))
        grad_act = grad_act * (sigma * (1.0 + pre * (1.0 - sigma)))
    out_ref[...] = grad_act.astype(jnp.bfloat16).reshape(blocks, frames, chans)


def temporal_backward_k(acts, grads, kernel, step_size, pre_below):
    count, frames, chans = acts.shape
    spec = pl.BlockSpec((JB, frames, chans), lambda j, d: (j, 0, 0))
    wt = kernel.reshape(5 * chans, chans)
    with_pre = pre_below is not None
    in_specs = [spec, spec, pl.BlockSpec((5 * chans, chans), lambda j, d: (0, 0))]
    operands = [step_size.reshape(1), acts, grads, wt]
    if with_pre:
        in_specs.append(spec)
        operands.append(pre_below)
    out, tg = pl.pallas_call(
        functools.partial(tbwd_kernel, with_pre),
        grid_spec=pltpu.PrefetchScalarGridSpec(
            num_scalar_prefetch=1,
            grid=(count // JB,),
            in_specs=in_specs,
            out_specs=[spec, pl.BlockSpec((5, chans, chans), lambda j, d: (0, 0, 0))],
        ),
        out_shape=[
            jax.ShapeDtypeStruct(acts.shape, jnp.bfloat16),
            jax.ShapeDtypeStruct((5, chans, chans), jnp.float32),
        ],
        compiler_params=pltpu.CompilerParams(dimension_semantics=("arbitrary",)),
        cost_estimate=pl.CostEstimate(
            flops=2 * count * frames * chans * chans * 14,
            transcendentals=count * frames * chans,
            bytes_accessed=count * frames * chans * 10,
        ),
    )(*operands)
    return out, tg


def all_sum(parts, scale):
    chans = parts[0].shape[-1]
    count = lax.axis_size(("seg", "grp"))
    rows = [p.reshape(-1, chans) for p in parts]
    used = sum(r.shape[0] for r in rows)
    per = -(-used // (count * 8)) * 8
    rows.append(jnp.zeros((per * count - used, chans), jnp.float32))
    stack = jnp.concatenate(rows, axis=0).reshape(count, per, chans)
    pieces = lax.all_to_all(stack, ("seg", "grp"), split_axis=0, concat_axis=0, tiled=True)
    mine = (jnp.sum(pieces, axis=0, keepdims=True) * scale).astype(jnp.bfloat16)
    spread = jnp.broadcast_to(mine, stack.shape)
    whole = lax.all_to_all(spread, ("seg", "grp"), split_axis=0, concat_axis=0, tiled=True)
    whole = whole.astype(jnp.float32).reshape(-1, chans)
    out = []
    offset = 0
    for p in parts:
        size = p.size // chans
        out.append(whole[offset : offset + size].reshape(p.shape))
        offset += size
    return out


def local(
    frames_in, spatial_weight, temporal_weight, uniting_weight, key_index, dilation, cotangent
):
    local_frames, rows, cols, chans = frames_in.shape
    pixels = rows * cols
    seg_count = lax.axis_size("seg")
    pre_spatial = spatial_forward(frames_in, spatial_weight)
    act_zero = jax.nn.silu(pre_spatial).astype(jnp.bfloat16).reshape(local_frames, pixels, chans)
    cot_local = cotangent.reshape(local_frames, pixels, chans)
    act_blocks = to_pixels(act_zero)
    act_blocks, cot_local = lax.optimization_barrier((act_blocks, cot_local))
    cot_blocks = to_pixels(cot_local)
    acts = [act_blocks]
    block, total_frames = act_blocks.shape[0], act_blocks.shape[1]
    seg_frames = total_frames // seg_count
    pres = []
    for layer in range(LAYERS):
        pre, act = temporal_forward_k(acts[-1], temporal_weight[layer], dilation[layer])
        pres.append(pre)
        acts.append(act)
    feat = acts[-1]
    seg_shape = (block, seg_count, seg_frames, chans)
    feat_seg = feat.reshape(seg_shape)
    positions = jnp.arange(seg_frames, dtype=jnp.int32)
    onehot = positions[None, :] == key_index[:, None]
    keys = jnp.einsum(
        "ns,jnsc->jnc", onehot.astype(jnp.bfloat16), feat_seg, preferred_element_type=jnp.float32
    ).astype(jnp.bfloat16)
    key_full = jnp.broadcast_to(keys[:, :, None], seg_shape).reshape(-1, chans)
    feat_flat = feat.reshape(-1, chans)
    key_part = jnp.dot(
        keys.reshape(-1, chans), uniting_weight[1], preferred_element_type=jnp.float32
    ).reshape(block, seg_count, 1, chans)
    main_part = jnp.dot(feat_flat, uniting_weight[0], preferred_element_type=jnp.float32)
    united_blocks = (main_part.reshape(seg_shape) + key_part).astype(jnp.bfloat16)
    united = to_frames(united_blocks.reshape(block, total_frames, chans))
    cot_flat = cot_blocks.reshape(-1, chans)
    grad_feat = jnp.dot(cot_flat, uniting_weight[0].T, preferred_element_type=jnp.float32)
    seg_cot = jnp.sum(cot_blocks.reshape(seg_shape).astype(jnp.float32), axis=2)
    key_term = jnp.dot(
        seg_cot.reshape(-1, chans),
        uniting_weight[1].T.astype(jnp.float32),
        precision=lax.Precision.HIGHEST,
    ).reshape(block, seg_count, 1, chans)
    placed = onehot.astype(jnp.float32)[None, :, :, None] * key_term
    grad_feat = grad_feat.reshape(seg_shape) + placed
    grad_feat = grad_feat.reshape(block, total_frames, chans)
    grad_uniting = jnp.stack([inner(feat_flat, cot_flat), inner(key_full, cot_flat)])
    grad_pre = (grad_feat * silu_grad(pres[-1])).astype(jnp.bfloat16)
    tgrads = [None] * LAYERS
    for layer in range(LAYERS - 1, -1, -1):
        below = pres[layer - 1] if layer > 0 else None
        grad_pre, tgrads[layer] = temporal_backward_k(
            acts[layer], grad_pre, temporal_weight[layer], dilation[layer], below
        )
    grad_act0 = grad_pre
    grad_time = to_frames(grad_act0).reshape(frames_in.shape)
    grad_spre = (grad_time.astype(jnp.float32) * silu_grad(pre_spatial)).astype(jnp.bfloat16)
    grad_frames = spatial_back(grad_spre, spatial_weight).astype(jnp.bfloat16)
    grad_spatial = spatial_wgrad(frames_in, grad_spre)
    scale = 1.0 / jnp.sqrt(jnp.float32(total_frames * pixels))
    summed = all_sum((grad_spatial, jnp.stack(tgrads), grad_uniting), scale)
    return (
        united.reshape(frames_in.shape),
        grad_frames,
        summed[0],
        summed[1],
        summed[2],
    )


def solution(mesh):
    placed = (
        P(("seg", "grp"), None, None, None),
        P(),
        P(),
        P(),
        P(),
        P(),
        P(("seg", "grp"), None, None, None),
    )
    return jax.shard_map(
        local,
        mesh=mesh,
        in_specs=placed,
        out_specs=(
            P(("seg", "grp"), None, None, None),
            P(("seg", "grp"), None, None, None),
            P(),
            P(),
            P(),
        ),
        check_vma=False,
    )
```

```python
import functools

import jax
import jax.numpy as jnp
from jax import lax
from jax.sharding import PartitionSpec as P
from jax.experimental import pallas as pl
from jax.experimental.pallas import tpu as pltpu

LAYERS = 2
DMAX = 8


def from_root(value, axis, root):
    mine = lax.axis_index(axis) == root
    return lax.psum(jnp.where(mine, value, jnp.zeros_like(value)), axis)


def silu_grad(value):
    sigma = jax.nn.sigmoid(value)
    return sigma * (1.0 + value * (1.0 - sigma))


def inner(left, right):
    return lax.dot_general(
        left, right, (((0,), (0,)), ((), ())), preferred_element_type=jnp.float32
    )


def spatial_forward(frames, kernel):
    count, rows, cols, chans = frames.shape
    padded = jnp.pad(frames, ((0, 0), (1, 1), (1, 1), (0, 0)))
    total = jnp.zeros((count * rows * cols, chans), jnp.float32)
    for row_tap in range(3):
        for col_tap in range(3):
            piece = padded[:, row_tap : row_tap + rows, col_tap : col_tap + cols, :].reshape(
                -1, chans
            )
            total = total + jnp.dot(
                piece, kernel[3 * row_tap + col_tap], preferred_element_type=jnp.float32
            )
    return total.reshape(frames.shape)


def spatial_back(grads, kernel):
    count, rows, cols, chans = grads.shape
    padded = jnp.pad(grads, ((0, 0), (1, 1), (1, 1), (0, 0)))
    total = jnp.zeros((count * rows * cols, chans), jnp.float32)
    for row_tap in range(3):
        for col_tap in range(3):
            piece = padded[
                :, 2 - row_tap : 2 - row_tap + rows, 2 - col_tap : 2 - col_tap + cols, :
            ].reshape(-1, chans)
            total = total + jnp.dot(
                piece, kernel[3 * row_tap + col_tap].T, preferred_element_type=jnp.float32
            )
    return total.reshape(grads.shape)


def spatial_wgrad(frames, grads):
    count, rows, cols, chans = frames.shape
    padded = jnp.pad(frames, ((0, 0), (1, 1), (1, 1), (0, 0)))
    flat_grads = grads.reshape(-1, chans)
    result = []
    for row_tap in range(3):
        for col_tap in range(3):
            piece = padded[:, row_tap : row_tap + rows, col_tap : col_tap + cols, :].reshape(
                -1, chans
            )
            result.append(inner(piece, flat_grads))
    return jnp.stack(result)


def shifted(values, offset):
    padded = jnp.pad(values, ((2 * DMAX, 2 * DMAX), (0, 0), (0, 0)))
    start = 2 * DMAX + offset
    return lax.dynamic_slice_in_dim(padded, start, values.shape[0], 0)


def temporal_forward(acts, kernel, step_size):
    chans = acts.shape[2]
    total = jnp.zeros((acts.shape[0] * acts.shape[1], chans), jnp.float32)
    for tap in range(5):
        piece = shifted(acts, (tap - 2) * step_size).reshape(-1, chans)
        total = total + jnp.dot(piece, kernel[tap], preferred_element_type=jnp.float32)
    return total.reshape(acts.shape)


def temporal_back(grads, kernel, step_size):
    chans = grads.shape[2]
    total = jnp.zeros((grads.shape[0] * grads.shape[1], chans), jnp.float32)
    for tap in range(5):
        piece = shifted(grads, (2 - tap) * step_size).reshape(-1, chans)
        total = total + jnp.dot(piece, kernel[tap].T, preferred_element_type=jnp.float32)
    return total.reshape(grads.shape)


def temporal_wgrad(acts, grads, step_size):
    chans = acts.shape[2]
    flat_grads = grads.reshape(-1, chans)
    return jnp.stack(
        [
            inner(shifted(acts, (tap - 2) * step_size).reshape(-1, chans), flat_grads)
            for tap in range(5)
        ]
    )


def to_pixels(flat):
    count = lax.axis_size(("seg", "grp"))
    chans = flat.shape[-1]
    strided = flat.reshape(-1, count, chans)
    return lax.all_to_all(strided, ("seg", "grp"), split_axis=1, concat_axis=1, tiled=True)


def to_frames(blocks):
    out = lax.all_to_all(blocks, ("seg", "grp"), split_axis=1, concat_axis=1, tiled=True)
    return out.reshape(1, -1, blocks.shape[-1])


def shifted1(values, offset):
    padded = jnp.pad(values, ((0, 0), (2 * DMAX, 2 * DMAX), (0, 0)))
    start = 2 * DMAX + offset
    return lax.dynamic_slice_in_dim(padded, start, values.shape[1], 1)


def temporal_forward1(acts, kernel, step_size):
    chans = acts.shape[2]
    total = jnp.zeros((acts.shape[0] * acts.shape[1], chans), jnp.float32)
    for tap in range(5):
        piece = shifted1(acts, (tap - 2) * step_size).reshape(-1, chans)
        total = total + jnp.dot(piece, kernel[tap], preferred_element_type=jnp.float32)
    return total.reshape(acts.shape)


def temporal_back1(grads, kernel, step_size):
    chans = grads.shape[2]
    total = jnp.zeros((grads.shape[0] * grads.shape[1], chans), jnp.float32)
    for tap in range(5):
        piece = shifted1(grads, (2 - tap) * step_size).reshape(-1, chans)
        total = total + jnp.dot(piece, kernel[tap].T, preferred_element_type=jnp.float32)
    return total.reshape(grads.shape)


def temporal_wgrad1(acts, grads, step_size):
    chans = acts.shape[2]
    flat_grads = grads.reshape(-1, chans)
    return jnp.stack(
        [
            inner(shifted1(acts, (tap - 2) * step_size).reshape(-1, chans), flat_grads)
            for tap in range(5)
        ]
    )


HALO = 2 * DMAX
FB = 16


def fm_to_pixels(flat):
    count = lax.axis_size(("seg", "grp"))
    chans = flat.shape[-1]
    strided = flat.reshape(-1, count, chans)
    rows = -(-strided.shape[0] // 16) * 16
    strided = jnp.pad(strided, ((0, rows - strided.shape[0]), (0, 0), (0, 0)))
    out = lax.all_to_all(strided, ("seg", "grp"), split_axis=1, concat_axis=1, tiled=True)
    return jnp.transpose(out, (1, 0, 2))


def fm_to_frames(blocks, used):
    moved = jnp.transpose(blocks, (1, 0, 2))
    out = lax.all_to_all(moved, ("seg", "grp"), split_axis=1, concat_axis=1, tiled=True)
    return out[:used].reshape(1, -1, blocks.shape[-1])


def fill_halo(src_ref, pad_ref):
    frames = src_ref.shape[0]
    zeros = jnp.zeros((HALO,) + pad_ref.shape[1:], pad_ref.dtype)
    pad_ref[0:HALO] = zeros
    pad_ref[HALO + frames : 2 * HALO + frames] = zeros
    pad_ref[HALO : HALO + frames] = src_ref[...]


def tap_rows(pad_ref, start, rows):
    return pad_ref[pl.ds(start, FB)].reshape(rows, pad_ref.shape[-1])


def tfwd_kernel(dil_ref, act_ref, w_ref, pre_ref, out_ref, pad_ref):
    frames, width, chans = act_ref.shape
    fill_halo(act_ref, pad_ref)
    step = dil_ref[0]
    rows = FB * width
    for block in range(frames // FB):
        base = HALO + block * FB
        stacked = jnp.concatenate(
            [tap_rows(pad_ref, base + (tap - 2) * step, rows) for tap in range(5)], axis=1
        )
        pre = jnp.dot(stacked, w_ref[...], preferred_element_type=jnp.float32)
        pre_ref[block * FB : (block + 1) * FB] = pre.reshape(FB, width, chans)
        out_ref[block * FB : (block + 1) * FB] = (
            (pre / (1.0 + jnp.exp(-pre))).astype(jnp.bfloat16).reshape(FB, width, chans)
        )


def temporal_forward_k(acts, kernel, step_size):
    frames, width, chans = acts.shape
    return pl.pallas_call(
        tfwd_kernel,
        grid_spec=pltpu.PrefetchScalarGridSpec(
            num_scalar_prefetch=1,
            grid=(1,),
            in_specs=[
                pl.BlockSpec(acts.shape, lambda i, d: (0, 0, 0)),
                pl.BlockSpec((5 * chans, chans), lambda i, d: (0, 0)),
            ],
            out_specs=[
                pl.BlockSpec(acts.shape, lambda i, d: (0, 0, 0)),
                pl.BlockSpec(acts.shape, lambda i, d: (0, 0, 0)),
            ],
            scratch_shapes=[pltpu.VMEM((frames + 2 * HALO, width, chans), jnp.bfloat16)],
        ),
        out_shape=[
            jax.ShapeDtypeStruct(acts.shape, jnp.float32),
            jax.ShapeDtypeStruct(acts.shape, jnp.bfloat16),
        ],
        cost_estimate=pl.CostEstimate(
            flops=2 * frames * width * chans * chans * 5,
            transcendentals=frames * width * chans,
            bytes_accessed=frames * width * chans * 8,
        ),
    )(step_size.reshape(1), acts, kernel.reshape(5 * chans, chans))


def tbwd_kernel(with_pre, dil_ref, act_ref, grad_ref, wt_ref, *rest):
    if with_pre:
        pre_ref, out_ref, tg_ref, pad_ref = rest
    else:
        out_ref, tg_ref, pad_ref = rest
    frames, width, chans = act_ref.shape
    fill_halo(grad_ref, pad_ref)
    step = dil_ref[0]
    rows = FB * width
    total = None
    for block in range(frames // FB):
        base = HALO + block * FB
        stacked = jnp.concatenate(
            [tap_rows(pad_ref, base - (tap - 2) * step, rows) for tap in range(5)], axis=1
        )
        grad_act = None
        for tap in range(5):
            term = lax.dot_general(
                stacked[:, tap * chans : (tap + 1) * chans],
                wt_ref[tap * chans : (tap + 1) * chans, :],
                (((1,), (1,)), ((), ())),
                preferred_element_type=jnp.float32,
            )
            grad_act = term if grad_act is None else grad_act + term
        flat_act = act_ref[block * FB : (block + 1) * FB].reshape(rows, chans)
        part = lax.dot_general(
            flat_act, stacked, (((0,), (0,)), ((), ())), preferred_element_type=jnp.float32
        )
        total = part if total is None else total + part
        if with_pre:
            pre = pre_ref[block * FB : (block + 1) * FB].reshape(rows, chans)
            sigma = 1.0 / (1.0 + jnp.exp(-pre))
            grad_act = grad_act * (sigma * (1.0 + pre * (1.0 - sigma)))
        out_ref[block * FB : (block + 1) * FB] = (
            grad_act.astype(jnp.bfloat16).reshape(FB, width, chans)
        )
    for tap in range(5):
        tg_ref[tap] = total[:, tap * chans : (tap + 1) * chans]


def temporal_backward_k(acts, grads, kernel, step_size, pre_below):
    frames, width, chans = acts.shape
    full = pl.BlockSpec(acts.shape, lambda i, d: (0, 0, 0))
    with_pre = pre_below is not None
    in_specs = [full, full, pl.BlockSpec((5 * chans, chans), lambda i, d: (0, 0))]
    operands = [step_size.reshape(1), acts, grads, kernel.reshape(5 * chans, chans)]
    if with_pre:
        in_specs.append(full)
        operands.append(pre_below)
    out, tg = pl.pallas_call(
        functools.partial(tbwd_kernel, with_pre),
        grid_spec=pltpu.PrefetchScalarGridSpec(
            num_scalar_prefetch=1,
            grid=(1,),
            in_specs=in_specs,
            out_specs=[full, pl.BlockSpec((5, chans, chans), lambda i, d: (0, 0, 0))],
            scratch_shapes=[pltpu.VMEM((frames + 2 * HALO, width, chans), jnp.bfloat16)],
        ),
        out_shape=[
            jax.ShapeDtypeStruct(acts.shape, jnp.bfloat16),
            jax.ShapeDtypeStruct((5, chans, chans), jnp.float32),
        ],
        cost_estimate=pl.CostEstimate(
            flops=2 * frames * width * chans * chans * 10,
            transcendentals=frames * width * chans,
            bytes_accessed=frames * width * chans * 10,
        ),
    )(*operands)
    return out, tg


def all_sum(parts, scale):
    chans = parts[0].shape[-1]
    count = lax.axis_size(("seg", "grp"))
    rows = [p.reshape(-1, chans) for p in parts]
    used = sum(r.shape[0] for r in rows)
    per = -(-used // (count * 8)) * 8
    rows.append(jnp.zeros((per * count - used, chans), jnp.float32))
    stack = jnp.concatenate(rows, axis=0).reshape(count, per, chans)
    pieces = lax.all_to_all(stack, ("seg", "grp"), split_axis=0, concat_axis=0, tiled=True)
    mine = (jnp.sum(pieces, axis=0, keepdims=True) * scale).astype(jnp.bfloat16)
    spread = jnp.broadcast_to(mine, stack.shape)
    whole = lax.all_to_all(spread, ("seg", "grp"), split_axis=0, concat_axis=0, tiled=True)
    whole = whole.astype(jnp.float32).reshape(-1, chans)
    out = []
    offset = 0
    for p in parts:
        size = p.size // chans
        out.append(whole[offset : offset + size].reshape(p.shape))
        offset += size
    return out


def local(
    frames_in, spatial_weight, temporal_weight, uniting_weight, key_index, dilation, cotangent
):
    local_frames, rows, cols, chans = frames_in.shape
    pixels = rows * cols
    seg_count = lax.axis_size("seg")
    count = lax.axis_size(("seg", "grp"))
    used = pixels // count
    pre_spatial = spatial_forward(frames_in, spatial_weight)
    act_zero = jax.nn.silu(pre_spatial).astype(jnp.bfloat16).reshape(local_frames, pixels, chans)
    cot_local = cotangent.reshape(local_frames, pixels, chans)
    act_blocks = fm_to_pixels(act_zero)
    act_blocks, cot_local = lax.optimization_barrier((act_blocks, cot_local))
    cot_blocks = fm_to_pixels(cot_local)
    acts = [act_blocks]
    total_frames, width = act_blocks.shape[0], act_blocks.shape[1]
    seg_frames = total_frames // seg_count
    pres = []
    for layer in range(LAYERS):
        pre, act = temporal_forward_k(acts[-1], temporal_weight[layer], dilation[layer])
        pres.append(pre)
        acts.append(act)
    feat = acts[-1]
    seg_shape = (seg_count, seg_frames, width, chans)
    feat_seg = feat.reshape(seg_shape)
    positions = jnp.arange(seg_frames, dtype=jnp.int32)
    onehot = positions[None, :] == key_index[:, None]
    keys = jnp.einsum(
        "ns,nsjc->njc", onehot.astype(jnp.bfloat16), feat_seg, preferred_element_type=jnp.float32
    ).astype(jnp.bfloat16)
    key_full = jnp.broadcast_to(keys[:, None], seg_shape).reshape(-1, chans)
    feat_flat = feat.reshape(-1, chans)
    key_part = jnp.dot(
        keys.reshape(-1, chans), uniting_weight[1], preferred_element_type=jnp.float32
    ).reshape(seg_count, 1, width, chans)
    main_part = jnp.dot(feat_flat, uniting_weight[0], preferred_element_type=jnp.float32)
    united_blocks = (main_part.reshape(seg_shape) + key_part).astype(jnp.bfloat16)
    united = fm_to_frames(united_blocks.reshape(total_frames, width, chans), used)
    cot_flat = cot_blocks.reshape(-1, chans)
    grad_feat = jnp.dot(cot_flat, uniting_weight[0].T, preferred_element_type=jnp.float32)
    seg_cot = jnp.sum(cot_blocks.reshape(seg_shape).astype(jnp.float32), axis=1)
    key_term = jnp.dot(
        seg_cot.reshape(-1, chans),
        uniting_weight[1].T.astype(jnp.float32),
        precision=lax.Precision.HIGHEST,
    ).reshape(seg_count, 1, width, chans)
    placed = onehot.astype(jnp.float32)[:, :, None, None] * key_term
    grad_feat = grad_feat.reshape(seg_shape) + placed
    grad_feat = grad_feat.reshape(total_frames, width, chans)
    grad_uniting = jnp.stack([inner(feat_flat, cot_flat), inner(key_full, cot_flat)])
    grad_pre = (grad_feat * silu_grad(pres[-1])).astype(jnp.bfloat16)
    tgrads = [None] * LAYERS
    for layer in range(LAYERS - 1, -1, -1):
        below = pres[layer - 1] if layer > 0 else None
        grad_pre, tgrads[layer] = temporal_backward_k(
            acts[layer], grad_pre, temporal_weight[layer], dilation[layer], below
        )
    grad_act0 = grad_pre
    grad_time = fm_to_frames(grad_act0, used).reshape(frames_in.shape)
    grad_spre = (grad_time.astype(jnp.float32) * silu_grad(pre_spatial)).astype(jnp.bfloat16)
    grad_frames = spatial_back(grad_spre, spatial_weight).astype(jnp.bfloat16)
    grad_spatial = spatial_wgrad(frames_in, grad_spre)
    scale = 1.0 / jnp.sqrt(jnp.float32(total_frames * pixels))
    summed = all_sum((grad_spatial, jnp.stack(tgrads), grad_uniting), scale)
    return (
        united.reshape(frames_in.shape),
        grad_frames,
        summed[0],
        summed[1],
        summed[2],
    )


def solution(mesh):
    placed = (
        P(("seg", "grp"), None, None, None),
        P(),
        P(),
        P(),
        P(),
        P(),
        P(("seg", "grp"), None, None, None),
    )
    return jax.shard_map(
        local,
        mesh=mesh,
        in_specs=placed,
        out_specs=(
            P(("seg", "grp"), None, None, None),
            P(("seg", "grp"), None, None, None),
            P(),
            P(),
            P(),
        ),
        check_vma=False,
    )
```

```python
import functools

import jax
import jax.numpy as jnp
from jax import lax
from jax.sharding import PartitionSpec as P
from jax.experimental import pallas as pl
from jax.experimental.pallas import tpu as pltpu

LAYERS = 2
DMAX = 8


def from_root(value, axis, root):
    mine = lax.axis_index(axis) == root
    return lax.psum(jnp.where(mine, value, jnp.zeros_like(value)), axis)


def silu_grad(value):
    sigma = jax.nn.sigmoid(value)
    return sigma * (1.0 + value * (1.0 - sigma))


def inner(left, right):
    return lax.dot_general(
        left, right, (((0,), (0,)), ((), ())), preferred_element_type=jnp.float32
    )


def spatial_forward(frames, kernel):
    count, rows, cols, chans = frames.shape
    padded = jnp.pad(frames, ((0, 0), (1, 1), (1, 1), (0, 0)))
    total = jnp.zeros((count * rows * cols, chans), jnp.float32)
    for row_tap in range(3):
        for col_tap in range(3):
            piece = padded[:, row_tap : row_tap + rows, col_tap : col_tap + cols, :].reshape(
                -1, chans
            )
            total = total + jnp.dot(
                piece, kernel[3 * row_tap + col_tap], preferred_element_type=jnp.float32
            )
    return total.reshape(frames.shape)


def spatial_back(grads, kernel):
    count, rows, cols, chans = grads.shape
    padded = jnp.pad(grads, ((0, 0), (1, 1), (1, 1), (0, 0)))
    total = jnp.zeros((count * rows * cols, chans), jnp.float32)
    for row_tap in range(3):
        for col_tap in range(3):
            piece = padded[
                :, 2 - row_tap : 2 - row_tap + rows, 2 - col_tap : 2 - col_tap + cols, :
            ].reshape(-1, chans)
            total = total + jnp.dot(
                piece, kernel[3 * row_tap + col_tap].T, preferred_element_type=jnp.float32
            )
    return total.reshape(grads.shape)


def spatial_wgrad(frames, grads):
    count, rows, cols, chans = frames.shape
    padded = jnp.pad(frames, ((0, 0), (1, 1), (1, 1), (0, 0)))
    flat_grads = grads.reshape(-1, chans)
    result = []
    for row_tap in range(3):
        for col_tap in range(3):
            piece = padded[:, row_tap : row_tap + rows, col_tap : col_tap + cols, :].reshape(
                -1, chans
            )
            result.append(inner(piece, flat_grads))
    return jnp.stack(result)


def shifted(values, offset):
    padded = jnp.pad(values, ((2 * DMAX, 2 * DMAX), (0, 0), (0, 0)))
    start = 2 * DMAX + offset
    return lax.dynamic_slice_in_dim(padded, start, values.shape[0], 0)


def temporal_forward(acts, kernel, step_size):
    chans = acts.shape[2]
    total = jnp.zeros((acts.shape[0] * acts.shape[1], chans), jnp.float32)
    for tap in range(5):
        piece = shifted(acts, (tap - 2) * step_size).reshape(-1, chans)
        total = total + jnp.dot(piece, kernel[tap], preferred_element_type=jnp.float32)
    return total.reshape(acts.shape)


def temporal_back(grads, kernel, step_size):
    chans = grads.shape[2]
    total = jnp.zeros((grads.shape[0] * grads.shape[1], chans), jnp.float32)
    for tap in range(5):
        piece = shifted(grads, (2 - tap) * step_size).reshape(-1, chans)
        total = total + jnp.dot(piece, kernel[tap].T, preferred_element_type=jnp.float32)
    return total.reshape(grads.shape)


def temporal_wgrad(acts, grads, step_size):
    chans = acts.shape[2]
    flat_grads = grads.reshape(-1, chans)
    return jnp.stack(
        [
            inner(shifted(acts, (tap - 2) * step_size).reshape(-1, chans), flat_grads)
            for tap in range(5)
        ]
    )


def to_pixels(flat):
    count = lax.axis_size(("seg", "grp"))
    chans = flat.shape[-1]
    strided = flat.reshape(-1, count, chans)
    return lax.all_to_all(strided, ("seg", "grp"), split_axis=1, concat_axis=1, tiled=True)


def to_frames(blocks):
    out = lax.all_to_all(blocks, ("seg", "grp"), split_axis=1, concat_axis=1, tiled=True)
    return out.reshape(1, -1, blocks.shape[-1])


def shifted1(values, offset):
    padded = jnp.pad(values, ((0, 0), (2 * DMAX, 2 * DMAX), (0, 0)))
    start = 2 * DMAX + offset
    return lax.dynamic_slice_in_dim(padded, start, values.shape[1], 1)


def temporal_forward1(acts, kernel, step_size):
    chans = acts.shape[2]
    total = jnp.zeros((acts.shape[0] * acts.shape[1], chans), jnp.float32)
    for tap in range(5):
        piece = shifted1(acts, (tap - 2) * step_size).reshape(-1, chans)
        total = total + jnp.dot(piece, kernel[tap], preferred_element_type=jnp.float32)
    return total.reshape(acts.shape)


def temporal_back1(grads, kernel, step_size):
    chans = grads.shape[2]
    total = jnp.zeros((grads.shape[0] * grads.shape[1], chans), jnp.float32)
    for tap in range(5):
        piece = shifted1(grads, (2 - tap) * step_size).reshape(-1, chans)
        total = total + jnp.dot(piece, kernel[tap].T, preferred_element_type=jnp.float32)
    return total.reshape(grads.shape)


def temporal_wgrad1(acts, grads, step_size):
    chans = acts.shape[2]
    flat_grads = grads.reshape(-1, chans)
    return jnp.stack(
        [
            inner(shifted1(acts, (tap - 2) * step_size).reshape(-1, chans), flat_grads)
            for tap in range(5)
        ]
    )


HALO = 2 * DMAX
FB = 16


def fm_to_pixels(flat):
    count = lax.axis_size(("seg", "grp"))
    chans = flat.shape[-1]
    strided = flat.reshape(-1, count, chans)
    rows = -(-strided.shape[0] // 16) * 16
    strided = jnp.pad(strided, ((0, rows - strided.shape[0]), (0, 0), (0, 0)))
    out = lax.all_to_all(strided, ("seg", "grp"), split_axis=1, concat_axis=1, tiled=True)
    return jnp.transpose(out, (1, 0, 2))


def fm_to_frames(blocks, used):
    moved = jnp.transpose(blocks, (1, 0, 2))
    out = lax.all_to_all(moved, ("seg", "grp"), split_axis=1, concat_axis=1, tiled=True)
    return out[:used].reshape(1, -1, blocks.shape[-1])


def fill_halo(src_ref, pad_ref):
    frames = src_ref.shape[0]
    zeros = jnp.zeros((HALO,) + pad_ref.shape[1:], pad_ref.dtype)
    pad_ref[0:HALO] = zeros
    pad_ref[HALO + frames : 2 * HALO + frames] = zeros
    pad_ref[HALO : HALO + frames] = src_ref[...]


def tap_rows(pad_ref, start, rows):
    return pad_ref[pl.ds(start, FB)].reshape(rows, pad_ref.shape[-1])


def tfwd_kernel(dil_ref, act_ref, w_ref, pre_ref, out_ref, pad_ref):
    frames, width, chans = act_ref.shape
    fill_halo(act_ref, pad_ref)
    step = dil_ref[0]
    rows = FB * width

    def body(block, carry):
        first = pl.multiple_of(block * FB, FB)
        stacked = jnp.concatenate(
            [tap_rows(pad_ref, HALO + first + (tap - 2) * step, rows) for tap in range(5)], axis=1
        )
        pre = jnp.dot(stacked, w_ref[...], preferred_element_type=jnp.float32)
        pre_ref[pl.ds(first, FB)] = pre.reshape(FB, width, chans)
        out_ref[pl.ds(first, FB)] = (
            (pre / (1.0 + jnp.exp(-pre))).astype(jnp.bfloat16).reshape(FB, width, chans)
        )
        return carry

    lax.fori_loop(0, frames // FB, body, 0)


def temporal_forward_k(acts, kernel, step_size):
    frames, width, chans = acts.shape
    return pl.pallas_call(
        tfwd_kernel,
        grid_spec=pltpu.PrefetchScalarGridSpec(
            num_scalar_prefetch=1,
            grid=(1,),
            in_specs=[
                pl.BlockSpec(acts.shape, lambda i, d: (0, 0, 0)),
                pl.BlockSpec((5 * chans, chans), lambda i, d: (0, 0)),
            ],
            out_specs=[
                pl.BlockSpec(acts.shape, lambda i, d: (0, 0, 0)),
                pl.BlockSpec(acts.shape, lambda i, d: (0, 0, 0)),
            ],
            scratch_shapes=[pltpu.VMEM((frames + 2 * HALO, width, chans), jnp.bfloat16)],
        ),
        out_shape=[
            jax.ShapeDtypeStruct(acts.shape, jnp.float32),
            jax.ShapeDtypeStruct(acts.shape, jnp.bfloat16),
        ],
        cost_estimate=pl.CostEstimate(
            flops=2 * frames * width * chans * chans * 5,
            transcendentals=frames * width * chans,
            bytes_accessed=frames * width * chans * 8,
        ),
    )(step_size.reshape(1), acts, kernel.reshape(5 * chans, chans))


def tbwd_kernel(with_pre, dil_ref, act_ref, grad_ref, wt_ref, *rest):
    if with_pre:
        pre_ref, out_ref, tg_ref, pad_ref = rest
    else:
        out_ref, tg_ref, pad_ref = rest
    frames, width, chans = act_ref.shape
    fill_halo(grad_ref, pad_ref)
    step = dil_ref[0]
    rows = FB * width
    tg_ref[...] = jnp.zeros_like(tg_ref)

    def body(block, carry):
        first = pl.multiple_of(block * FB, FB)
        stacked = jnp.concatenate(
            [tap_rows(pad_ref, HALO + first - (tap - 2) * step, rows) for tap in range(5)], axis=1
        )
        grad_act = None
        for tap in range(5):
            term = lax.dot_general(
                stacked[:, tap * chans : (tap + 1) * chans],
                wt_ref[tap * chans : (tap + 1) * chans, :],
                (((1,), (1,)), ((), ())),
                preferred_element_type=jnp.float32,
            )
            grad_act = term if grad_act is None else grad_act + term
        flat_act = act_ref[pl.ds(first, FB)].reshape(rows, chans)
        part = lax.dot_general(
            flat_act, stacked, (((0,), (0,)), ((), ())), preferred_element_type=jnp.float32
        )
        for tap in range(5):
            tg_ref[tap] += part[:, tap * chans : (tap + 1) * chans]
        if with_pre:
            pre = pre_ref[pl.ds(first, FB)].reshape(rows, chans)
            sigma = 1.0 / (1.0 + jnp.exp(-pre))
            grad_act = grad_act * (sigma * (1.0 + pre * (1.0 - sigma)))
        out_ref[pl.ds(first, FB)] = grad_act.astype(jnp.bfloat16).reshape(FB, width, chans)
        return carry

    lax.fori_loop(0, frames // FB, body, 0)


def temporal_backward_k(acts, grads, kernel, step_size, pre_below):
    frames, width, chans = acts.shape
    full = pl.BlockSpec(acts.shape, lambda i, d: (0, 0, 0))
    with_pre = pre_below is not None
    in_specs = [full, full, pl.BlockSpec((5 * chans, chans), lambda i, d: (0, 0))]
    operands = [step_size.reshape(1), acts, grads, kernel.reshape(5 * chans, chans)]
    if with_pre:
        in_specs.append(full)
        operands.append(pre_below)
    out, tg = pl.pallas_call(
        functools.partial(tbwd_kernel, with_pre),
        grid_spec=pltpu.PrefetchScalarGridSpec(
            num_scalar_prefetch=1,
            grid=(1,),
            in_specs=in_specs,
            out_specs=[full, pl.BlockSpec((5, chans, chans), lambda i, d: (0, 0, 0))],
            scratch_shapes=[pltpu.VMEM((frames + 2 * HALO, width, chans), jnp.bfloat16)],
        ),
        out_shape=[
            jax.ShapeDtypeStruct(acts.shape, jnp.bfloat16),
            jax.ShapeDtypeStruct((5, chans, chans), jnp.float32),
        ],
        cost_estimate=pl.CostEstimate(
            flops=2 * frames * width * chans * chans * 10,
            transcendentals=frames * width * chans,
            bytes_accessed=frames * width * chans * 10,
        ),
    )(*operands)
    return out, tg


def all_sum(parts, scale):
    chans = parts[0].shape[-1]
    count = lax.axis_size(("seg", "grp"))
    rows = [p.reshape(-1, chans) for p in parts]
    used = sum(r.shape[0] for r in rows)
    per = -(-used // (count * 8)) * 8
    rows.append(jnp.zeros((per * count - used, chans), jnp.float32))
    stack = jnp.concatenate(rows, axis=0).reshape(count, per, chans)
    pieces = lax.all_to_all(stack, ("seg", "grp"), split_axis=0, concat_axis=0, tiled=True)
    mine = (jnp.sum(pieces, axis=0, keepdims=True) * scale).astype(jnp.bfloat16)
    spread = jnp.broadcast_to(mine, stack.shape)
    whole = lax.all_to_all(spread, ("seg", "grp"), split_axis=0, concat_axis=0, tiled=True)
    whole = whole.astype(jnp.float32).reshape(-1, chans)
    out = []
    offset = 0
    for p in parts:
        size = p.size // chans
        out.append(whole[offset : offset + size].reshape(p.shape))
        offset += size
    return out


def local(
    frames_in, spatial_weight, temporal_weight, uniting_weight, key_index, dilation, cotangent
):
    local_frames, rows, cols, chans = frames_in.shape
    pixels = rows * cols
    seg_count = lax.axis_size("seg")
    count = lax.axis_size(("seg", "grp"))
    used = pixels // count
    pre_spatial = spatial_forward(frames_in, spatial_weight)
    act_zero = jax.nn.silu(pre_spatial).astype(jnp.bfloat16).reshape(local_frames, pixels, chans)
    cot_local = cotangent.reshape(local_frames, pixels, chans)
    act_blocks = fm_to_pixels(act_zero)
    act_blocks, cot_local = lax.optimization_barrier((act_blocks, cot_local))
    cot_blocks = fm_to_pixels(cot_local)
    acts = [act_blocks]
    total_frames, width = act_blocks.shape[0], act_blocks.shape[1]
    seg_frames = total_frames // seg_count
    pres = []
    for layer in range(LAYERS):
        pre, act = temporal_forward_k(acts[-1], temporal_weight[layer], dilation[layer])
        pres.append(pre)
        acts.append(act)
    feat = acts[-1]
    seg_shape = (seg_count, seg_frames, width, chans)
    feat_seg = feat.reshape(seg_shape)
    positions = jnp.arange(seg_frames, dtype=jnp.int32)
    onehot = positions[None, :] == key_index[:, None]
    keys = jnp.einsum(
        "ns,nsjc->njc", onehot.astype(jnp.bfloat16), feat_seg, preferred_element_type=jnp.float32
    ).astype(jnp.bfloat16)
    key_full = jnp.broadcast_to(keys[:, None], seg_shape).reshape(-1, chans)
    feat_flat = feat.reshape(-1, chans)
    key_part = jnp.dot(
        keys.reshape(-1, chans), uniting_weight[1], preferred_element_type=jnp.float32
    ).reshape(seg_count, 1, width, chans)
    main_part = jnp.dot(feat_flat, uniting_weight[0], preferred_element_type=jnp.float32)
    united_blocks = (main_part.reshape(seg_shape) + key_part).astype(jnp.bfloat16)
    united = fm_to_frames(united_blocks.reshape(total_frames, width, chans), used)
    cot_flat = cot_blocks.reshape(-1, chans)
    grad_feat = jnp.dot(cot_flat, uniting_weight[0].T, preferred_element_type=jnp.float32)
    seg_cot = jnp.sum(cot_blocks.reshape(seg_shape).astype(jnp.float32), axis=1)
    key_term = jnp.dot(
        seg_cot.reshape(-1, chans),
        uniting_weight[1].T.astype(jnp.float32),
        precision=lax.Precision.HIGHEST,
    ).reshape(seg_count, 1, width, chans)
    placed = onehot.astype(jnp.float32)[:, :, None, None] * key_term
    grad_feat = grad_feat.reshape(seg_shape) + placed
    grad_feat = grad_feat.reshape(total_frames, width, chans)
    grad_uniting = jnp.stack([inner(feat_flat, cot_flat), inner(key_full, cot_flat)])
    grad_pre = (grad_feat * silu_grad(pres[-1])).astype(jnp.bfloat16)
    tgrads = [None] * LAYERS
    for layer in range(LAYERS - 1, -1, -1):
        below = pres[layer - 1] if layer > 0 else None
        grad_pre, tgrads[layer] = temporal_backward_k(
            acts[layer], grad_pre, temporal_weight[layer], dilation[layer], below
        )
    grad_act0 = grad_pre
    grad_time = fm_to_frames(grad_act0, used).reshape(frames_in.shape)
    grad_spre = (grad_time.astype(jnp.float32) * silu_grad(pre_spatial)).astype(jnp.bfloat16)
    grad_frames = spatial_back(grad_spre, spatial_weight).astype(jnp.bfloat16)
    grad_spatial = spatial_wgrad(frames_in, grad_spre)
    scale = 1.0 / jnp.sqrt(jnp.float32(total_frames * pixels))
    summed = all_sum((grad_spatial, jnp.stack(tgrads), grad_uniting), scale)
    return (
        united.reshape(frames_in.shape),
        grad_frames,
        summed[0],
        summed[1],
        summed[2],
    )


def solution(mesh):
    placed = (
        P(("seg", "grp"), None, None, None),
        P(),
        P(),
        P(),
        P(),
        P(),
        P(("seg", "grp"), None, None, None),
    )
    return jax.shard_map(
        local,
        mesh=mesh,
        in_specs=placed,
        out_specs=(
            P(("seg", "grp"), None, None, None),
            P(("seg", "grp"), None, None, None),
            P(),
            P(),
            P(),
        ),
        check_vma=False,
    )
```

```python
import functools

import jax
import jax.numpy as jnp
from jax import lax
from jax.sharding import PartitionSpec as P
from jax.experimental import pallas as pl
from jax.experimental.pallas import tpu as pltpu

LAYERS = 2
DMAX = 8


def from_root(value, axis, root):
    mine = lax.axis_index(axis) == root
    return lax.psum(jnp.where(mine, value, jnp.zeros_like(value)), axis)


def silu_grad(value):
    sigma = jax.nn.sigmoid(value)
    return sigma * (1.0 + value * (1.0 - sigma))


def inner(left, right):
    return lax.dot_general(
        left, right, (((0,), (0,)), ((), ())), preferred_element_type=jnp.float32
    )


def spatial_forward(frames, kernel):
    count, rows, cols, chans = frames.shape
    padded = jnp.pad(frames, ((0, 0), (1, 1), (1, 1), (0, 0)))
    total = jnp.zeros((count * rows * cols, chans), jnp.float32)
    for row_tap in range(3):
        for col_tap in range(3):
            piece = padded[:, row_tap : row_tap + rows, col_tap : col_tap + cols, :].reshape(
                -1, chans
            )
            total = total + jnp.dot(
                piece, kernel[3 * row_tap + col_tap], preferred_element_type=jnp.float32
            )
    return total.reshape(frames.shape)


def spatial_back(grads, kernel):
    count, rows, cols, chans = grads.shape
    padded = jnp.pad(grads, ((0, 0), (1, 1), (1, 1), (0, 0)))
    total = jnp.zeros((count * rows * cols, chans), jnp.float32)
    for row_tap in range(3):
        for col_tap in range(3):
            piece = padded[
                :, 2 - row_tap : 2 - row_tap + rows, 2 - col_tap : 2 - col_tap + cols, :
            ].reshape(-1, chans)
            total = total + jnp.dot(
                piece, kernel[3 * row_tap + col_tap].T, preferred_element_type=jnp.float32
            )
    return total.reshape(grads.shape)


def spatial_wgrad(frames, grads):
    count, rows, cols, chans = frames.shape
    padded = jnp.pad(frames, ((0, 0), (1, 1), (1, 1), (0, 0)))
    flat_grads = grads.reshape(-1, chans)
    result = []
    for row_tap in range(3):
        for col_tap in range(3):
            piece = padded[:, row_tap : row_tap + rows, col_tap : col_tap + cols, :].reshape(
                -1, chans
            )
            result.append(inner(piece, flat_grads))
    return jnp.stack(result)


def shifted(values, offset):
    padded = jnp.pad(values, ((2 * DMAX, 2 * DMAX), (0, 0), (0, 0)))
    start = 2 * DMAX + offset
    return lax.dynamic_slice_in_dim(padded, start, values.shape[0], 0)


def temporal_forward(acts, kernel, step_size):
    chans = acts.shape[2]
    total = jnp.zeros((acts.shape[0] * acts.shape[1], chans), jnp.float32)
    for tap in range(5):
        piece = shifted(acts, (tap - 2) * step_size).reshape(-1, chans)
        total = total + jnp.dot(piece, kernel[tap], preferred_element_type=jnp.float32)
    return total.reshape(acts.shape)


def temporal_back(grads, kernel, step_size):
    chans = grads.shape[2]
    total = jnp.zeros((grads.shape[0] * grads.shape[1], chans), jnp.float32)
    for tap in range(5):
        piece = shifted(grads, (2 - tap) * step_size).reshape(-1, chans)
        total = total + jnp.dot(piece, kernel[tap].T, preferred_element_type=jnp.float32)
    return total.reshape(grads.shape)


def temporal_wgrad(acts, grads, step_size):
    chans = acts.shape[2]
    flat_grads = grads.reshape(-1, chans)
    return jnp.stack(
        [
            inner(shifted(acts, (tap - 2) * step_size).reshape(-1, chans), flat_grads)
            for tap in range(5)
        ]
    )


def to_pixels(flat):
    count = lax.axis_size(("seg", "grp"))
    chans = flat.shape[-1]
    strided = flat.reshape(-1, count, chans)
    return lax.all_to_all(strided, ("seg", "grp"), split_axis=1, concat_axis=1, tiled=True)


def to_frames(blocks):
    out = lax.all_to_all(blocks, ("seg", "grp"), split_axis=1, concat_axis=1, tiled=True)
    return out.reshape(1, -1, blocks.shape[-1])


def shifted1(values, offset):
    padded = jnp.pad(values, ((0, 0), (2 * DMAX, 2 * DMAX), (0, 0)))
    start = 2 * DMAX + offset
    return lax.dynamic_slice_in_dim(padded, start, values.shape[1], 1)


def temporal_forward1(acts, kernel, step_size):
    chans = acts.shape[2]
    total = jnp.zeros((acts.shape[0] * acts.shape[1], chans), jnp.float32)
    for tap in range(5):
        piece = shifted1(acts, (tap - 2) * step_size).reshape(-1, chans)
        total = total + jnp.dot(piece, kernel[tap], preferred_element_type=jnp.float32)
    return total.reshape(acts.shape)


def temporal_back1(grads, kernel, step_size):
    chans = grads.shape[2]
    total = jnp.zeros((grads.shape[0] * grads.shape[1], chans), jnp.float32)
    for tap in range(5):
        piece = shifted1(grads, (2 - tap) * step_size).reshape(-1, chans)
        total = total + jnp.dot(piece, kernel[tap].T, preferred_element_type=jnp.float32)
    return total.reshape(grads.shape)


def temporal_wgrad1(acts, grads, step_size):
    chans = acts.shape[2]
    flat_grads = grads.reshape(-1, chans)
    return jnp.stack(
        [
            inner(shifted1(acts, (tap - 2) * step_size).reshape(-1, chans), flat_grads)
            for tap in range(5)
        ]
    )


HALO = 2 * DMAX
FB = 16


def fm_to_pixels(flat):
    count = lax.axis_size(("seg", "grp"))
    chans = flat.shape[-1]
    strided = flat.reshape(-1, count, chans)
    rows = -(-strided.shape[0] // 16) * 16
    strided = jnp.pad(strided, ((0, rows - strided.shape[0]), (0, 0), (0, 0)))
    out = lax.all_to_all(strided, ("seg", "grp"), split_axis=1, concat_axis=1, tiled=True)
    return jnp.transpose(out, (1, 0, 2))


def fm_to_frames(blocks, used):
    moved = jnp.transpose(blocks, (1, 0, 2))
    out = lax.all_to_all(moved, ("seg", "grp"), split_axis=1, concat_axis=1, tiled=True)
    return out[:used].reshape(1, -1, blocks.shape[-1])


def fill_halo(src_ref, pad_ref):
    frames = src_ref.shape[0]
    zeros = jnp.zeros((HALO,) + pad_ref.shape[1:], pad_ref.dtype)
    pad_ref[0:HALO] = zeros
    pad_ref[HALO + frames : 2 * HALO + frames] = zeros
    pad_ref[HALO : HALO + frames] = src_ref[...]


def tap_rows(pad_ref, start, rows):
    return pad_ref[pl.ds(start, FB)].reshape(rows, pad_ref.shape[-1])


def tfwd_kernel(dil_ref, act_ref, w_ref, pre_ref, out_ref, pad_ref):
    frames, width, chans = act_ref.shape
    fill_halo(act_ref, pad_ref)
    step = dil_ref[0]
    rows = FB * width
    for block in range(frames // FB):
        base = HALO + block * FB
        stacked = jnp.concatenate(
            [tap_rows(pad_ref, base + (tap - 2) * step, rows) for tap in range(5)], axis=1
        )
        pre = jnp.dot(stacked, w_ref[...], preferred_element_type=jnp.float32)
        pre_ref[block * FB : (block + 1) * FB] = pre.reshape(FB, width, chans)
        out_ref[block * FB : (block + 1) * FB] = (
            (pre / (1.0 + jnp.exp(-pre))).astype(jnp.bfloat16).reshape(FB, width, chans)
        )


def temporal_forward_k(acts, kernel, step_size):
    frames, width, chans = acts.shape
    return pl.pallas_call(
        tfwd_kernel,
        grid_spec=pltpu.PrefetchScalarGridSpec(
            num_scalar_prefetch=1,
            grid=(1,),
            in_specs=[
                pl.BlockSpec(acts.shape, lambda i, d: (0, 0, 0)),
                pl.BlockSpec((5 * chans, chans), lambda i, d: (0, 0)),
            ],
            out_specs=[
                pl.BlockSpec(acts.shape, lambda i, d: (0, 0, 0)),
                pl.BlockSpec(acts.shape, lambda i, d: (0, 0, 0)),
            ],
            scratch_shapes=[pltpu.VMEM((frames + 2 * HALO, width, chans), jnp.bfloat16)],
        ),
        out_shape=[
            jax.ShapeDtypeStruct(acts.shape, jnp.float32),
            jax.ShapeDtypeStruct(acts.shape, jnp.bfloat16),
        ],
        cost_estimate=pl.CostEstimate(
            flops=2 * frames * width * chans * chans * 5,
            transcendentals=frames * width * chans,
            bytes_accessed=frames * width * chans * 8,
        ),
    )(step_size.reshape(1), acts, kernel.reshape(5 * chans, chans))


def tbwd_kernel(with_pre, dil_ref, act_ref, grad_ref, wt_ref, *rest):
    if with_pre:
        pre_ref, out_ref, pad_ref = rest
    else:
        out_ref, pad_ref = rest
    frames, width, chans = act_ref.shape
    fill_halo(grad_ref, pad_ref)
    step = dil_ref[0]
    rows = FB * width
    for block in range(frames // FB):
        base = HALO + block * FB
        stacked = jnp.concatenate(
            [tap_rows(pad_ref, base - (tap - 2) * step, rows) for tap in range(5)], axis=1
        )
        grad_act = None
        for tap in range(5):
            term = lax.dot_general(
                stacked[:, tap * chans : (tap + 1) * chans],
                wt_ref[tap * chans : (tap + 1) * chans, :],
                (((1,), (1,)), ((), ())),
                preferred_element_type=jnp.float32,
            )
            grad_act = term if grad_act is None else grad_act + term
        if with_pre:
            pre = pre_ref[block * FB : (block + 1) * FB].reshape(rows, chans)
            sigma = 1.0 / (1.0 + jnp.exp(-pre))
            grad_act = grad_act * (sigma * (1.0 + pre * (1.0 - sigma)))
        out_ref[block * FB : (block + 1) * FB] = (
            grad_act.astype(jnp.bfloat16).reshape(FB, width, chans)
        )


def twgrad_kernel(dil_ref, act_ref, grad_ref, tg_ref, pad_ref):
    frames, width, chans = act_ref.shape
    fill_halo(grad_ref, pad_ref)
    step = dil_ref[0]
    rows = FB * width
    total = None
    for block in range(frames // FB):
        base = HALO + block * FB
        stacked = jnp.concatenate(
            [tap_rows(pad_ref, base - (tap - 2) * step, rows) for tap in range(5)], axis=1
        )
        flat_act = act_ref[block * FB : (block + 1) * FB].reshape(rows, chans)
        part = lax.dot_general(
            flat_act, stacked, (((0,), (0,)), ((), ())), preferred_element_type=jnp.float32
        )
        total = part if total is None else total + part
    for tap in range(5):
        tg_ref[tap] = total[:, tap * chans : (tap + 1) * chans]


def temporal_wgrad_k(acts, grads, step_size):
    frames, width, chans = acts.shape
    full = pl.BlockSpec(acts.shape, lambda i, d: (0, 0, 0))
    return pl.pallas_call(
        twgrad_kernel,
        grid_spec=pltpu.PrefetchScalarGridSpec(
            num_scalar_prefetch=1,
            grid=(1,),
            in_specs=[full, full],
            out_specs=pl.BlockSpec((5, chans, chans), lambda i, d: (0, 0, 0)),
            scratch_shapes=[pltpu.VMEM((frames + 2 * HALO, width, chans), jnp.bfloat16)],
        ),
        out_shape=jax.ShapeDtypeStruct((5, chans, chans), jnp.float32),
        cost_estimate=pl.CostEstimate(
            flops=2 * frames * width * chans * chans * 5,
            transcendentals=0,
            bytes_accessed=frames * width * chans * 4,
        ),
    )(step_size.reshape(1), acts, grads)


def temporal_backward_k(acts, grads, kernel, step_size, pre_below):
    frames, width, chans = acts.shape
    full = pl.BlockSpec(acts.shape, lambda i, d: (0, 0, 0))
    with_pre = pre_below is not None
    in_specs = [full, full, pl.BlockSpec((5 * chans, chans), lambda i, d: (0, 0))]
    operands = [step_size.reshape(1), acts, grads, kernel.reshape(5 * chans, chans)]
    if with_pre:
        in_specs.append(full)
        operands.append(pre_below)
    return pl.pallas_call(
        functools.partial(tbwd_kernel, with_pre),
        grid_spec=pltpu.PrefetchScalarGridSpec(
            num_scalar_prefetch=1,
            grid=(1,),
            in_specs=in_specs,
            out_specs=full,
            scratch_shapes=[pltpu.VMEM((frames + 2 * HALO, width, chans), jnp.bfloat16)],
        ),
        out_shape=jax.ShapeDtypeStruct(acts.shape, jnp.bfloat16),
        cost_estimate=pl.CostEstimate(
            flops=2 * frames * width * chans * chans * 5,
            transcendentals=frames * width * chans,
            bytes_accessed=frames * width * chans * 10,
        ),
    )(*operands)


def all_sum(parts, scale):
    chans = parts[0].shape[-1]
    count = lax.axis_size(("seg", "grp"))
    rows = [p.reshape(-1, chans) for p in parts]
    used = sum(r.shape[0] for r in rows)
    per = -(-used // (count * 8)) * 8
    rows.append(jnp.zeros((per * count - used, chans), jnp.float32))
    stack = jnp.concatenate(rows, axis=0).reshape(count, per, chans)
    pieces = lax.all_to_all(stack, ("seg", "grp"), split_axis=0, concat_axis=0, tiled=True)
    mine = (jnp.sum(pieces, axis=0, keepdims=True) * scale).astype(jnp.bfloat16)
    spread = jnp.broadcast_to(mine, stack.shape)
    whole = lax.all_to_all(spread, ("seg", "grp"), split_axis=0, concat_axis=0, tiled=True)
    whole = whole.astype(jnp.float32).reshape(-1, chans)
    out = []
    offset = 0
    for p in parts:
        size = p.size // chans
        out.append(whole[offset : offset + size].reshape(p.shape))
        offset += size
    return out


def local(
    frames_in, spatial_weight, temporal_weight, uniting_weight, key_index, dilation, cotangent
):
    local_frames, rows, cols, chans = frames_in.shape
    pixels = rows * cols
    seg_count = lax.axis_size("seg")
    count = lax.axis_size(("seg", "grp"))
    used = pixels // count
    pre_spatial = spatial_forward(frames_in, spatial_weight)
    act_zero = jax.nn.silu(pre_spatial).astype(jnp.bfloat16).reshape(local_frames, pixels, chans)
    cot_local = cotangent.reshape(local_frames, pixels, chans)
    act_blocks = fm_to_pixels(act_zero)
    act_blocks, cot_local = lax.optimization_barrier((act_blocks, cot_local))
    cot_blocks = fm_to_pixels(cot_local)
    acts = [act_blocks]
    total_frames, width = act_blocks.shape[0], act_blocks.shape[1]
    seg_frames = total_frames // seg_count
    pres = []
    for layer in range(LAYERS):
        pre, act = temporal_forward_k(acts[-1], temporal_weight[layer], dilation[layer])
        pres.append(pre)
        acts.append(act)
    feat = acts[-1]
    seg_shape = (seg_count, seg_frames, width, chans)
    feat_seg = feat.reshape(seg_shape)
    positions = jnp.arange(seg_frames, dtype=jnp.int32)
    onehot = positions[None, :] == key_index[:, None]
    keys = jnp.einsum(
        "ns,nsjc->njc", onehot.astype(jnp.bfloat16), feat_seg, preferred_element_type=jnp.float32
    ).astype(jnp.bfloat16)
    key_full = jnp.broadcast_to(keys[:, None], seg_shape).reshape(-1, chans)
    feat_flat = feat.reshape(-1, chans)
    key_part = jnp.dot(
        keys.reshape(-1, chans), uniting_weight[1], preferred_element_type=jnp.float32
    ).reshape(seg_count, 1, width, chans)
    main_part = jnp.dot(feat_flat, uniting_weight[0], preferred_element_type=jnp.float32)
    united_blocks = (main_part.reshape(seg_shape) + key_part).astype(jnp.bfloat16)
    united = fm_to_frames(united_blocks.reshape(total_frames, width, chans), used)
    cot_flat = cot_blocks.reshape(-1, chans)
    grad_feat = jnp.dot(cot_flat, uniting_weight[0].T, preferred_element_type=jnp.float32)
    seg_cot = jnp.sum(cot_blocks.reshape(seg_shape).astype(jnp.float32), axis=1)
    key_term = jnp.dot(
        seg_cot.reshape(-1, chans),
        uniting_weight[1].T.astype(jnp.float32),
        precision=lax.Precision.HIGHEST,
    ).reshape(seg_count, 1, width, chans)
    placed = onehot.astype(jnp.float32)[:, :, None, None] * key_term
    grad_feat = grad_feat.reshape(seg_shape) + placed
    grad_feat = grad_feat.reshape(total_frames, width, chans)
    grad_uniting = jnp.stack([inner(feat_flat, cot_flat), inner(key_full, cot_flat)])
    grad_pre = (grad_feat * silu_grad(pres[-1])).astype(jnp.bfloat16)
    tgrads = [None] * LAYERS
    layer_grads = [None] * LAYERS
    for layer in range(LAYERS - 1, -1, -1):
        below = pres[layer - 1] if layer > 0 else None
        layer_grads[layer] = grad_pre
        grad_pre = temporal_backward_k(
            acts[layer], grad_pre, temporal_weight[layer], dilation[layer], below
        )
    grad_act0 = grad_pre
    grad_time = fm_to_frames(grad_act0, used).reshape(frames_in.shape)
    for layer in range(LAYERS):
        tgrads[layer] = temporal_wgrad_k(acts[layer], layer_grads[layer], dilation[layer])
    grad_spre = (grad_time.astype(jnp.float32) * silu_grad(pre_spatial)).astype(jnp.bfloat16)
    grad_frames = spatial_back(grad_spre, spatial_weight).astype(jnp.bfloat16)
    grad_spatial = spatial_wgrad(frames_in, grad_spre)
    scale = 1.0 / jnp.sqrt(jnp.float32(total_frames * pixels))
    summed = all_sum((grad_spatial, jnp.stack(tgrads), grad_uniting), scale)
    return (
        united.reshape(frames_in.shape),
        grad_frames,
        summed[0],
        summed[1],
        summed[2],
    )


def solution(mesh):
    placed = (
        P(("seg", "grp"), None, None, None),
        P(),
        P(),
        P(),
        P(),
        P(),
        P(("seg", "grp"), None, None, None),
    )
    return jax.shard_map(
        local,
        mesh=mesh,
        in_specs=placed,
        out_specs=(
            P(("seg", "grp"), None, None, None),
            P(("seg", "grp"), None, None, None),
            P(),
            P(),
            P(),
        ),
        check_vma=False,
    )
```

```python
import functools

import jax
import jax.numpy as jnp
from jax import lax
from jax.sharding import PartitionSpec as P
from jax.experimental import pallas as pl
from jax.experimental.pallas import tpu as pltpu

LAYERS = 2
DMAX = 8


def from_root(value, axis, root):
    mine = lax.axis_index(axis) == root
    return lax.psum(jnp.where(mine, value, jnp.zeros_like(value)), axis)


def silu_grad(value):
    sigma = jax.nn.sigmoid(value)
    return sigma * (1.0 + value * (1.0 - sigma))


def inner(left, right):
    return lax.dot_general(
        left, right, (((0,), (0,)), ((), ())), preferred_element_type=jnp.float32
    )


def spatial_forward(frames, kernel):
    count, rows, cols, chans = frames.shape
    padded = jnp.pad(frames, ((0, 0), (1, 1), (1, 1), (0, 0)))
    total = jnp.zeros((count * rows * cols, chans), jnp.float32)
    for row_tap in range(3):
        for col_tap in range(3):
            piece = padded[:, row_tap : row_tap + rows, col_tap : col_tap + cols, :].reshape(
                -1, chans
            )
            total = total + jnp.dot(
                piece, kernel[3 * row_tap + col_tap], preferred_element_type=jnp.float32
            )
    return total.reshape(frames.shape)


def spatial_back(grads, kernel):
    count, rows, cols, chans = grads.shape
    padded = jnp.pad(grads, ((0, 0), (1, 1), (1, 1), (0, 0)))
    total = jnp.zeros((count * rows * cols, chans), jnp.float32)
    for row_tap in range(3):
        for col_tap in range(3):
            piece = padded[
                :, 2 - row_tap : 2 - row_tap + rows, 2 - col_tap : 2 - col_tap + cols, :
            ].reshape(-1, chans)
            total = total + jnp.dot(
                piece, kernel[3 * row_tap + col_tap].T, preferred_element_type=jnp.float32
            )
    return total.reshape(grads.shape)


def spatial_wgrad(frames, grads):
    count, rows, cols, chans = frames.shape
    padded = jnp.pad(frames, ((0, 0), (1, 1), (1, 1), (0, 0)))
    flat_grads = grads.reshape(-1, chans)
    result = []
    for row_tap in range(3):
        for col_tap in range(3):
            piece = padded[:, row_tap : row_tap + rows, col_tap : col_tap + cols, :].reshape(
                -1, chans
            )
            result.append(inner(piece, flat_grads))
    return jnp.stack(result)


def shifted(values, offset):
    padded = jnp.pad(values, ((2 * DMAX, 2 * DMAX), (0, 0), (0, 0)))
    start = 2 * DMAX + offset
    return lax.dynamic_slice_in_dim(padded, start, values.shape[0], 0)


def temporal_forward(acts, kernel, step_size):
    chans = acts.shape[2]
    total = jnp.zeros((acts.shape[0] * acts.shape[1], chans), jnp.float32)
    for tap in range(5):
        piece = shifted(acts, (tap - 2) * step_size).reshape(-1, chans)
        total = total + jnp.dot(piece, kernel[tap], preferred_element_type=jnp.float32)
    return total.reshape(acts.shape)


def temporal_back(grads, kernel, step_size):
    chans = grads.shape[2]
    total = jnp.zeros((grads.shape[0] * grads.shape[1], chans), jnp.float32)
    for tap in range(5):
        piece = shifted(grads, (2 - tap) * step_size).reshape(-1, chans)
        total = total + jnp.dot(piece, kernel[tap].T, preferred_element_type=jnp.float32)
    return total.reshape(grads.shape)


def temporal_wgrad(acts, grads, step_size):
    chans = acts.shape[2]
    flat_grads = grads.reshape(-1, chans)
    return jnp.stack(
        [
            inner(shifted(acts, (tap - 2) * step_size).reshape(-1, chans), flat_grads)
            for tap in range(5)
        ]
    )


def to_pixels(flat):
    count = lax.axis_size(("seg", "grp"))
    chans = flat.shape[-1]
    strided = flat.reshape(-1, count, chans)
    return lax.all_to_all(strided, ("seg", "grp"), split_axis=1, concat_axis=1, tiled=True)


def to_frames(blocks):
    out = lax.all_to_all(blocks, ("seg", "grp"), split_axis=1, concat_axis=1, tiled=True)
    return out.reshape(1, -1, blocks.shape[-1])


def shifted1(values, offset):
    padded = jnp.pad(values, ((0, 0), (2 * DMAX, 2 * DMAX), (0, 0)))
    start = 2 * DMAX + offset
    return lax.dynamic_slice_in_dim(padded, start, values.shape[1], 1)


def temporal_forward1(acts, kernel, step_size):
    chans = acts.shape[2]
    total = jnp.zeros((acts.shape[0] * acts.shape[1], chans), jnp.float32)
    for tap in range(5):
        piece = shifted1(acts, (tap - 2) * step_size).reshape(-1, chans)
        total = total + jnp.dot(piece, kernel[tap], preferred_element_type=jnp.float32)
    return total.reshape(acts.shape)


def temporal_back1(grads, kernel, step_size):
    chans = grads.shape[2]
    total = jnp.zeros((grads.shape[0] * grads.shape[1], chans), jnp.float32)
    for tap in range(5):
        piece = shifted1(grads, (2 - tap) * step_size).reshape(-1, chans)
        total = total + jnp.dot(piece, kernel[tap].T, preferred_element_type=jnp.float32)
    return total.reshape(grads.shape)


def temporal_wgrad1(acts, grads, step_size):
    chans = acts.shape[2]
    flat_grads = grads.reshape(-1, chans)
    return jnp.stack(
        [
            inner(shifted1(acts, (tap - 2) * step_size).reshape(-1, chans), flat_grads)
            for tap in range(5)
        ]
    )


HALO = 2 * DMAX
FB = 32


def fm_to_pixels(flat):
    count = lax.axis_size(("seg", "grp"))
    chans = flat.shape[-1]
    strided = flat.reshape(-1, count, chans)
    rows = -(-strided.shape[0] // 16) * 16
    strided = jnp.pad(strided, ((0, rows - strided.shape[0]), (0, 0), (0, 0)))
    out = lax.all_to_all(strided, ("seg", "grp"), split_axis=1, concat_axis=1, tiled=True)
    return jnp.transpose(out, (1, 0, 2))


def fm_to_frames(blocks, used):
    moved = jnp.transpose(blocks, (1, 0, 2))
    out = lax.all_to_all(moved, ("seg", "grp"), split_axis=1, concat_axis=1, tiled=True)
    return out[:used].reshape(1, -1, blocks.shape[-1])


def fill_halo(src_ref, pad_ref):
    frames = src_ref.shape[0]
    zeros = jnp.zeros((HALO,) + pad_ref.shape[1:], pad_ref.dtype)
    pad_ref[0:HALO] = zeros
    pad_ref[HALO + frames : 2 * HALO + frames] = zeros
    pad_ref[HALO : HALO + frames] = src_ref[...]


def tap_rows(pad_ref, start, rows):
    return pad_ref[pl.ds(start, FB)].reshape(rows, pad_ref.shape[-1])


def tfwd_kernel(dil_ref, act_ref, w_ref, pre_ref, out_ref, pad_ref):
    frames, width, chans = act_ref.shape
    fill_halo(act_ref, pad_ref)
    step = dil_ref[0]
    rows = FB * width
    for block in range(frames // FB):
        base = HALO + block * FB
        stacked = jnp.concatenate(
            [tap_rows(pad_ref, base + (tap - 2) * step, rows) for tap in range(5)], axis=1
        )
        pre = jnp.dot(stacked, w_ref[...], preferred_element_type=jnp.float32)
        pre_ref[block * FB : (block + 1) * FB] = pre.reshape(FB, width, chans)
        out_ref[block * FB : (block + 1) * FB] = (
            (pre / (1.0 + jnp.exp(-pre))).astype(jnp.bfloat16).reshape(FB, width, chans)
        )


def temporal_forward_k(acts, kernel, step_size):
    frames, width, chans = acts.shape
    return pl.pallas_call(
        tfwd_kernel,
        grid_spec=pltpu.PrefetchScalarGridSpec(
            num_scalar_prefetch=1,
            grid=(1,),
            in_specs=[
                pl.BlockSpec(acts.shape, lambda i, d: (0, 0, 0)),
                pl.BlockSpec((5 * chans, chans), lambda i, d: (0, 0)),
            ],
            out_specs=[
                pl.BlockSpec(acts.shape, lambda i, d: (0, 0, 0)),
                pl.BlockSpec(acts.shape, lambda i, d: (0, 0, 0)),
            ],
            scratch_shapes=[pltpu.VMEM((frames + 2 * HALO, width, chans), jnp.bfloat16)],
        ),
        out_shape=[
            jax.ShapeDtypeStruct(acts.shape, jnp.float32),
            jax.ShapeDtypeStruct(acts.shape, jnp.bfloat16),
        ],
        cost_estimate=pl.CostEstimate(
            flops=2 * frames * width * chans * chans * 5,
            transcendentals=frames * width * chans,
            bytes_accessed=frames * width * chans * 8,
        ),
    )(step_size.reshape(1), acts, kernel.reshape(5 * chans, chans))


def tbwd_kernel(with_pre, dil_ref, act_ref, grad_ref, wt_ref, *rest):
    if with_pre:
        pre_ref, out_ref, pad_ref = rest
    else:
        out_ref, pad_ref = rest
    frames, width, chans = act_ref.shape
    fill_halo(grad_ref, pad_ref)
    step = dil_ref[0]
    rows = FB * width
    for block in range(frames // FB):
        base = HALO + block * FB
        stacked = jnp.concatenate(
            [tap_rows(pad_ref, base - (tap - 2) * step, rows) for tap in range(5)], axis=1
        )
        grad_act = None
        for tap in range(5):
            term = lax.dot_general(
                stacked[:, tap * chans : (tap + 1) * chans],
                wt_ref[tap * chans : (tap + 1) * chans, :],
                (((1,), (1,)), ((), ())),
                preferred_element_type=jnp.float32,
            )
            grad_act = term if grad_act is None else grad_act + term
        if with_pre:
            pre = pre_ref[block * FB : (block + 1) * FB].reshape(rows, chans)
            sigma = 1.0 / (1.0 + jnp.exp(-pre))
            grad_act = grad_act * (sigma * (1.0 + pre * (1.0 - sigma)))
        out_ref[block * FB : (block + 1) * FB] = (
            grad_act.astype(jnp.bfloat16).reshape(FB, width, chans)
        )


def twgrad_kernel(dil_ref, act_ref, grad_ref, tg_ref, pad_ref):
    frames, width, chans = act_ref.shape
    fill_halo(grad_ref, pad_ref)
    step = dil_ref[0]
    rows = FB * width
    total = None
    for block in range(frames // FB):
        base = HALO + block * FB
        stacked = jnp.concatenate(
            [tap_rows(pad_ref, base - (tap - 2) * step, rows) for tap in range(5)], axis=1
        )
        flat_act = act_ref[block * FB : (block + 1) * FB].reshape(rows, chans)
        part = lax.dot_general(
            flat_act, stacked, (((0,), (0,)), ((), ())), preferred_element_type=jnp.float32
        )
        total = part if total is None else total + part
    for tap in range(5):
        tg_ref[tap] = total[:, tap * chans : (tap + 1) * chans]


def temporal_wgrad_k(acts, grads, step_size):
    frames, width, chans = acts.shape
    full = pl.BlockSpec(acts.shape, lambda i, d: (0, 0, 0))
    return pl.pallas_call(
        twgrad_kernel,
        grid_spec=pltpu.PrefetchScalarGridSpec(
            num_scalar_prefetch=1,
            grid=(1,),
            in_specs=[full, full],
            out_specs=pl.BlockSpec((5, chans, chans), lambda i, d: (0, 0, 0)),
            scratch_shapes=[pltpu.VMEM((frames + 2 * HALO, width, chans), jnp.bfloat16)],
        ),
        out_shape=jax.ShapeDtypeStruct((5, chans, chans), jnp.float32),
        cost_estimate=pl.CostEstimate(
            flops=2 * frames * width * chans * chans * 5,
            transcendentals=0,
            bytes_accessed=frames * width * chans * 4,
        ),
    )(step_size.reshape(1), acts, grads)


def temporal_backward_k(acts, grads, kernel, step_size, pre_below):
    frames, width, chans = acts.shape
    full = pl.BlockSpec(acts.shape, lambda i, d: (0, 0, 0))
    with_pre = pre_below is not None
    in_specs = [full, full, pl.BlockSpec((5 * chans, chans), lambda i, d: (0, 0))]
    operands = [step_size.reshape(1), acts, grads, kernel.reshape(5 * chans, chans)]
    if with_pre:
        in_specs.append(full)
        operands.append(pre_below)
    return pl.pallas_call(
        functools.partial(tbwd_kernel, with_pre),
        grid_spec=pltpu.PrefetchScalarGridSpec(
            num_scalar_prefetch=1,
            grid=(1,),
            in_specs=in_specs,
            out_specs=full,
            scratch_shapes=[pltpu.VMEM((frames + 2 * HALO, width, chans), jnp.bfloat16)],
        ),
        out_shape=jax.ShapeDtypeStruct(acts.shape, jnp.bfloat16),
        cost_estimate=pl.CostEstimate(
            flops=2 * frames * width * chans * chans * 5,
            transcendentals=frames * width * chans,
            bytes_accessed=frames * width * chans * 10,
        ),
    )(*operands)


def all_sum(parts, scale):
    chans = parts[0].shape[-1]
    count = lax.axis_size(("seg", "grp"))
    rows = [p.reshape(-1, chans) for p in parts]
    used = sum(r.shape[0] for r in rows)
    per = -(-used // (count * 8)) * 8
    rows.append(jnp.zeros((per * count - used, chans), jnp.float32))
    stack = jnp.concatenate(rows, axis=0).reshape(count, per, chans)
    pieces = lax.all_to_all(stack, ("seg", "grp"), split_axis=0, concat_axis=0, tiled=True)
    mine = (jnp.sum(pieces, axis=0, keepdims=True) * scale).astype(jnp.bfloat16)
    spread = jnp.broadcast_to(mine, stack.shape)
    whole = lax.all_to_all(spread, ("seg", "grp"), split_axis=0, concat_axis=0, tiled=True)
    whole = whole.astype(jnp.float32).reshape(-1, chans)
    out = []
    offset = 0
    for p in parts:
        size = p.size // chans
        out.append(whole[offset : offset + size].reshape(p.shape))
        offset += size
    return out


def local(
    frames_in, spatial_weight, temporal_weight, uniting_weight, key_index, dilation, cotangent
):
    local_frames, rows, cols, chans = frames_in.shape
    pixels = rows * cols
    seg_count = lax.axis_size("seg")
    count = lax.axis_size(("seg", "grp"))
    used = pixels // count
    pre_spatial = spatial_forward(frames_in, spatial_weight)
    act_zero = jax.nn.silu(pre_spatial).astype(jnp.bfloat16).reshape(local_frames, pixels, chans)
    cot_local = cotangent.reshape(local_frames, pixels, chans)
    act_blocks = fm_to_pixels(act_zero)
    act_blocks, cot_local = lax.optimization_barrier((act_blocks, cot_local))
    cot_blocks = fm_to_pixels(cot_local)
    acts = [act_blocks]
    total_frames, width = act_blocks.shape[0], act_blocks.shape[1]
    seg_frames = total_frames // seg_count
    pres = []
    for layer in range(LAYERS):
        pre, act = temporal_forward_k(acts[-1], temporal_weight[layer], dilation[layer])
        pres.append(pre)
        acts.append(act)
    feat = acts[-1]
    seg_shape = (seg_count, seg_frames, width, chans)
    feat_seg = feat.reshape(seg_shape)
    positions = jnp.arange(seg_frames, dtype=jnp.int32)
    onehot = positions[None, :] == key_index[:, None]
    keys = jnp.einsum(
        "ns,nsjc->njc", onehot.astype(jnp.bfloat16), feat_seg, preferred_element_type=jnp.float32
    ).astype(jnp.bfloat16)
    key_full = jnp.broadcast_to(keys[:, None], seg_shape).reshape(-1, chans)
    feat_flat = feat.reshape(-1, chans)
    key_part = jnp.dot(
        keys.reshape(-1, chans), uniting_weight[1], preferred_element_type=jnp.float32
    ).reshape(seg_count, 1, width, chans)
    main_part = jnp.dot(feat_flat, uniting_weight[0], preferred_element_type=jnp.float32)
    united_blocks = (main_part.reshape(seg_shape) + key_part).astype(jnp.bfloat16)
    united = fm_to_frames(united_blocks.reshape(total_frames, width, chans), used)
    cot_flat = cot_blocks.reshape(-1, chans)
    grad_feat = jnp.dot(cot_flat, uniting_weight[0].T, preferred_element_type=jnp.float32)
    seg_cot = jnp.sum(cot_blocks.reshape(seg_shape).astype(jnp.float32), axis=1)
    key_term = jnp.dot(
        seg_cot.reshape(-1, chans),
        uniting_weight[1].T.astype(jnp.float32),
        precision=lax.Precision.HIGHEST,
    ).reshape(seg_count, 1, width, chans)
    placed = onehot.astype(jnp.float32)[:, :, None, None] * key_term
    grad_feat = grad_feat.reshape(seg_shape) + placed
    grad_feat = grad_feat.reshape(total_frames, width, chans)
    grad_uniting = jnp.stack([inner(feat_flat, cot_flat), inner(key_full, cot_flat)])
    grad_pre = (grad_feat * silu_grad(pres[-1])).astype(jnp.bfloat16)
    tgrads = [None] * LAYERS
    layer_grads = [None] * LAYERS
    for layer in range(LAYERS - 1, -1, -1):
        below = pres[layer - 1] if layer > 0 else None
        layer_grads[layer] = grad_pre
        grad_pre = temporal_backward_k(
            acts[layer], grad_pre, temporal_weight[layer], dilation[layer], below
        )
    grad_act0 = grad_pre
    grad_time = fm_to_frames(grad_act0, used).reshape(frames_in.shape)
    for layer in range(LAYERS):
        tgrads[layer] = temporal_wgrad_k(acts[layer], layer_grads[layer], dilation[layer])
    grad_spre = (grad_time.astype(jnp.float32) * silu_grad(pre_spatial)).astype(jnp.bfloat16)
    grad_frames = spatial_back(grad_spre, spatial_weight).astype(jnp.bfloat16)
    grad_spatial = spatial_wgrad(frames_in, grad_spre)
    scale = 1.0 / jnp.sqrt(jnp.float32(total_frames * pixels))
    summed = all_sum((grad_spatial, jnp.stack(tgrads), grad_uniting), scale)
    return (
        united.reshape(frames_in.shape),
        grad_frames,
        summed[0],
        summed[1],
        summed[2],
    )


def solution(mesh):
    placed = (
        P(("seg", "grp"), None, None, None),
        P(),
        P(),
        P(),
        P(),
        P(),
        P(("seg", "grp"), None, None, None),
    )
    return jax.shard_map(
        local,
        mesh=mesh,
        in_specs=placed,
        out_specs=(
            P(("seg", "grp"), None, None, None),
            P(("seg", "grp"), None, None, None),
            P(),
            P(),
            P(),
        ),
        check_vma=False,
    )
```

```python
import functools

import jax
import jax.numpy as jnp
from jax import lax
from jax.sharding import PartitionSpec as P
from jax.experimental import pallas as pl
from jax.experimental.pallas import tpu as pltpu

LAYERS = 2
DMAX = 8


def from_root(value, axis, root):
    mine = lax.axis_index(axis) == root
    return lax.psum(jnp.where(mine, value, jnp.zeros_like(value)), axis)


def silu_grad(value):
    sigma = jax.nn.sigmoid(value)
    return sigma * (1.0 + value * (1.0 - sigma))


def inner(left, right):
    return lax.dot_general(
        left, right, (((0,), (0,)), ((), ())), preferred_element_type=jnp.float32
    )


def spatial_forward(frames, kernel):
    count, rows, cols, chans = frames.shape
    padded = jnp.pad(frames, ((0, 0), (1, 1), (1, 1), (0, 0)))
    total = jnp.zeros((count * rows * cols, chans), jnp.float32)
    for row_tap in range(3):
        for col_tap in range(3):
            piece = padded[:, row_tap : row_tap + rows, col_tap : col_tap + cols, :].reshape(
                -1, chans
            )
            total = total + jnp.dot(
                piece, kernel[3 * row_tap + col_tap], preferred_element_type=jnp.float32
            )
    return total.reshape(frames.shape)


def spatial_back(grads, kernel):
    count, rows, cols, chans = grads.shape
    padded = jnp.pad(grads, ((0, 0), (1, 1), (1, 1), (0, 0)))
    total = jnp.zeros((count * rows * cols, chans), jnp.float32)
    for row_tap in range(3):
        for col_tap in range(3):
            piece = padded[
                :, 2 - row_tap : 2 - row_tap + rows, 2 - col_tap : 2 - col_tap + cols, :
            ].reshape(-1, chans)
            total = total + jnp.dot(
                piece, kernel[3 * row_tap + col_tap].T, preferred_element_type=jnp.float32
            )
    return total.reshape(grads.shape)


def spatial_wgrad(frames, grads):
    count, rows, cols, chans = frames.shape
    padded = jnp.pad(frames, ((0, 0), (1, 1), (1, 1), (0, 0)))
    flat_grads = grads.reshape(-1, chans)
    result = []
    for row_tap in range(3):
        for col_tap in range(3):
            piece = padded[:, row_tap : row_tap + rows, col_tap : col_tap + cols, :].reshape(
                -1, chans
            )
            result.append(inner(piece, flat_grads))
    return jnp.stack(result)


def shifted(values, offset):
    padded = jnp.pad(values, ((2 * DMAX, 2 * DMAX), (0, 0), (0, 0)))
    start = 2 * DMAX + offset
    return lax.dynamic_slice_in_dim(padded, start, values.shape[0], 0)


def temporal_forward(acts, kernel, step_size):
    chans = acts.shape[2]
    total = jnp.zeros((acts.shape[0] * acts.shape[1], chans), jnp.float32)
    for tap in range(5):
        piece = shifted(acts, (tap - 2) * step_size).reshape(-1, chans)
        total = total + jnp.dot(piece, kernel[tap], preferred_element_type=jnp.float32)
    return total.reshape(acts.shape)


def temporal_back(grads, kernel, step_size):
    chans = grads.shape[2]
    total = jnp.zeros((grads.shape[0] * grads.shape[1], chans), jnp.float32)
    for tap in range(5):
        piece = shifted(grads, (2 - tap) * step_size).reshape(-1, chans)
        total = total + jnp.dot(piece, kernel[tap].T, preferred_element_type=jnp.float32)
    return total.reshape(grads.shape)


def temporal_wgrad(acts, grads, step_size):
    chans = acts.shape[2]
    flat_grads = grads.reshape(-1, chans)
    return jnp.stack(
        [
            inner(shifted(acts, (tap - 2) * step_size).reshape(-1, chans), flat_grads)
            for tap in range(5)
        ]
    )


def to_pixels(flat):
    count = lax.axis_size(("seg", "grp"))
    chans = flat.shape[-1]
    strided = flat.reshape(-1, count, chans)
    return lax.all_to_all(strided, ("seg", "grp"), split_axis=1, concat_axis=1, tiled=True)


def to_frames(blocks):
    out = lax.all_to_all(blocks, ("seg", "grp"), split_axis=1, concat_axis=1, tiled=True)
    return out.reshape(1, -1, blocks.shape[-1])


def shifted1(values, offset):
    padded = jnp.pad(values, ((0, 0), (2 * DMAX, 2 * DMAX), (0, 0)))
    start = 2 * DMAX + offset
    return lax.dynamic_slice_in_dim(padded, start, values.shape[1], 1)


def temporal_forward1(acts, kernel, step_size):
    chans = acts.shape[2]
    total = jnp.zeros((acts.shape[0] * acts.shape[1], chans), jnp.float32)
    for tap in range(5):
        piece = shifted1(acts, (tap - 2) * step_size).reshape(-1, chans)
        total = total + jnp.dot(piece, kernel[tap], preferred_element_type=jnp.float32)
    return total.reshape(acts.shape)


def temporal_back1(grads, kernel, step_size):
    chans = grads.shape[2]
    total = jnp.zeros((grads.shape[0] * grads.shape[1], chans), jnp.float32)
    for tap in range(5):
        piece = shifted1(grads, (2 - tap) * step_size).reshape(-1, chans)
        total = total + jnp.dot(piece, kernel[tap].T, preferred_element_type=jnp.float32)
    return total.reshape(grads.shape)


def temporal_wgrad1(acts, grads, step_size):
    chans = acts.shape[2]
    flat_grads = grads.reshape(-1, chans)
    return jnp.stack(
        [
            inner(shifted1(acts, (tap - 2) * step_size).reshape(-1, chans), flat_grads)
            for tap in range(5)
        ]
    )


HALO = 2 * DMAX
FB = 32


def fm_to_pixels(flat):
    count = lax.axis_size(("seg", "grp"))
    chans = flat.shape[-1]
    strided = flat.reshape(-1, count, chans)
    rows = -(-strided.shape[0] // 16) * 16
    strided = jnp.pad(strided, ((0, rows - strided.shape[0]), (0, 0), (0, 0)))
    out = lax.all_to_all(strided, ("seg", "grp"), split_axis=1, concat_axis=1, tiled=True)
    return jnp.transpose(out, (1, 0, 2))


def fm_to_frames(blocks, used):
    moved = jnp.transpose(blocks, (1, 0, 2))
    out = lax.all_to_all(moved, ("seg", "grp"), split_axis=1, concat_axis=1, tiled=True)
    return out[:used].reshape(1, -1, blocks.shape[-1])


def fill_halo(src_ref, pad_ref):
    frames = src_ref.shape[0]
    zeros = jnp.zeros((HALO,) + pad_ref.shape[1:], pad_ref.dtype)
    pad_ref[0:HALO] = zeros
    pad_ref[HALO + frames : 2 * HALO + frames] = zeros
    pad_ref[HALO : HALO + frames] = src_ref[...]


def tap_rows(pad_ref, start, rows):
    return pad_ref[pl.ds(start, FB)].reshape(rows, pad_ref.shape[-1])


def tfwd_kernel(dil_ref, act_ref, w_ref, pre_ref, out_ref, pad_ref):
    frames, width, chans = act_ref.shape

    @pl.when(pl.program_id(0) == 0)
    def _():
        fill_halo(act_ref, pad_ref)

    step = dil_ref[0]
    rows = FB * width
    base = HALO + pl.program_id(0) * FB
    stacked = jnp.concatenate(
        [tap_rows(pad_ref, base + (tap - 2) * step, rows) for tap in range(5)], axis=1
    )
    pre = jnp.dot(stacked, w_ref[...], preferred_element_type=jnp.float32)
    pre_ref[...] = pre.reshape(FB, width, chans)
    out_ref[...] = (pre / (1.0 + jnp.exp(-pre))).astype(jnp.bfloat16).reshape(FB, width, chans)


def temporal_forward_k(acts, kernel, step_size):
    frames, width, chans = acts.shape
    part = pl.BlockSpec((FB, width, chans), lambda i, d: (i, 0, 0))
    return pl.pallas_call(
        tfwd_kernel,
        grid_spec=pltpu.PrefetchScalarGridSpec(
            num_scalar_prefetch=1,
            grid=(frames // FB,),
            in_specs=[
                pl.BlockSpec(acts.shape, lambda i, d: (0, 0, 0)),
                pl.BlockSpec((5 * chans, chans), lambda i, d: (0, 0)),
            ],
            out_specs=[part, part],
            scratch_shapes=[pltpu.VMEM((frames + 2 * HALO, width, chans), jnp.bfloat16)],
        ),
        out_shape=[
            jax.ShapeDtypeStruct(acts.shape, jnp.float32),
            jax.ShapeDtypeStruct(acts.shape, jnp.bfloat16),
        ],
        compiler_params=pltpu.CompilerParams(dimension_semantics=("arbitrary",)),
        cost_estimate=pl.CostEstimate(
            flops=2 * frames * width * chans * chans * 5,
            transcendentals=frames * width * chans,
            bytes_accessed=frames * width * chans * 8,
        ),
    )(step_size.reshape(1), acts, kernel.reshape(5 * chans, chans))


def tbwd_kernel(with_pre, dil_ref, grad_ref, wt_ref, *rest):
    if with_pre:
        pre_ref, out_ref, pad_ref = rest
    else:
        out_ref, pad_ref = rest
    frames, width, chans = grad_ref.shape

    @pl.when(pl.program_id(0) == 0)
    def _():
        fill_halo(grad_ref, pad_ref)

    step = dil_ref[0]
    rows = FB * width
    base = HALO + pl.program_id(0) * FB
    stacked = jnp.concatenate(
        [tap_rows(pad_ref, base - (tap - 2) * step, rows) for tap in range(5)], axis=1
    )
    grad_act = None
    for tap in range(5):
        term = lax.dot_general(
            stacked[:, tap * chans : (tap + 1) * chans],
            wt_ref[tap * chans : (tap + 1) * chans, :],
            (((1,), (1,)), ((), ())),
            preferred_element_type=jnp.float32,
        )
        grad_act = term if grad_act is None else grad_act + term
    if with_pre:
        pre = pre_ref[...].reshape(rows, chans)
        sigma = 1.0 / (1.0 + jnp.exp(-pre))
        grad_act = grad_act * (sigma * (1.0 + pre * (1.0 - sigma)))
    out_ref[...] = grad_act.astype(jnp.bfloat16).reshape(FB, width, chans)


def twgrad_kernel(dil_ref, act_ref, grad_ref, tg_ref, pad_ref):
    frames, width, chans = act_ref.shape
    fill_halo(grad_ref, pad_ref)
    step = dil_ref[0]
    rows = FB * width
    total = None
    for block in range(frames // FB):
        base = HALO + block * FB
        stacked = jnp.concatenate(
            [tap_rows(pad_ref, base - (tap - 2) * step, rows) for tap in range(5)], axis=1
        )
        flat_act = act_ref[block * FB : (block + 1) * FB].reshape(rows, chans)
        part = lax.dot_general(
            flat_act, stacked, (((0,), (0,)), ((), ())), preferred_element_type=jnp.float32
        )
        total = part if total is None else total + part
    for tap in range(5):
        tg_ref[tap] = total[:, tap * chans : (tap + 1) * chans]


def temporal_wgrad_k(acts, grads, step_size):
    frames, width, chans = acts.shape
    full = pl.BlockSpec(acts.shape, lambda i, d: (0, 0, 0))
    return pl.pallas_call(
        twgrad_kernel,
        grid_spec=pltpu.PrefetchScalarGridSpec(
            num_scalar_prefetch=1,
            grid=(1,),
            in_specs=[full, full],
            out_specs=pl.BlockSpec((5, chans, chans), lambda i, d: (0, 0, 0)),
            scratch_shapes=[pltpu.VMEM((frames + 2 * HALO, width, chans), jnp.bfloat16)],
        ),
        out_shape=jax.ShapeDtypeStruct((5, chans, chans), jnp.float32),
        cost_estimate=pl.CostEstimate(
            flops=2 * frames * width * chans * chans * 5,
            transcendentals=0,
            bytes_accessed=frames * width * chans * 4,
        ),
    )(step_size.reshape(1), acts, grads)


def temporal_backward_k(acts, grads, kernel, step_size, pre_below):
    frames, width, chans = grads.shape
    part = pl.BlockSpec((FB, width, chans), lambda i, d: (i, 0, 0))
    with_pre = pre_below is not None
    in_specs = [
        pl.BlockSpec(grads.shape, lambda i, d: (0, 0, 0)),
        pl.BlockSpec((5 * chans, chans), lambda i, d: (0, 0)),
    ]
    operands = [step_size.reshape(1), grads, kernel.reshape(5 * chans, chans)]
    if with_pre:
        in_specs.append(part)
        operands.append(pre_below)
    return pl.pallas_call(
        functools.partial(tbwd_kernel, with_pre),
        grid_spec=pltpu.PrefetchScalarGridSpec(
            num_scalar_prefetch=1,
            grid=(frames // FB,),
            in_specs=in_specs,
            out_specs=part,
            scratch_shapes=[pltpu.VMEM((frames + 2 * HALO, width, chans), jnp.bfloat16)],
        ),
        out_shape=jax.ShapeDtypeStruct(grads.shape, jnp.bfloat16),
        compiler_params=pltpu.CompilerParams(dimension_semantics=("arbitrary",)),
        cost_estimate=pl.CostEstimate(
            flops=2 * frames * width * chans * chans * 5,
            transcendentals=frames * width * chans,
            bytes_accessed=frames * width * chans * 10,
        ),
    )(*operands)


def all_sum(parts, scale):
    chans = parts[0].shape[-1]
    count = lax.axis_size(("seg", "grp"))
    rows = [p.reshape(-1, chans) for p in parts]
    used = sum(r.shape[0] for r in rows)
    per = -(-used // (count * 8)) * 8
    rows.append(jnp.zeros((per * count - used, chans), jnp.float32))
    stack = jnp.concatenate(rows, axis=0).reshape(count, per, chans)
    pieces = lax.all_to_all(stack, ("seg", "grp"), split_axis=0, concat_axis=0, tiled=True)
    mine = (jnp.sum(pieces, axis=0, keepdims=True) * scale).astype(jnp.bfloat16)
    spread = jnp.broadcast_to(mine, stack.shape)
    whole = lax.all_to_all(spread, ("seg", "grp"), split_axis=0, concat_axis=0, tiled=True)
    whole = whole.astype(jnp.float32).reshape(-1, chans)
    out = []
    offset = 0
    for p in parts:
        size = p.size // chans
        out.append(whole[offset : offset + size].reshape(p.shape))
        offset += size
    return out


def local(
    frames_in, spatial_weight, temporal_weight, uniting_weight, key_index, dilation, cotangent
):
    local_frames, rows, cols, chans = frames_in.shape
    pixels = rows * cols
    seg_count = lax.axis_size("seg")
    count = lax.axis_size(("seg", "grp"))
    used = pixels // count
    pre_spatial = spatial_forward(frames_in, spatial_weight)
    act_zero = jax.nn.silu(pre_spatial).astype(jnp.bfloat16).reshape(local_frames, pixels, chans)
    cot_local = cotangent.reshape(local_frames, pixels, chans)
    act_blocks = fm_to_pixels(act_zero)
    act_blocks, cot_local = lax.optimization_barrier((act_blocks, cot_local))
    cot_blocks = fm_to_pixels(cot_local)
    acts = [act_blocks]
    total_frames, width = act_blocks.shape[0], act_blocks.shape[1]
    seg_frames = total_frames // seg_count
    pres = []
    for layer in range(LAYERS):
        pre, act = temporal_forward_k(acts[-1], temporal_weight[layer], dilation[layer])
        pres.append(pre)
        acts.append(act)
    feat = acts[-1]
    seg_shape = (seg_count, seg_frames, width, chans)
    feat_seg = feat.reshape(seg_shape)
    positions = jnp.arange(seg_frames, dtype=jnp.int32)
    onehot = positions[None, :] == key_index[:, None]
    keys = jnp.einsum(
        "ns,nsjc->njc", onehot.astype(jnp.bfloat16), feat_seg, preferred_element_type=jnp.float32
    ).astype(jnp.bfloat16)
    key_full = jnp.broadcast_to(keys[:, None], seg_shape).reshape(-1, chans)
    feat_flat = feat.reshape(-1, chans)
    key_part = jnp.dot(
        keys.reshape(-1, chans), uniting_weight[1], preferred_element_type=jnp.float32
    ).reshape(seg_count, 1, width, chans)
    main_part = jnp.dot(feat_flat, uniting_weight[0], preferred_element_type=jnp.float32)
    united_blocks = (main_part.reshape(seg_shape) + key_part).astype(jnp.bfloat16)
    united = fm_to_frames(united_blocks.reshape(total_frames, width, chans), used)
    cot_flat = cot_blocks.reshape(-1, chans)
    grad_feat = jnp.dot(cot_flat, uniting_weight[0].T, preferred_element_type=jnp.float32)
    seg_cot = jnp.sum(cot_blocks.reshape(seg_shape).astype(jnp.float32), axis=1)
    key_term = jnp.dot(
        seg_cot.reshape(-1, chans),
        uniting_weight[1].T.astype(jnp.float32),
        precision=lax.Precision.HIGHEST,
    ).reshape(seg_count, 1, width, chans)
    placed = onehot.astype(jnp.float32)[:, :, None, None] * key_term
    grad_feat = grad_feat.reshape(seg_shape) + placed
    grad_feat = grad_feat.reshape(total_frames, width, chans)
    grad_uniting = jnp.stack([inner(feat_flat, cot_flat), inner(key_full, cot_flat)])
    grad_pre = (grad_feat * silu_grad(pres[-1])).astype(jnp.bfloat16)
    tgrads = [None] * LAYERS
    layer_grads = [None] * LAYERS
    for layer in range(LAYERS - 1, -1, -1):
        below = pres[layer - 1] if layer > 0 else None
        layer_grads[layer] = grad_pre
        grad_pre = temporal_backward_k(
            acts[layer], grad_pre, temporal_weight[layer], dilation[layer], below
        )
    grad_act0 = grad_pre
    grad_time = fm_to_frames(grad_act0, used).reshape(frames_in.shape)
    for layer in range(LAYERS):
        tgrads[layer] = temporal_wgrad_k(acts[layer], layer_grads[layer], dilation[layer])
    grad_spre = (grad_time.astype(jnp.float32) * silu_grad(pre_spatial)).astype(jnp.bfloat16)
    grad_frames = spatial_back(grad_spre, spatial_weight).astype(jnp.bfloat16)
    grad_spatial = spatial_wgrad(frames_in, grad_spre)
    scale = 1.0 / jnp.sqrt(jnp.float32(total_frames * pixels))
    summed = all_sum((grad_spatial, jnp.stack(tgrads), grad_uniting), scale)
    return (
        united.reshape(frames_in.shape),
        grad_frames,
        summed[0],
        summed[1],
        summed[2],
    )


def solution(mesh):
    placed = (
        P(("seg", "grp"), None, None, None),
        P(),
        P(),
        P(),
        P(),
        P(),
        P(("seg", "grp"), None, None, None),
    )
    return jax.shard_map(
        local,
        mesh=mesh,
        in_specs=placed,
        out_specs=(
            P(("seg", "grp"), None, None, None),
            P(("seg", "grp"), None, None, None),
            P(),
            P(),
            P(),
        ),
        check_vma=False,
    )
```

```python
import functools

import jax
import jax.numpy as jnp
from jax import lax
from jax.sharding import PartitionSpec as P
from jax.experimental import pallas as pl
from jax.experimental.pallas import tpu as pltpu

LAYERS = 2
DMAX = 8


def from_root(value, axis, root):
    mine = lax.axis_index(axis) == root
    return lax.psum(jnp.where(mine, value, jnp.zeros_like(value)), axis)


def silu_grad(value):
    sigma = jax.nn.sigmoid(value)
    return sigma * (1.0 + value * (1.0 - sigma))


def inner(left, right):
    return lax.dot_general(
        left, right, (((0,), (0,)), ((), ())), preferred_element_type=jnp.float32
    )


def spatial_forward(frames, kernel):
    count, rows, cols, chans = frames.shape
    padded = jnp.pad(frames, ((0, 0), (1, 1), (1, 1), (0, 0)))
    total = jnp.zeros((count * rows * cols, chans), jnp.float32)
    for row_tap in range(3):
        for col_tap in range(3):
            piece = padded[:, row_tap : row_tap + rows, col_tap : col_tap + cols, :].reshape(
                -1, chans
            )
            total = total + jnp.dot(
                piece, kernel[3 * row_tap + col_tap], preferred_element_type=jnp.float32
            )
    return total.reshape(frames.shape)


def spatial_back(grads, kernel):
    count, rows, cols, chans = grads.shape
    padded = jnp.pad(grads, ((0, 0), (1, 1), (1, 1), (0, 0)))
    total = jnp.zeros((count * rows * cols, chans), jnp.float32)
    for row_tap in range(3):
        for col_tap in range(3):
            piece = padded[
                :, 2 - row_tap : 2 - row_tap + rows, 2 - col_tap : 2 - col_tap + cols, :
            ].reshape(-1, chans)
            total = total + jnp.dot(
                piece, kernel[3 * row_tap + col_tap].T, preferred_element_type=jnp.float32
            )
    return total.reshape(grads.shape)


def spatial_wgrad(frames, grads):
    count, rows, cols, chans = frames.shape
    padded = jnp.pad(frames, ((0, 0), (1, 1), (1, 1), (0, 0)))
    flat_grads = grads.reshape(-1, chans)
    result = []
    for row_tap in range(3):
        for col_tap in range(3):
            piece = padded[:, row_tap : row_tap + rows, col_tap : col_tap + cols, :].reshape(
                -1, chans
            )
            result.append(inner(piece, flat_grads))
    return jnp.stack(result)


def shifted(values, offset):
    padded = jnp.pad(values, ((2 * DMAX, 2 * DMAX), (0, 0), (0, 0)))
    start = 2 * DMAX + offset
    return lax.dynamic_slice_in_dim(padded, start, values.shape[0], 0)


def temporal_forward(acts, kernel, step_size):
    chans = acts.shape[2]
    total = jnp.zeros((acts.shape[0] * acts.shape[1], chans), jnp.float32)
    for tap in range(5):
        piece = shifted(acts, (tap - 2) * step_size).reshape(-1, chans)
        total = total + jnp.dot(piece, kernel[tap], preferred_element_type=jnp.float32)
    return total.reshape(acts.shape)


def temporal_back(grads, kernel, step_size):
    chans = grads.shape[2]
    total = jnp.zeros((grads.shape[0] * grads.shape[1], chans), jnp.float32)
    for tap in range(5):
        piece = shifted(grads, (2 - tap) * step_size).reshape(-1, chans)
        total = total + jnp.dot(piece, kernel[tap].T, preferred_element_type=jnp.float32)
    return total.reshape(grads.shape)


def temporal_wgrad(acts, grads, step_size):
    chans = acts.shape[2]
    flat_grads = grads.reshape(-1, chans)
    return jnp.stack(
        [
            inner(shifted(acts, (tap - 2) * step_size).reshape(-1, chans), flat_grads)
            for tap in range(5)
        ]
    )


def to_pixels(flat):
    count = lax.axis_size(("seg", "grp"))
    chans = flat.shape[-1]
    strided = flat.reshape(-1, count, chans)
    return lax.all_to_all(strided, ("seg", "grp"), split_axis=1, concat_axis=1, tiled=True)


def to_frames(blocks):
    out = lax.all_to_all(blocks, ("seg", "grp"), split_axis=1, concat_axis=1, tiled=True)
    return out.reshape(1, -1, blocks.shape[-1])


def shifted1(values, offset):
    padded = jnp.pad(values, ((0, 0), (2 * DMAX, 2 * DMAX), (0, 0)))
    start = 2 * DMAX + offset
    return lax.dynamic_slice_in_dim(padded, start, values.shape[1], 1)


def temporal_forward1(acts, kernel, step_size):
    chans = acts.shape[2]
    total = jnp.zeros((acts.shape[0] * acts.shape[1], chans), jnp.float32)
    for tap in range(5):
        piece = shifted1(acts, (tap - 2) * step_size).reshape(-1, chans)
        total = total + jnp.dot(piece, kernel[tap], preferred_element_type=jnp.float32)
    return total.reshape(acts.shape)


def temporal_back1(grads, kernel, step_size):
    chans = grads.shape[2]
    total = jnp.zeros((grads.shape[0] * grads.shape[1], chans), jnp.float32)
    for tap in range(5):
        piece = shifted1(grads, (2 - tap) * step_size).reshape(-1, chans)
        total = total + jnp.dot(piece, kernel[tap].T, preferred_element_type=jnp.float32)
    return total.reshape(grads.shape)


def temporal_wgrad1(acts, grads, step_size):
    chans = acts.shape[2]
    flat_grads = grads.reshape(-1, chans)
    return jnp.stack(
        [
            inner(shifted1(acts, (tap - 2) * step_size).reshape(-1, chans), flat_grads)
            for tap in range(5)
        ]
    )


HALO = 2 * DMAX
FB = 32


def fm_to_pixels(flat):
    count = lax.axis_size(("seg", "grp"))
    chans = flat.shape[-1]
    strided = flat.reshape(-1, count, chans)
    rows = -(-strided.shape[0] // 16) * 16
    strided = jnp.pad(strided, ((0, rows - strided.shape[0]), (0, 0), (0, 0)))
    out = lax.all_to_all(strided, ("seg", "grp"), split_axis=1, concat_axis=1, tiled=True)
    return jnp.transpose(out, (1, 0, 2))


def fm_to_frames(blocks, used):
    moved = jnp.transpose(blocks, (1, 0, 2))
    out = lax.all_to_all(moved, ("seg", "grp"), split_axis=1, concat_axis=1, tiled=True)
    return out[:used].reshape(1, -1, blocks.shape[-1])


def fill_halo(src_ref, pad_ref):
    frames = src_ref.shape[0]
    zeros = jnp.zeros((HALO,) + pad_ref.shape[1:], pad_ref.dtype)
    pad_ref[0:HALO] = zeros
    pad_ref[HALO + frames : 2 * HALO + frames] = zeros
    pad_ref[HALO : HALO + frames] = src_ref[...]


def tap_rows(pad_ref, start, rows):
    return pad_ref[pl.ds(start, FB)].reshape(rows, pad_ref.shape[-1])


def tfwd_kernel(dil_ref, act_ref, w_ref, pre_ref, out_ref, pad_ref):
    frames, width, chans = act_ref.shape
    fill_halo(act_ref, pad_ref)
    step = dil_ref[0]
    rows = FB * width
    for block in range(frames // FB):
        base = HALO + block * FB
        pre = None
        for tap in range(5):
            term = jnp.dot(
                tap_rows(pad_ref, base + (tap - 2) * step, rows),
                w_ref[tap * chans : (tap + 1) * chans, :],
                preferred_element_type=jnp.float32,
            )
            pre = term if pre is None else pre + term
        pre_ref[block * FB : (block + 1) * FB] = pre.reshape(FB, width, chans)
        out_ref[block * FB : (block + 1) * FB] = (
            (pre / (1.0 + jnp.exp(-pre))).astype(jnp.bfloat16).reshape(FB, width, chans)
        )


def temporal_forward_k(acts, kernel, step_size):
    frames, width, chans = acts.shape
    return pl.pallas_call(
        tfwd_kernel,
        grid_spec=pltpu.PrefetchScalarGridSpec(
            num_scalar_prefetch=1,
            grid=(1,),
            in_specs=[
                pl.BlockSpec(acts.shape, lambda i, d: (0, 0, 0)),
                pl.BlockSpec((5 * chans, chans), lambda i, d: (0, 0)),
            ],
            out_specs=[
                pl.BlockSpec(acts.shape, lambda i, d: (0, 0, 0)),
                pl.BlockSpec(acts.shape, lambda i, d: (0, 0, 0)),
            ],
            scratch_shapes=[pltpu.VMEM((frames + 2 * HALO, width, chans), jnp.bfloat16)],
        ),
        out_shape=[
            jax.ShapeDtypeStruct(acts.shape, jnp.float32),
            jax.ShapeDtypeStruct(acts.shape, jnp.bfloat16),
        ],
        cost_estimate=pl.CostEstimate(
            flops=2 * frames * width * chans * chans * 5,
            transcendentals=frames * width * chans,
            bytes_accessed=frames * width * chans * 8,
        ),
    )(step_size.reshape(1), acts, kernel.reshape(5 * chans, chans))


def tbwd_kernel(with_pre, dil_ref, act_ref, grad_ref, wt_ref, *rest):
    if with_pre:
        pre_ref, out_ref, pad_ref = rest
    else:
        out_ref, pad_ref = rest
    frames, width, chans = act_ref.shape
    fill_halo(grad_ref, pad_ref)
    step = dil_ref[0]
    rows = FB * width
    for block in range(frames // FB):
        base = HALO + block * FB
        grad_act = None
        for tap in range(5):
            term = lax.dot_general(
                tap_rows(pad_ref, base - (tap - 2) * step, rows),
                wt_ref[tap * chans : (tap + 1) * chans, :],
                (((1,), (1,)), ((), ())),
                preferred_element_type=jnp.float32,
            )
            grad_act = term if grad_act is None else grad_act + term
        if with_pre:
            pre = pre_ref[block * FB : (block + 1) * FB].reshape(rows, chans)
            sigma = 1.0 / (1.0 + jnp.exp(-pre))
            grad_act = grad_act * (sigma * (1.0 + pre * (1.0 - sigma)))
        out_ref[block * FB : (block + 1) * FB] = (
            grad_act.astype(jnp.bfloat16).reshape(FB, width, chans)
        )


def twgrad_kernel(dil_ref, act_ref, grad_ref, tg_ref, pad_ref):
    frames, width, chans = act_ref.shape
    fill_halo(grad_ref, pad_ref)
    step = dil_ref[0]
    rows = FB * width
    total = None
    for block in range(frames // FB):
        base = HALO + block * FB
        flat_act = act_ref[block * FB : (block + 1) * FB].reshape(rows, chans)
        parts = [
            lax.dot_general(
                flat_act,
                tap_rows(pad_ref, base - (tap - 2) * step, rows),
                (((0,), (0,)), ((), ())),
                preferred_element_type=jnp.float32,
            )
            for tap in range(5)
        ]
        total = parts if total is None else [t + q for t, q in zip(total, parts)]
    for tap in range(5):
        tg_ref[tap] = total[tap]


def temporal_wgrad_k(acts, grads, step_size):
    frames, width, chans = acts.shape
    full = pl.BlockSpec(acts.shape, lambda i, d: (0, 0, 0))
    return pl.pallas_call(
        twgrad_kernel,
        grid_spec=pltpu.PrefetchScalarGridSpec(
            num_scalar_prefetch=1,
            grid=(1,),
            in_specs=[full, full],
            out_specs=pl.BlockSpec((5, chans, chans), lambda i, d: (0, 0, 0)),
            scratch_shapes=[pltpu.VMEM((frames + 2 * HALO, width, chans), jnp.bfloat16)],
        ),
        out_shape=jax.ShapeDtypeStruct((5, chans, chans), jnp.float32),
        cost_estimate=pl.CostEstimate(
            flops=2 * frames * width * chans * chans * 5,
            transcendentals=0,
            bytes_accessed=frames * width * chans * 4,
        ),
    )(step_size.reshape(1), acts, grads)


def temporal_backward_k(acts, grads, kernel, step_size, pre_below):
    frames, width, chans = acts.shape
    full = pl.BlockSpec(acts.shape, lambda i, d: (0, 0, 0))
    with_pre = pre_below is not None
    in_specs = [full, full, pl.BlockSpec((5 * chans, chans), lambda i, d: (0, 0))]
    operands = [step_size.reshape(1), acts, grads, kernel.reshape(5 * chans, chans)]
    if with_pre:
        in_specs.append(full)
        operands.append(pre_below)
    return pl.pallas_call(
        functools.partial(tbwd_kernel, with_pre),
        grid_spec=pltpu.PrefetchScalarGridSpec(
            num_scalar_prefetch=1,
            grid=(1,),
            in_specs=in_specs,
            out_specs=full,
            scratch_shapes=[pltpu.VMEM((frames + 2 * HALO, width, chans), jnp.bfloat16)],
        ),
        out_shape=jax.ShapeDtypeStruct(acts.shape, jnp.bfloat16),
        cost_estimate=pl.CostEstimate(
            flops=2 * frames * width * chans * chans * 5,
            transcendentals=frames * width * chans,
            bytes_accessed=frames * width * chans * 10,
        ),
    )(*operands)


def all_sum(parts, scale):
    chans = parts[0].shape[-1]
    count = lax.axis_size(("seg", "grp"))
    rows = [p.reshape(-1, chans) for p in parts]
    used = sum(r.shape[0] for r in rows)
    per = -(-used // (count * 8)) * 8
    rows.append(jnp.zeros((per * count - used, chans), jnp.float32))
    stack = jnp.concatenate(rows, axis=0).reshape(count, per, chans)
    pieces = lax.all_to_all(stack, ("seg", "grp"), split_axis=0, concat_axis=0, tiled=True)
    mine = (jnp.sum(pieces, axis=0, keepdims=True) * scale).astype(jnp.bfloat16)
    spread = jnp.broadcast_to(mine, stack.shape)
    whole = lax.all_to_all(spread, ("seg", "grp"), split_axis=0, concat_axis=0, tiled=True)
    whole = whole.astype(jnp.float32).reshape(-1, chans)
    out = []
    offset = 0
    for p in parts:
        size = p.size // chans
        out.append(whole[offset : offset + size].reshape(p.shape))
        offset += size
    return out


def local(
    frames_in, spatial_weight, temporal_weight, uniting_weight, key_index, dilation, cotangent
):
    local_frames, rows, cols, chans = frames_in.shape
    pixels = rows * cols
    seg_count = lax.axis_size("seg")
    count = lax.axis_size(("seg", "grp"))
    used = pixels // count
    pre_spatial = spatial_forward(frames_in, spatial_weight)
    act_zero = jax.nn.silu(pre_spatial).astype(jnp.bfloat16).reshape(local_frames, pixels, chans)
    cot_local = cotangent.reshape(local_frames, pixels, chans)
    act_blocks = fm_to_pixels(act_zero)
    act_blocks, cot_local = lax.optimization_barrier((act_blocks, cot_local))
    cot_blocks = fm_to_pixels(cot_local)
    acts = [act_blocks]
    total_frames, width = act_blocks.shape[0], act_blocks.shape[1]
    seg_frames = total_frames // seg_count
    pres = []
    for layer in range(LAYERS):
        pre, act = temporal_forward_k(acts[-1], temporal_weight[layer], dilation[layer])
        pres.append(pre)
        acts.append(act)
    feat = acts[-1]
    seg_shape = (seg_count, seg_frames, width, chans)
    feat_seg = feat.reshape(seg_shape)
    positions = jnp.arange(seg_frames, dtype=jnp.int32)
    onehot = positions[None, :] == key_index[:, None]
    keys = jnp.einsum(
        "ns,nsjc->njc", onehot.astype(jnp.bfloat16), feat_seg, preferred_element_type=jnp.float32
    ).astype(jnp.bfloat16)
    key_full = jnp.broadcast_to(keys[:, None], seg_shape).reshape(-1, chans)
    feat_flat = feat.reshape(-1, chans)
    key_part = jnp.dot(
        keys.reshape(-1, chans), uniting_weight[1], preferred_element_type=jnp.float32
    ).reshape(seg_count, 1, width, chans)
    main_part = jnp.dot(feat_flat, uniting_weight[0], preferred_element_type=jnp.float32)
    united_blocks = (main_part.reshape(seg_shape) + key_part).astype(jnp.bfloat16)
    united = fm_to_frames(united_blocks.reshape(total_frames, width, chans), used)
    cot_flat = cot_blocks.reshape(-1, chans)
    grad_feat = jnp.dot(cot_flat, uniting_weight[0].T, preferred_element_type=jnp.float32)
    seg_cot = jnp.sum(cot_blocks.reshape(seg_shape).astype(jnp.float32), axis=1)
    key_term = jnp.dot(
        seg_cot.reshape(-1, chans),
        uniting_weight[1].T.astype(jnp.float32),
        precision=lax.Precision.HIGHEST,
    ).reshape(seg_count, 1, width, chans)
    placed = onehot.astype(jnp.float32)[:, :, None, None] * key_term
    grad_feat = grad_feat.reshape(seg_shape) + placed
    grad_feat = grad_feat.reshape(total_frames, width, chans)
    grad_uniting = jnp.stack([inner(feat_flat, cot_flat), inner(key_full, cot_flat)])
    grad_pre = (grad_feat * silu_grad(pres[-1])).astype(jnp.bfloat16)
    tgrads = [None] * LAYERS
    layer_grads = [None] * LAYERS
    for layer in range(LAYERS - 1, -1, -1):
        below = pres[layer - 1] if layer > 0 else None
        layer_grads[layer] = grad_pre
        grad_pre = temporal_backward_k(
            acts[layer], grad_pre, temporal_weight[layer], dilation[layer], below
        )
    grad_act0 = grad_pre
    grad_time = fm_to_frames(grad_act0, used).reshape(frames_in.shape)
    for layer in range(LAYERS):
        tgrads[layer] = temporal_wgrad_k(acts[layer], layer_grads[layer], dilation[layer])
    grad_spre = (grad_time.astype(jnp.float32) * silu_grad(pre_spatial)).astype(jnp.bfloat16)
    grad_frames = spatial_back(grad_spre, spatial_weight).astype(jnp.bfloat16)
    grad_spatial = spatial_wgrad(frames_in, grad_spre)
    scale = 1.0 / jnp.sqrt(jnp.float32(total_frames * pixels))
    summed = all_sum((grad_spatial, jnp.stack(tgrads), grad_uniting), scale)
    return (
        united.reshape(frames_in.shape),
        grad_frames,
        summed[0],
        summed[1],
        summed[2],
    )


def solution(mesh):
    placed = (
        P(("seg", "grp"), None, None, None),
        P(),
        P(),
        P(),
        P(),
        P(),
        P(("seg", "grp"), None, None, None),
    )
    return jax.shard_map(
        local,
        mesh=mesh,
        in_specs=placed,
        out_specs=(
            P(("seg", "grp"), None, None, None),
            P(("seg", "grp"), None, None, None),
            P(),
            P(),
            P(),
        ),
        check_vma=False,
    )
```

```python
import functools

import jax
import jax.numpy as jnp
from jax import lax
from jax.sharding import PartitionSpec as P
from jax.experimental import pallas as pl
from jax.experimental.pallas import tpu as pltpu

LAYERS = 2
DMAX = 8


def from_root(value, axis, root):
    mine = lax.axis_index(axis) == root
    return lax.psum(jnp.where(mine, value, jnp.zeros_like(value)), axis)


def silu_grad(value):
    sigma = jax.nn.sigmoid(value)
    return sigma * (1.0 + value * (1.0 - sigma))


def inner(left, right):
    return lax.dot_general(
        left, right, (((0,), (0,)), ((), ())), preferred_element_type=jnp.float32
    )


def spatial_forward(frames, kernel):
    count, rows, cols, chans = frames.shape
    padded = jnp.pad(frames, ((0, 0), (1, 1), (1, 1), (0, 0)))
    total = jnp.zeros((count * rows * cols, chans), jnp.float32)
    for row_tap in range(3):
        for col_tap in range(3):
            piece = padded[:, row_tap : row_tap + rows, col_tap : col_tap + cols, :].reshape(
                -1, chans
            )
            total = total + jnp.dot(
                piece, kernel[3 * row_tap + col_tap], preferred_element_type=jnp.float32
            )
    return total.reshape(frames.shape)


def spatial_back(grads, kernel):
    count, rows, cols, chans = grads.shape
    padded = jnp.pad(grads, ((0, 0), (1, 1), (1, 1), (0, 0)))
    total = jnp.zeros((count * rows * cols, chans), jnp.float32)
    for row_tap in range(3):
        for col_tap in range(3):
            piece = padded[
                :, 2 - row_tap : 2 - row_tap + rows, 2 - col_tap : 2 - col_tap + cols, :
            ].reshape(-1, chans)
            total = total + jnp.dot(
                piece, kernel[3 * row_tap + col_tap].T, preferred_element_type=jnp.float32
            )
    return total.reshape(grads.shape)


def spatial_wgrad(frames, grads):
    count, rows, cols, chans = frames.shape
    padded = jnp.pad(frames, ((0, 0), (1, 1), (1, 1), (0, 0)))
    flat_grads = grads.reshape(-1, chans)
    result = []
    for row_tap in range(3):
        for col_tap in range(3):
            piece = padded[:, row_tap : row_tap + rows, col_tap : col_tap + cols, :].reshape(
                -1, chans
            )
            result.append(inner(piece, flat_grads))
    return jnp.stack(result)


def shifted(values, offset):
    padded = jnp.pad(values, ((2 * DMAX, 2 * DMAX), (0, 0), (0, 0)))
    start = 2 * DMAX + offset
    return lax.dynamic_slice_in_dim(padded, start, values.shape[0], 0)


def temporal_forward(acts, kernel, step_size):
    chans = acts.shape[2]
    total = jnp.zeros((acts.shape[0] * acts.shape[1], chans), jnp.float32)
    for tap in range(5):
        piece = shifted(acts, (tap - 2) * step_size).reshape(-1, chans)
        total = total + jnp.dot(piece, kernel[tap], preferred_element_type=jnp.float32)
    return total.reshape(acts.shape)


def temporal_back(grads, kernel, step_size):
    chans = grads.shape[2]
    total = jnp.zeros((grads.shape[0] * grads.shape[1], chans), jnp.float32)
    for tap in range(5):
        piece = shifted(grads, (2 - tap) * step_size).reshape(-1, chans)
        total = total + jnp.dot(piece, kernel[tap].T, preferred_element_type=jnp.float32)
    return total.reshape(grads.shape)


def temporal_wgrad(acts, grads, step_size):
    chans = acts.shape[2]
    flat_grads = grads.reshape(-1, chans)
    return jnp.stack(
        [
            inner(shifted(acts, (tap - 2) * step_size).reshape(-1, chans), flat_grads)
            for tap in range(5)
        ]
    )


def to_pixels(flat):
    count = lax.axis_size(("seg", "grp"))
    chans = flat.shape[-1]
    strided = flat.reshape(-1, count, chans)
    return lax.all_to_all(strided, ("seg", "grp"), split_axis=1, concat_axis=1, tiled=True)


def to_frames(blocks):
    out = lax.all_to_all(blocks, ("seg", "grp"), split_axis=1, concat_axis=1, tiled=True)
    return out.reshape(1, -1, blocks.shape[-1])


def shifted1(values, offset):
    padded = jnp.pad(values, ((0, 0), (2 * DMAX, 2 * DMAX), (0, 0)))
    start = 2 * DMAX + offset
    return lax.dynamic_slice_in_dim(padded, start, values.shape[1], 1)


def temporal_forward1(acts, kernel, step_size):
    chans = acts.shape[2]
    total = jnp.zeros((acts.shape[0] * acts.shape[1], chans), jnp.float32)
    for tap in range(5):
        piece = shifted1(acts, (tap - 2) * step_size).reshape(-1, chans)
        total = total + jnp.dot(piece, kernel[tap], preferred_element_type=jnp.float32)
    return total.reshape(acts.shape)


def temporal_back1(grads, kernel, step_size):
    chans = grads.shape[2]
    total = jnp.zeros((grads.shape[0] * grads.shape[1], chans), jnp.float32)
    for tap in range(5):
        piece = shifted1(grads, (2 - tap) * step_size).reshape(-1, chans)
        total = total + jnp.dot(piece, kernel[tap].T, preferred_element_type=jnp.float32)
    return total.reshape(grads.shape)


def temporal_wgrad1(acts, grads, step_size):
    chans = acts.shape[2]
    flat_grads = grads.reshape(-1, chans)
    return jnp.stack(
        [
            inner(shifted1(acts, (tap - 2) * step_size).reshape(-1, chans), flat_grads)
            for tap in range(5)
        ]
    )


HALO = 2 * DMAX
FB = 32


def fm_to_pixels(flat):
    count = lax.axis_size(("seg", "grp"))
    chans = flat.shape[-1]
    strided = flat.reshape(-1, count, chans)
    rows = -(-strided.shape[0] // 16) * 16
    strided = jnp.pad(strided, ((0, rows - strided.shape[0]), (0, 0), (0, 0)))
    out = lax.all_to_all(strided, ("seg", "grp"), split_axis=1, concat_axis=1, tiled=True)
    return jnp.transpose(out, (1, 0, 2))


def fm_to_frames(blocks, used):
    moved = jnp.transpose(blocks, (1, 0, 2))
    out = lax.all_to_all(moved, ("seg", "grp"), split_axis=1, concat_axis=1, tiled=True)
    return out[:used].reshape(1, -1, blocks.shape[-1])


def fill_halo(src_ref, pad_ref):
    frames = src_ref.shape[0]
    zeros = jnp.zeros((HALO,) + pad_ref.shape[1:], pad_ref.dtype)
    pad_ref[0:HALO] = zeros
    pad_ref[HALO + frames : 2 * HALO + frames] = zeros
    pad_ref[HALO : HALO + frames] = src_ref[...]


def tap_rows(pad_ref, start, rows):
    return pad_ref[pl.ds(start, FB)].reshape(rows, pad_ref.shape[-1])


def tfwd_kernel(dil_ref, act_ref, w_ref, pre_ref, out_ref, pad_ref):
    frames, width, chans = act_ref.shape
    fill_halo(act_ref, pad_ref)
    step = dil_ref[0]
    rows = FB * width
    for block in range(frames // FB):
        base = HALO + block * FB
        stacked = jnp.concatenate(
            [tap_rows(pad_ref, base + (tap - 2) * step, rows) for tap in range(5)], axis=1
        )
        pre = jnp.dot(stacked, w_ref[...], preferred_element_type=jnp.float32)
        pre_ref[block * FB : (block + 1) * FB] = pre.reshape(FB, width, chans)
        out_ref[block * FB : (block + 1) * FB] = (
            (pre / (1.0 + jnp.exp(-pre))).astype(jnp.bfloat16).reshape(FB, width, chans)
        )


def temporal_forward_k(acts, kernel, step_size):
    frames, width, chans = acts.shape
    return pl.pallas_call(
        tfwd_kernel,
        grid_spec=pltpu.PrefetchScalarGridSpec(
            num_scalar_prefetch=1,
            grid=(1,),
            in_specs=[
                pl.BlockSpec(acts.shape, lambda i, d: (0, 0, 0)),
                pl.BlockSpec((5 * chans, chans), lambda i, d: (0, 0)),
            ],
            out_specs=[
                pl.BlockSpec(acts.shape, lambda i, d: (0, 0, 0)),
                pl.BlockSpec(acts.shape, lambda i, d: (0, 0, 0)),
            ],
            scratch_shapes=[pltpu.VMEM((frames + 2 * HALO, width, chans), jnp.bfloat16)],
        ),
        out_shape=[
            jax.ShapeDtypeStruct(acts.shape, jnp.float32),
            jax.ShapeDtypeStruct(acts.shape, jnp.bfloat16),
        ],
        cost_estimate=pl.CostEstimate(
            flops=2 * frames * width * chans * chans * 5,
            transcendentals=frames * width * chans,
            bytes_accessed=frames * width * chans * 8,
        ),
    )(step_size.reshape(1), acts, kernel.reshape(5 * chans, chans))


def tbwd_kernel(with_pre, dil_ref, act_ref, grad_ref, wt_ref, *rest):
    if with_pre:
        pre_ref, out_ref, pad_ref = rest
    else:
        out_ref, pad_ref = rest
    frames, width, chans = act_ref.shape
    fill_halo(grad_ref, pad_ref)
    step = dil_ref[0]
    rows = FB * width
    for block in range(frames // FB):
        base = HALO + block * FB
        stacked = jnp.concatenate(
            [tap_rows(pad_ref, base - (tap - 2) * step, rows) for tap in range(5)], axis=1
        )
        grad_act = None
        for tap in range(5):
            term = lax.dot_general(
                stacked[:, tap * chans : (tap + 1) * chans],
                wt_ref[tap * chans : (tap + 1) * chans, :],
                (((1,), (1,)), ((), ())),
                preferred_element_type=jnp.float32,
            )
            grad_act = term if grad_act is None else grad_act + term
        if with_pre:
            pre = pre_ref[block * FB : (block + 1) * FB].reshape(rows, chans)
            sigma = 1.0 / (1.0 + jnp.exp(-pre))
            grad_act = grad_act * (sigma * (1.0 + pre * (1.0 - sigma)))
        out_ref[block * FB : (block + 1) * FB] = (
            grad_act.astype(jnp.bfloat16).reshape(FB, width, chans)
        )


def twgrad_kernel(dil_ref, act_ref, grad_ref, tg_ref, pad_ref):
    frames, width, chans = act_ref.shape
    fill_halo(grad_ref, pad_ref)
    step = dil_ref[0]
    rows = FB * width
    total = None
    for block in range(frames // FB):
        base = HALO + block * FB
        stacked = jnp.concatenate(
            [tap_rows(pad_ref, base - (tap - 2) * step, rows) for tap in range(5)], axis=1
        )
        flat_act = act_ref[block * FB : (block + 1) * FB].reshape(rows, chans)
        part = lax.dot_general(
            flat_act, stacked, (((0,), (0,)), ((), ())), preferred_element_type=jnp.float32
        )
        total = part if total is None else total + part
    for tap in range(5):
        tg_ref[tap] = total[:, tap * chans : (tap + 1) * chans]


def temporal_wgrad_k(acts, grads, step_size):
    frames, width, chans = acts.shape
    full = pl.BlockSpec(acts.shape, lambda i, d: (0, 0, 0))
    return pl.pallas_call(
        twgrad_kernel,
        grid_spec=pltpu.PrefetchScalarGridSpec(
            num_scalar_prefetch=1,
            grid=(1,),
            in_specs=[full, full],
            out_specs=pl.BlockSpec((5, chans, chans), lambda i, d: (0, 0, 0)),
            scratch_shapes=[pltpu.VMEM((frames + 2 * HALO, width, chans), jnp.bfloat16)],
        ),
        out_shape=jax.ShapeDtypeStruct((5, chans, chans), jnp.float32),
        cost_estimate=pl.CostEstimate(
            flops=2 * frames * width * chans * chans * 5,
            transcendentals=0,
            bytes_accessed=frames * width * chans * 4,
        ),
    )(step_size.reshape(1), acts, grads)


def temporal_backward_k(acts, grads, kernel, step_size, pre_below):
    frames, width, chans = acts.shape
    full = pl.BlockSpec(acts.shape, lambda i, d: (0, 0, 0))
    with_pre = pre_below is not None
    in_specs = [full, full, pl.BlockSpec((5 * chans, chans), lambda i, d: (0, 0))]
    operands = [step_size.reshape(1), acts, grads, kernel.reshape(5 * chans, chans)]
    if with_pre:
        in_specs.append(full)
        operands.append(pre_below)
    return pl.pallas_call(
        functools.partial(tbwd_kernel, with_pre),
        grid_spec=pltpu.PrefetchScalarGridSpec(
            num_scalar_prefetch=1,
            grid=(1,),
            in_specs=in_specs,
            out_specs=full,
            scratch_shapes=[pltpu.VMEM((frames + 2 * HALO, width, chans), jnp.bfloat16)],
        ),
        out_shape=jax.ShapeDtypeStruct(acts.shape, jnp.bfloat16),
        cost_estimate=pl.CostEstimate(
            flops=2 * frames * width * chans * chans * 5,
            transcendentals=frames * width * chans,
            bytes_accessed=frames * width * chans * 10,
        ),
    )(*operands)


def all_sum(parts, scale):
    chans = parts[0].shape[-1]
    count = lax.axis_size(("seg", "grp"))
    rows = [p.reshape(-1, chans) for p in parts]
    used = sum(r.shape[0] for r in rows)
    per = -(-used // (count * 8)) * 8
    rows.append(jnp.zeros((per * count - used, chans), jnp.float32))
    stack = jnp.concatenate(rows, axis=0).reshape(count, per, chans)
    pieces = lax.all_to_all(stack, ("seg", "grp"), split_axis=0, concat_axis=0, tiled=True)
    mine = (jnp.sum(pieces, axis=0, keepdims=True) * scale).astype(jnp.bfloat16)
    spread = jnp.broadcast_to(mine, stack.shape)
    whole = lax.all_to_all(spread, ("seg", "grp"), split_axis=0, concat_axis=0, tiled=True)
    whole = whole.astype(jnp.float32).reshape(-1, chans)
    out = []
    offset = 0
    for p in parts:
        size = p.size // chans
        out.append(whole[offset : offset + size].reshape(p.shape))
        offset += size
    return out


def local(
    frames_in, spatial_weight, temporal_weight, uniting_weight, key_index, dilation, cotangent
):
    local_frames, rows, cols, chans = frames_in.shape
    pixels = rows * cols
    seg_count = lax.axis_size("seg")
    count = lax.axis_size(("seg", "grp"))
    used = pixels // count
    pre_spatial = lax.conv_general_dilated(
        frames_in,
        spatial_weight.reshape(3, 3, chans, chans),
        (1, 1),
        "SAME",
        dimension_numbers=("NHWC", "HWIO", "NHWC"),
        preferred_element_type=jnp.float32,
    )
    act_zero = jax.nn.silu(pre_spatial).astype(jnp.bfloat16).reshape(local_frames, pixels, chans)
    cot_local = cotangent.reshape(local_frames, pixels, chans)
    act_blocks = fm_to_pixels(act_zero)
    act_blocks, cot_local = lax.optimization_barrier((act_blocks, cot_local))
    cot_blocks = fm_to_pixels(cot_local)
    acts = [act_blocks]
    total_frames, width = act_blocks.shape[0], act_blocks.shape[1]
    seg_frames = total_frames // seg_count
    pres = []
    for layer in range(LAYERS):
        pre, act = temporal_forward_k(acts[-1], temporal_weight[layer], dilation[layer])
        pres.append(pre)
        acts.append(act)
    feat = acts[-1]
    seg_shape = (seg_count, seg_frames, width, chans)
    feat_seg = feat.reshape(seg_shape)
    positions = jnp.arange(seg_frames, dtype=jnp.int32)
    onehot = positions[None, :] == key_index[:, None]
    keys = jnp.einsum(
        "ns,nsjc->njc", onehot.astype(jnp.bfloat16), feat_seg, preferred_element_type=jnp.float32
    ).astype(jnp.bfloat16)
    key_full = jnp.broadcast_to(keys[:, None], seg_shape).reshape(-1, chans)
    feat_flat = feat.reshape(-1, chans)
    key_part = jnp.dot(
        keys.reshape(-1, chans), uniting_weight[1], preferred_element_type=jnp.float32
    ).reshape(seg_count, 1, width, chans)
    main_part = jnp.dot(feat_flat, uniting_weight[0], preferred_element_type=jnp.float32)
    united_blocks = (main_part.reshape(seg_shape) + key_part).astype(jnp.bfloat16)
    united = fm_to_frames(united_blocks.reshape(total_frames, width, chans), used)
    cot_flat = cot_blocks.reshape(-1, chans)
    grad_feat = jnp.dot(cot_flat, uniting_weight[0].T, preferred_element_type=jnp.float32)
    seg_cot = jnp.sum(cot_blocks.reshape(seg_shape).astype(jnp.float32), axis=1)
    key_term = jnp.dot(
        seg_cot.reshape(-1, chans),
        uniting_weight[1].T.astype(jnp.float32),
        precision=lax.Precision.HIGHEST,
    ).reshape(seg_count, 1, width, chans)
    placed = onehot.astype(jnp.float32)[:, :, None, None] * key_term
    grad_feat = grad_feat.reshape(seg_shape) + placed
    grad_feat = grad_feat.reshape(total_frames, width, chans)
    grad_uniting = jnp.stack([inner(feat_flat, cot_flat), inner(key_full, cot_flat)])
    grad_pre = (grad_feat * silu_grad(pres[-1])).astype(jnp.bfloat16)
    tgrads = [None] * LAYERS
    layer_grads = [None] * LAYERS
    for layer in range(LAYERS - 1, -1, -1):
        below = pres[layer - 1] if layer > 0 else None
        layer_grads[layer] = grad_pre
        grad_pre = temporal_backward_k(
            acts[layer], grad_pre, temporal_weight[layer], dilation[layer], below
        )
    grad_act0 = grad_pre
    grad_time = fm_to_frames(grad_act0, used).reshape(frames_in.shape)
    for layer in range(LAYERS):
        tgrads[layer] = temporal_wgrad_k(acts[layer], layer_grads[layer], dilation[layer])
    grad_spre = (grad_time.astype(jnp.float32) * silu_grad(pre_spatial)).astype(jnp.bfloat16)
    grad_frames = spatial_back(grad_spre, spatial_weight).astype(jnp.bfloat16)
    grad_spatial = spatial_wgrad(frames_in, grad_spre)
    scale = 1.0 / jnp.sqrt(jnp.float32(total_frames * pixels))
    summed = all_sum((grad_spatial, jnp.stack(tgrads), grad_uniting), scale)
    return (
        united.reshape(frames_in.shape),
        grad_frames,
        summed[0],
        summed[1],
        summed[2],
    )


def solution(mesh):
    placed = (
        P(("seg", "grp"), None, None, None),
        P(),
        P(),
        P(),
        P(),
        P(),
        P(("seg", "grp"), None, None, None),
    )
    return jax.shard_map(
        local,
        mesh=mesh,
        in_specs=placed,
        out_specs=(
            P(("seg", "grp"), None, None, None),
            P(("seg", "grp"), None, None, None),
            P(),
            P(),
            P(),
        ),
        check_vma=False,
    )
```

```python
import functools

import jax
import jax.numpy as jnp
from jax import lax
from jax.sharding import PartitionSpec as P
from jax.experimental import pallas as pl
from jax.experimental.pallas import tpu as pltpu

LAYERS = 2
DMAX = 8


def from_root(value, axis, root):
    mine = lax.axis_index(axis) == root
    return lax.psum(jnp.where(mine, value, jnp.zeros_like(value)), axis)


def silu_grad(value):
    sigma = jax.nn.sigmoid(value)
    return sigma * (1.0 + value * (1.0 - sigma))


def inner(left, right):
    return lax.dot_general(
        left, right, (((0,), (0,)), ((), ())), preferred_element_type=jnp.float32
    )


def spatial_forward(frames, kernel):
    count, rows, cols, chans = frames.shape
    padded = jnp.pad(frames, ((0, 0), (1, 1), (1, 1), (0, 0)))
    total = jnp.zeros((count * rows * cols, chans), jnp.float32)
    for row_tap in range(3):
        for col_tap in range(3):
            piece = padded[:, row_tap : row_tap + rows, col_tap : col_tap + cols, :].reshape(
                -1, chans
            )
            total = total + jnp.dot(
                piece, kernel[3 * row_tap + col_tap], preferred_element_type=jnp.float32
            )
    return total.reshape(frames.shape)


def spatial_back(grads, kernel):
    count, rows, cols, chans = grads.shape
    padded = jnp.pad(grads, ((0, 0), (1, 1), (1, 1), (0, 0)))
    total = jnp.zeros((count * rows * cols, chans), jnp.float32)
    for row_tap in range(3):
        for col_tap in range(3):
            piece = padded[
                :, 2 - row_tap : 2 - row_tap + rows, 2 - col_tap : 2 - col_tap + cols, :
            ].reshape(-1, chans)
            total = total + jnp.dot(
                piece, kernel[3 * row_tap + col_tap].T, preferred_element_type=jnp.float32
            )
    return total.reshape(grads.shape)


def spatial_wgrad(frames, grads):
    count, rows, cols, chans = frames.shape
    padded = jnp.pad(frames, ((0, 0), (1, 1), (1, 1), (0, 0)))
    flat_grads = grads.reshape(-1, chans)
    result = []
    for row_tap in range(3):
        for col_tap in range(3):
            piece = padded[:, row_tap : row_tap + rows, col_tap : col_tap + cols, :].reshape(
                -1, chans
            )
            result.append(inner(piece, flat_grads))
    return jnp.stack(result)


def shifted(values, offset):
    padded = jnp.pad(values, ((2 * DMAX, 2 * DMAX), (0, 0), (0, 0)))
    start = 2 * DMAX + offset
    return lax.dynamic_slice_in_dim(padded, start, values.shape[0], 0)


def temporal_forward(acts, kernel, step_size):
    chans = acts.shape[2]
    total = jnp.zeros((acts.shape[0] * acts.shape[1], chans), jnp.float32)
    for tap in range(5):
        piece = shifted(acts, (tap - 2) * step_size).reshape(-1, chans)
        total = total + jnp.dot(piece, kernel[tap], preferred_element_type=jnp.float32)
    return total.reshape(acts.shape)


def temporal_back(grads, kernel, step_size):
    chans = grads.shape[2]
    total = jnp.zeros((grads.shape[0] * grads.shape[1], chans), jnp.float32)
    for tap in range(5):
        piece = shifted(grads, (2 - tap) * step_size).reshape(-1, chans)
        total = total + jnp.dot(piece, kernel[tap].T, preferred_element_type=jnp.float32)
    return total.reshape(grads.shape)


def temporal_wgrad(acts, grads, step_size):
    chans = acts.shape[2]
    flat_grads = grads.reshape(-1, chans)
    return jnp.stack(
        [
            inner(shifted(acts, (tap - 2) * step_size).reshape(-1, chans), flat_grads)
            for tap in range(5)
        ]
    )


def to_pixels(flat):
    count = lax.axis_size(("seg", "grp"))
    chans = flat.shape[-1]
    strided = flat.reshape(-1, count, chans)
    return lax.all_to_all(strided, ("seg", "grp"), split_axis=1, concat_axis=1, tiled=True)


def to_frames(blocks):
    out = lax.all_to_all(blocks, ("seg", "grp"), split_axis=1, concat_axis=1, tiled=True)
    return out.reshape(1, -1, blocks.shape[-1])


def shifted1(values, offset):
    padded = jnp.pad(values, ((0, 0), (2 * DMAX, 2 * DMAX), (0, 0)))
    start = 2 * DMAX + offset
    return lax.dynamic_slice_in_dim(padded, start, values.shape[1], 1)


def temporal_forward1(acts, kernel, step_size):
    chans = acts.shape[2]
    total = jnp.zeros((acts.shape[0] * acts.shape[1], chans), jnp.float32)
    for tap in range(5):
        piece = shifted1(acts, (tap - 2) * step_size).reshape(-1, chans)
        total = total + jnp.dot(piece, kernel[tap], preferred_element_type=jnp.float32)
    return total.reshape(acts.shape)


def temporal_back1(grads, kernel, step_size):
    chans = grads.shape[2]
    total = jnp.zeros((grads.shape[0] * grads.shape[1], chans), jnp.float32)
    for tap in range(5):
        piece = shifted1(grads, (2 - tap) * step_size).reshape(-1, chans)
        total = total + jnp.dot(piece, kernel[tap].T, preferred_element_type=jnp.float32)
    return total.reshape(grads.shape)


def temporal_wgrad1(acts, grads, step_size):
    chans = acts.shape[2]
    flat_grads = grads.reshape(-1, chans)
    return jnp.stack(
        [
            inner(shifted1(acts, (tap - 2) * step_size).reshape(-1, chans), flat_grads)
            for tap in range(5)
        ]
    )


HALO = 2 * DMAX
FB = 32


def fm_to_pixels(flat):
    count = lax.axis_size(("seg", "grp"))
    chans = flat.shape[-1]
    strided = flat.reshape(-1, count, chans)
    rows = -(-strided.shape[0] // 16) * 16
    strided = jnp.pad(strided, ((0, rows - strided.shape[0]), (0, 0), (0, 0)))
    out = lax.all_to_all(strided, ("seg", "grp"), split_axis=1, concat_axis=1, tiled=True)
    return jnp.transpose(out, (1, 0, 2))


def fm_to_frames(blocks, used):
    moved = jnp.transpose(blocks, (1, 0, 2))
    out = lax.all_to_all(moved, ("seg", "grp"), split_axis=1, concat_axis=1, tiled=True)
    return out[:used].reshape(1, -1, blocks.shape[-1])


def fill_halo(src_ref, pad_ref):
    frames = src_ref.shape[0]
    zeros = jnp.zeros((HALO,) + pad_ref.shape[1:], pad_ref.dtype)
    pad_ref[0:HALO] = zeros
    pad_ref[HALO + frames : 2 * HALO + frames] = zeros
    pad_ref[HALO : HALO + frames] = src_ref[...]


def tap_rows(pad_ref, start, rows):
    return pad_ref[pl.ds(start, FB)].reshape(rows, pad_ref.shape[-1])


def tfwd_kernel(dil_ref, act_ref, w_ref, pre_ref, out_ref, pad_ref):
    frames, width, chans = act_ref.shape
    fill_halo(act_ref, pad_ref)
    step = dil_ref[0]
    rows = FB * width
    for block in range(frames // FB):
        base = HALO + block * FB
        stacked = jnp.concatenate(
            [tap_rows(pad_ref, base + (tap - 2) * step, rows) for tap in range(5)], axis=1
        )
        pre = jnp.dot(stacked, w_ref[...], preferred_element_type=jnp.float32)
        pre_ref[block * FB : (block + 1) * FB] = pre.reshape(FB, width, chans)
        out_ref[block * FB : (block + 1) * FB] = (
            (pre / (1.0 + jnp.exp(-pre))).astype(jnp.bfloat16).reshape(FB, width, chans)
        )


def temporal_forward_k(acts, kernel, step_size):
    frames, width, chans = acts.shape
    return pl.pallas_call(
        tfwd_kernel,
        grid_spec=pltpu.PrefetchScalarGridSpec(
            num_scalar_prefetch=1,
            grid=(1,),
            in_specs=[
                pl.BlockSpec(acts.shape, lambda i, d: (0, 0, 0)),
                pl.BlockSpec((5 * chans, chans), lambda i, d: (0, 0)),
            ],
            out_specs=[
                pl.BlockSpec(acts.shape, lambda i, d: (0, 0, 0)),
                pl.BlockSpec(acts.shape, lambda i, d: (0, 0, 0)),
            ],
            scratch_shapes=[pltpu.VMEM((frames + 2 * HALO, width, chans), jnp.bfloat16)],
        ),
        out_shape=[
            jax.ShapeDtypeStruct(acts.shape, jnp.float32),
            jax.ShapeDtypeStruct(acts.shape, jnp.bfloat16),
        ],
        cost_estimate=pl.CostEstimate(
            flops=2 * frames * width * chans * chans * 5,
            transcendentals=frames * width * chans,
            bytes_accessed=frames * width * chans * 8,
        ),
    )(step_size.reshape(1), acts, kernel.reshape(5 * chans, chans))


def tbwd_kernel(with_pre, dil_ref, act_ref, grad_ref, wt_ref, *rest):
    if with_pre:
        pre_ref, out_ref, pad_ref = rest
    else:
        out_ref, pad_ref = rest
    frames, width, chans = act_ref.shape
    fill_halo(grad_ref, pad_ref)
    step = dil_ref[0]
    rows = FB * width
    for block in range(frames // FB):
        base = HALO + block * FB
        stacked = jnp.concatenate(
            [tap_rows(pad_ref, base - (tap - 2) * step, rows) for tap in range(5)], axis=1
        )
        grad_act = None
        for tap in range(5):
            term = lax.dot_general(
                stacked[:, tap * chans : (tap + 1) * chans],
                wt_ref[tap * chans : (tap + 1) * chans, :],
                (((1,), (1,)), ((), ())),
                preferred_element_type=jnp.float32,
            )
            grad_act = term if grad_act is None else grad_act + term
        if with_pre:
            pre = pre_ref[block * FB : (block + 1) * FB].reshape(rows, chans)
            sigma = 1.0 / (1.0 + jnp.exp(-pre))
            grad_act = grad_act * (sigma * (1.0 + pre * (1.0 - sigma)))
        out_ref[block * FB : (block + 1) * FB] = (
            grad_act.astype(jnp.bfloat16).reshape(FB, width, chans)
        )


def twgrad_kernel(dil_ref, act0_ref, act1_ref, grad0_ref, grad1_ref, tg_ref, pad_ref):
    frames, width, chans = act0_ref.shape
    rows = FB * width
    for layer, (act_ref, grad_ref) in enumerate(((act0_ref, grad0_ref), (act1_ref, grad1_ref))):
        fill_halo(grad_ref, pad_ref)
        step = dil_ref[layer]
        total = None
        for block in range(frames // FB):
            base = HALO + block * FB
            stacked = jnp.concatenate(
                [tap_rows(pad_ref, base - (tap - 2) * step, rows) for tap in range(5)], axis=1
            )
            flat_act = act_ref[block * FB : (block + 1) * FB].reshape(rows, chans)
            part = lax.dot_general(
                flat_act, stacked, (((0,), (0,)), ((), ())), preferred_element_type=jnp.float32
            )
            total = part if total is None else total + part
        for tap in range(5):
            tg_ref[layer, tap] = total[:, tap * chans : (tap + 1) * chans]


def temporal_wgrad_k(acts, grads, dilation):
    frames, width, chans = acts[0].shape
    full = pl.BlockSpec(acts[0].shape, lambda i, d: (0, 0, 0))
    return pl.pallas_call(
        twgrad_kernel,
        grid_spec=pltpu.PrefetchScalarGridSpec(
            num_scalar_prefetch=1,
            grid=(1,),
            in_specs=[full, full, full, full],
            out_specs=pl.BlockSpec((2, 5, chans, chans), lambda i, d: (0, 0, 0, 0)),
            scratch_shapes=[pltpu.VMEM((frames + 2 * HALO, width, chans), jnp.bfloat16)],
        ),
        out_shape=jax.ShapeDtypeStruct((2, 5, chans, chans), jnp.float32),
        cost_estimate=pl.CostEstimate(
            flops=2 * 2 * frames * width * chans * chans * 5,
            transcendentals=0,
            bytes_accessed=2 * frames * width * chans * 4,
        ),
    )(dilation, acts[0], acts[1], grads[0], grads[1])


def temporal_backward_k(acts, grads, kernel, step_size, pre_below):
    frames, width, chans = acts.shape
    full = pl.BlockSpec(acts.shape, lambda i, d: (0, 0, 0))
    with_pre = pre_below is not None
    in_specs = [full, full, pl.BlockSpec((5 * chans, chans), lambda i, d: (0, 0))]
    operands = [step_size.reshape(1), acts, grads, kernel.reshape(5 * chans, chans)]
    if with_pre:
        in_specs.append(full)
        operands.append(pre_below)
    return pl.pallas_call(
        functools.partial(tbwd_kernel, with_pre),
        grid_spec=pltpu.PrefetchScalarGridSpec(
            num_scalar_prefetch=1,
            grid=(1,),
            in_specs=in_specs,
            out_specs=full,
            scratch_shapes=[pltpu.VMEM((frames + 2 * HALO, width, chans), jnp.bfloat16)],
        ),
        out_shape=jax.ShapeDtypeStruct(acts.shape, jnp.bfloat16),
        cost_estimate=pl.CostEstimate(
            flops=2 * frames * width * chans * chans * 5,
            transcendentals=frames * width * chans,
            bytes_accessed=frames * width * chans * 10,
        ),
    )(*operands)


def all_sum(parts, scale):
    chans = parts[0].shape[-1]
    count = lax.axis_size(("seg", "grp"))
    rows = [p.reshape(-1, chans) for p in parts]
    used = sum(r.shape[0] for r in rows)
    per = -(-used // (count * 8)) * 8
    rows.append(jnp.zeros((per * count - used, chans), jnp.float32))
    stack = jnp.concatenate(rows, axis=0).reshape(count, per, chans)
    pieces = lax.all_to_all(stack, ("seg", "grp"), split_axis=0, concat_axis=0, tiled=True)
    mine = (jnp.sum(pieces, axis=0, keepdims=True) * scale).astype(jnp.bfloat16)
    spread = jnp.broadcast_to(mine, stack.shape)
    whole = lax.all_to_all(spread, ("seg", "grp"), split_axis=0, concat_axis=0, tiled=True)
    whole = whole.astype(jnp.float32).reshape(-1, chans)
    out = []
    offset = 0
    for p in parts:
        size = p.size // chans
        out.append(whole[offset : offset + size].reshape(p.shape))
        offset += size
    return out


def local(
    frames_in, spatial_weight, temporal_weight, uniting_weight, key_index, dilation, cotangent
):
    local_frames, rows, cols, chans = frames_in.shape
    pixels = rows * cols
    seg_count = lax.axis_size("seg")
    count = lax.axis_size(("seg", "grp"))
    used = pixels // count
    pre_spatial = spatial_forward(frames_in, spatial_weight)
    act_zero = jax.nn.silu(pre_spatial).astype(jnp.bfloat16).reshape(local_frames, pixels, chans)
    cot_local = cotangent.reshape(local_frames, pixels, chans)
    act_blocks = fm_to_pixels(act_zero)
    act_blocks, cot_local = lax.optimization_barrier((act_blocks, cot_local))
    cot_blocks = fm_to_pixels(cot_local)
    acts = [act_blocks]
    total_frames, width = act_blocks.shape[0], act_blocks.shape[1]
    seg_frames = total_frames // seg_count
    pres = []
    for layer in range(LAYERS):
        pre, act = temporal_forward_k(acts[-1], temporal_weight[layer], dilation[layer])
        pres.append(pre)
        acts.append(act)
    feat = acts[-1]
    seg_shape = (seg_count, seg_frames, width, chans)
    feat_seg = feat.reshape(seg_shape)
    positions = jnp.arange(seg_frames, dtype=jnp.int32)
    onehot = positions[None, :] == key_index[:, None]
    keys = jnp.einsum(
        "ns,nsjc->njc", onehot.astype(jnp.bfloat16), feat_seg, preferred_element_type=jnp.float32
    ).astype(jnp.bfloat16)
    key_full = jnp.broadcast_to(keys[:, None], seg_shape).reshape(-1, chans)
    feat_flat = feat.reshape(-1, chans)
    key_part = jnp.dot(
        keys.reshape(-1, chans), uniting_weight[1], preferred_element_type=jnp.float32
    ).reshape(seg_count, 1, width, chans)
    main_part = jnp.dot(feat_flat, uniting_weight[0], preferred_element_type=jnp.float32)
    united_blocks = (main_part.reshape(seg_shape) + key_part).astype(jnp.bfloat16)
    united = fm_to_frames(united_blocks.reshape(total_frames, width, chans), used)
    cot_flat = cot_blocks.reshape(-1, chans)
    grad_feat = jnp.dot(cot_flat, uniting_weight[0].T, preferred_element_type=jnp.float32)
    seg_cot = jnp.sum(cot_blocks.reshape(seg_shape).astype(jnp.float32), axis=1)
    key_term = jnp.dot(
        seg_cot.reshape(-1, chans),
        uniting_weight[1].T.astype(jnp.float32),
        precision=lax.Precision.HIGHEST,
    ).reshape(seg_count, 1, width, chans)
    placed = onehot.astype(jnp.float32)[:, :, None, None] * key_term
    grad_feat = grad_feat.reshape(seg_shape) + placed
    grad_feat = grad_feat.reshape(total_frames, width, chans)
    grad_uniting = jnp.stack([inner(feat_flat, cot_flat), inner(key_full, cot_flat)])
    grad_pre = (grad_feat * silu_grad(pres[-1])).astype(jnp.bfloat16)
    tgrads = [None] * LAYERS
    layer_grads = [None] * LAYERS
    for layer in range(LAYERS - 1, -1, -1):
        below = pres[layer - 1] if layer > 0 else None
        layer_grads[layer] = grad_pre
        grad_pre = temporal_backward_k(
            acts[layer], grad_pre, temporal_weight[layer], dilation[layer], below
        )
    grad_act0 = grad_pre
    grad_time = fm_to_frames(grad_act0, used).reshape(frames_in.shape)
    tgrad_all = temporal_wgrad_k(acts[:LAYERS], layer_grads, dilation)
    grad_spre = (grad_time.astype(jnp.float32) * silu_grad(pre_spatial)).astype(jnp.bfloat16)
    grad_frames = spatial_back(grad_spre, spatial_weight).astype(jnp.bfloat16)
    grad_spatial = spatial_wgrad(frames_in, grad_spre)
    scale = 1.0 / jnp.sqrt(jnp.float32(total_frames * pixels))
    summed = all_sum((grad_spatial, tgrad_all, grad_uniting), scale)
    return (
        united.reshape(frames_in.shape),
        grad_frames,
        summed[0],
        summed[1],
        summed[2],
    )


def solution(mesh):
    placed = (
        P(("seg", "grp"), None, None, None),
        P(),
        P(),
        P(),
        P(),
        P(),
        P(("seg", "grp"), None, None, None),
    )
    return jax.shard_map(
        local,
        mesh=mesh,
        in_specs=placed,
        out_specs=(
            P(("seg", "grp"), None, None, None),
            P(("seg", "grp"), None, None, None),
            P(),
            P(),
            P(),
        ),
        check_vma=False,
    )
```

```python
import functools

import jax
import jax.numpy as jnp
from jax import lax
from jax.sharding import PartitionSpec as P
from jax.experimental import pallas as pl
from jax.experimental.pallas import tpu as pltpu

LAYERS = 2
DMAX = 8


def from_root(value, axis, root):
    mine = lax.axis_index(axis) == root
    return lax.psum(jnp.where(mine, value, jnp.zeros_like(value)), axis)


def silu_grad(value):
    sigma = jax.nn.sigmoid(value)
    return sigma * (1.0 + value * (1.0 - sigma))


def inner(left, right):
    return lax.dot_general(
        left, right, (((0,), (0,)), ((), ())), preferred_element_type=jnp.float32
    )


def spatial_forward(frames, kernel):
    count, rows, cols, chans = frames.shape
    padded = jnp.pad(frames, ((0, 0), (1, 1), (1, 1), (0, 0)))
    total = jnp.zeros((count * rows * cols, chans), jnp.float32)
    for row_tap in range(3):
        for col_tap in range(3):
            piece = padded[:, row_tap : row_tap + rows, col_tap : col_tap + cols, :].reshape(
                -1, chans
            )
            total = total + jnp.dot(
                piece, kernel[3 * row_tap + col_tap], preferred_element_type=jnp.float32
            )
    return total.reshape(frames.shape)


def spatial_back(grads, kernel):
    count, rows, cols, chans = grads.shape
    padded = jnp.pad(grads, ((0, 0), (1, 1), (1, 1), (0, 0)))
    total = jnp.zeros((count * rows * cols, chans), jnp.float32)
    for row_tap in range(3):
        for col_tap in range(3):
            piece = padded[
                :, 2 - row_tap : 2 - row_tap + rows, 2 - col_tap : 2 - col_tap + cols, :
            ].reshape(-1, chans)
            total = total + jnp.dot(
                piece, kernel[3 * row_tap + col_tap].T, preferred_element_type=jnp.float32
            )
    return total.reshape(grads.shape)


def spatial_wgrad(frames, grads):
    count, rows, cols, chans = frames.shape
    padded = jnp.pad(frames, ((0, 0), (1, 1), (1, 1), (0, 0)))
    flat_grads = grads.reshape(-1, chans)
    result = []
    for row_tap in range(3):
        for col_tap in range(3):
            piece = padded[:, row_tap : row_tap + rows, col_tap : col_tap + cols, :].reshape(
                -1, chans
            )
            result.append(inner(piece, flat_grads))
    return jnp.stack(result)


def shifted(values, offset):
    padded = jnp.pad(values, ((2 * DMAX, 2 * DMAX), (0, 0), (0, 0)))
    start = 2 * DMAX + offset
    return lax.dynamic_slice_in_dim(padded, start, values.shape[0], 0)


def temporal_forward(acts, kernel, step_size):
    chans = acts.shape[2]
    total = jnp.zeros((acts.shape[0] * acts.shape[1], chans), jnp.float32)
    for tap in range(5):
        piece = shifted(acts, (tap - 2) * step_size).reshape(-1, chans)
        total = total + jnp.dot(piece, kernel[tap], preferred_element_type=jnp.float32)
    return total.reshape(acts.shape)


def temporal_back(grads, kernel, step_size):
    chans = grads.shape[2]
    total = jnp.zeros((grads.shape[0] * grads.shape[1], chans), jnp.float32)
    for tap in range(5):
        piece = shifted(grads, (2 - tap) * step_size).reshape(-1, chans)
        total = total + jnp.dot(piece, kernel[tap].T, preferred_element_type=jnp.float32)
    return total.reshape(grads.shape)


def temporal_wgrad(acts, grads, step_size):
    chans = acts.shape[2]
    flat_grads = grads.reshape(-1, chans)
    return jnp.stack(
        [
            inner(shifted(acts, (tap - 2) * step_size).reshape(-1, chans), flat_grads)
            for tap in range(5)
        ]
    )


def to_pixels(flat):
    count = lax.axis_size(("seg", "grp"))
    chans = flat.shape[-1]
    strided = flat.reshape(-1, count, chans)
    return lax.all_to_all(strided, ("seg", "grp"), split_axis=1, concat_axis=1, tiled=True)


def to_frames(blocks):
    out = lax.all_to_all(blocks, ("seg", "grp"), split_axis=1, concat_axis=1, tiled=True)
    return out.reshape(1, -1, blocks.shape[-1])


def shifted1(values, offset):
    padded = jnp.pad(values, ((0, 0), (2 * DMAX, 2 * DMAX), (0, 0)))
    start = 2 * DMAX + offset
    return lax.dynamic_slice_in_dim(padded, start, values.shape[1], 1)


def temporal_forward1(acts, kernel, step_size):
    chans = acts.shape[2]
    total = jnp.zeros((acts.shape[0] * acts.shape[1], chans), jnp.float32)
    for tap in range(5):
        piece = shifted1(acts, (tap - 2) * step_size).reshape(-1, chans)
        total = total + jnp.dot(piece, kernel[tap], preferred_element_type=jnp.float32)
    return total.reshape(acts.shape)


def temporal_back1(grads, kernel, step_size):
    chans = grads.shape[2]
    total = jnp.zeros((grads.shape[0] * grads.shape[1], chans), jnp.float32)
    for tap in range(5):
        piece = shifted1(grads, (2 - tap) * step_size).reshape(-1, chans)
        total = total + jnp.dot(piece, kernel[tap].T, preferred_element_type=jnp.float32)
    return total.reshape(grads.shape)


def temporal_wgrad1(acts, grads, step_size):
    chans = acts.shape[2]
    flat_grads = grads.reshape(-1, chans)
    return jnp.stack(
        [
            inner(shifted1(acts, (tap - 2) * step_size).reshape(-1, chans), flat_grads)
            for tap in range(5)
        ]
    )


HALO = 2 * DMAX
FB = 32


def fm_to_pixels(flat):
    count = lax.axis_size(("seg", "grp"))
    chans = flat.shape[-1]
    strided = flat.reshape(-1, count, chans)
    rows = -(-strided.shape[0] // 16) * 16
    strided = jnp.pad(strided, ((0, rows - strided.shape[0]), (0, 0), (0, 0)))
    out = lax.all_to_all(strided, ("seg", "grp"), split_axis=1, concat_axis=1, tiled=True)
    return jnp.transpose(out, (1, 0, 2))


def fm_to_frames(blocks, used):
    moved = jnp.transpose(blocks, (1, 0, 2))
    out = lax.all_to_all(moved, ("seg", "grp"), split_axis=1, concat_axis=1, tiled=True)
    return out[:used].reshape(1, -1, blocks.shape[-1])


def fill_halo(src_ref, pad_ref):
    frames = src_ref.shape[0]
    zeros = jnp.zeros((HALO,) + pad_ref.shape[1:], pad_ref.dtype)
    pad_ref[0:HALO] = zeros
    pad_ref[HALO + frames : 2 * HALO + frames] = zeros
    pad_ref[HALO : HALO + frames] = src_ref[...]


def tap_rows(pad_ref, start, rows):
    return pad_ref[pl.ds(start, FB)].reshape(rows, pad_ref.shape[-1])


def tfwd_kernel(dil_ref, act_ref, w_ref, pre_ref, out_ref, pad_ref):
    frames, width, chans = act_ref.shape
    fill_halo(act_ref, pad_ref)
    step = dil_ref[0]
    rows = FB * width
    for block in range(frames // FB):
        base = HALO + block * FB
        stacked = jnp.concatenate(
            [tap_rows(pad_ref, base + (tap - 2) * step, rows) for tap in range(5)], axis=1
        )
        pre = jnp.dot(stacked, w_ref[...], preferred_element_type=jnp.float32)
        pre_ref[block * FB : (block + 1) * FB] = pre.reshape(FB, width, chans)
        out_ref[block * FB : (block + 1) * FB] = (
            (pre / (1.0 + jnp.exp(-pre))).astype(jnp.bfloat16).reshape(FB, width, chans)
        )


def temporal_forward_k(acts, kernel, step_size):
    frames, width, chans = acts.shape
    return pl.pallas_call(
        tfwd_kernel,
        grid_spec=pltpu.PrefetchScalarGridSpec(
            num_scalar_prefetch=1,
            grid=(1,),
            in_specs=[
                pl.BlockSpec(acts.shape, lambda i, d: (0, 0, 0)),
                pl.BlockSpec((5 * chans, chans), lambda i, d: (0, 0)),
            ],
            out_specs=[
                pl.BlockSpec(acts.shape, lambda i, d: (0, 0, 0)),
                pl.BlockSpec(acts.shape, lambda i, d: (0, 0, 0)),
            ],
            scratch_shapes=[pltpu.VMEM((frames + 2 * HALO, width, chans), jnp.bfloat16)],
        ),
        out_shape=[
            jax.ShapeDtypeStruct(acts.shape, jnp.float32),
            jax.ShapeDtypeStruct(acts.shape, jnp.bfloat16),
        ],
        cost_estimate=pl.CostEstimate(
            flops=2 * frames * width * chans * chans * 5,
            transcendentals=frames * width * chans,
            bytes_accessed=frames * width * chans * 8,
        ),
    )(step_size.reshape(1), acts, kernel.reshape(5 * chans, chans))


def tbwd_kernel(with_pre, dil_ref, act_ref, grad_ref, wt_ref, *rest):
    if with_pre:
        pre_ref, out_ref, pad_ref = rest
    else:
        out_ref, pad_ref = rest
    frames, width, chans = act_ref.shape
    fill_halo(grad_ref, pad_ref)
    step = dil_ref[0]
    rows = FB * width
    for block in range(frames // FB):
        base = HALO + block * FB
        stacked = jnp.concatenate(
            [tap_rows(pad_ref, base - (tap - 2) * step, rows) for tap in range(5)], axis=1
        )
        grad_act = None
        for tap in range(5):
            term = lax.dot_general(
                stacked[:, tap * chans : (tap + 1) * chans],
                wt_ref[tap * chans : (tap + 1) * chans, :],
                (((1,), (1,)), ((), ())),
                preferred_element_type=jnp.float32,
            )
            grad_act = term if grad_act is None else grad_act + term
        if with_pre:
            pre = pre_ref[block * FB : (block + 1) * FB].reshape(rows, chans)
            sigma = 1.0 / (1.0 + jnp.exp(-pre))
            grad_act = grad_act * (sigma * (1.0 + pre * (1.0 - sigma)))
        out_ref[block * FB : (block + 1) * FB] = (
            grad_act.astype(jnp.bfloat16).reshape(FB, width, chans)
        )


def twgrad_kernel(dil_ref, act_ref, grad_ref, tg_ref, pad_ref):
    frames, width, chans = act_ref.shape
    fill_halo(grad_ref, pad_ref)
    step = dil_ref[0]
    rows = FB * width
    total = None
    for block in range(frames // FB):
        base = HALO + block * FB
        stacked = jnp.concatenate(
            [tap_rows(pad_ref, base - (tap - 2) * step, rows) for tap in range(5)], axis=1
        )
        flat_act = act_ref[block * FB : (block + 1) * FB].reshape(rows, chans)
        part = lax.dot_general(
            flat_act, stacked, (((0,), (0,)), ((), ())), preferred_element_type=jnp.float32
        )
        total = part if total is None else total + part
    for tap in range(5):
        tg_ref[tap] = total[:, tap * chans : (tap + 1) * chans]


def temporal_wgrad_k(acts, grads, step_size):
    frames, width, chans = acts.shape
    full = pl.BlockSpec(acts.shape, lambda i, d: (0, 0, 0))
    return pl.pallas_call(
        twgrad_kernel,
        grid_spec=pltpu.PrefetchScalarGridSpec(
            num_scalar_prefetch=1,
            grid=(1,),
            in_specs=[full, full],
            out_specs=pl.BlockSpec((5, chans, chans), lambda i, d: (0, 0, 0)),
            scratch_shapes=[pltpu.VMEM((frames + 2 * HALO, width, chans), jnp.bfloat16)],
        ),
        out_shape=jax.ShapeDtypeStruct((5, chans, chans), jnp.float32),
        cost_estimate=pl.CostEstimate(
            flops=2 * frames * width * chans * chans * 5,
            transcendentals=0,
            bytes_accessed=frames * width * chans * 4,
        ),
    )(step_size.reshape(1), acts, grads)


def temporal_backward_k(acts, grads, kernel, step_size, pre_below):
    frames, width, chans = acts.shape
    full = pl.BlockSpec(acts.shape, lambda i, d: (0, 0, 0))
    with_pre = pre_below is not None
    in_specs = [full, full, pl.BlockSpec((5 * chans, chans), lambda i, d: (0, 0))]
    operands = [step_size.reshape(1), acts, grads, kernel.reshape(5 * chans, chans)]
    if with_pre:
        in_specs.append(full)
        operands.append(pre_below)
    return pl.pallas_call(
        functools.partial(tbwd_kernel, with_pre),
        grid_spec=pltpu.PrefetchScalarGridSpec(
            num_scalar_prefetch=1,
            grid=(1,),
            in_specs=in_specs,
            out_specs=full,
            scratch_shapes=[pltpu.VMEM((frames + 2 * HALO, width, chans), jnp.bfloat16)],
        ),
        out_shape=jax.ShapeDtypeStruct(acts.shape, jnp.bfloat16),
        cost_estimate=pl.CostEstimate(
            flops=2 * frames * width * chans * chans * 5,
            transcendentals=frames * width * chans,
            bytes_accessed=frames * width * chans * 10,
        ),
    )(*operands)


def all_sum(parts, scale):
    chans = parts[0].shape[-1]
    count = lax.axis_size(("seg", "grp"))
    rows = [p.reshape(-1, chans) for p in parts]
    used = sum(r.shape[0] for r in rows)
    per = -(-used // (count * 8)) * 8
    rows.append(jnp.zeros((per * count - used, chans), jnp.float32))
    stack = jnp.concatenate(rows, axis=0).reshape(count, per, chans)
    pieces = lax.all_to_all(stack, ("seg", "grp"), split_axis=0, concat_axis=0, tiled=True)
    mine = (jnp.sum(pieces, axis=0, keepdims=True) * scale).astype(jnp.bfloat16)
    spread = jnp.broadcast_to(mine, stack.shape)
    whole = lax.all_to_all(spread, ("seg", "grp"), split_axis=0, concat_axis=0, tiled=True)
    whole = whole.astype(jnp.float32).reshape(-1, chans)
    out = []
    offset = 0
    for p in parts:
        size = p.size // chans
        out.append(whole[offset : offset + size].reshape(p.shape))
        offset += size
    return out


def local(
    frames_in, spatial_weight, temporal_weight, uniting_weight, key_index, dilation, cotangent
):
    local_frames, rows, cols, chans = frames_in.shape
    pixels = rows * cols
    seg_count = lax.axis_size("seg")
    count = lax.axis_size(("seg", "grp"))
    used = pixels // count
    pre_spatial = spatial_forward(frames_in, spatial_weight)
    act_zero = jax.nn.silu(pre_spatial).astype(jnp.bfloat16).reshape(local_frames, pixels, chans)
    cot_local = cotangent.reshape(local_frames, pixels, chans)
    act_blocks = fm_to_pixels(act_zero)
    spatial_slope = silu_grad(pre_spatial)
    act_blocks, cot_local, spatial_slope = lax.optimization_barrier(
        (act_blocks, cot_local, spatial_slope)
    )
    cot_blocks = fm_to_pixels(cot_local)
    acts = [act_blocks]
    total_frames, width = act_blocks.shape[0], act_blocks.shape[1]
    seg_frames = total_frames // seg_count
    pres = []
    for layer in range(LAYERS):
        pre, act = temporal_forward_k(acts[-1], temporal_weight[layer], dilation[layer])
        pres.append(pre)
        acts.append(act)
    feat = acts[-1]
    seg_shape = (seg_count, seg_frames, width, chans)
    feat_seg = feat.reshape(seg_shape)
    positions = jnp.arange(seg_frames, dtype=jnp.int32)
    onehot = positions[None, :] == key_index[:, None]
    keys = jnp.einsum(
        "ns,nsjc->njc", onehot.astype(jnp.bfloat16), feat_seg, preferred_element_type=jnp.float32
    ).astype(jnp.bfloat16)
    key_full = jnp.broadcast_to(keys[:, None], seg_shape).reshape(-1, chans)
    feat_flat = feat.reshape(-1, chans)
    key_part = jnp.dot(
        keys.reshape(-1, chans), uniting_weight[1], preferred_element_type=jnp.float32
    ).reshape(seg_count, 1, width, chans)
    main_part = jnp.dot(feat_flat, uniting_weight[0], preferred_element_type=jnp.float32)
    united_blocks = (main_part.reshape(seg_shape) + key_part).astype(jnp.bfloat16)
    united = fm_to_frames(united_blocks.reshape(total_frames, width, chans), used)
    cot_flat = cot_blocks.reshape(-1, chans)
    grad_feat = jnp.dot(cot_flat, uniting_weight[0].T, preferred_element_type=jnp.float32)
    seg_cot = jnp.sum(cot_blocks.reshape(seg_shape).astype(jnp.float32), axis=1)
    key_term = jnp.dot(
        seg_cot.reshape(-1, chans),
        uniting_weight[1].T.astype(jnp.float32),
        precision=lax.Precision.HIGHEST,
    ).reshape(seg_count, 1, width, chans)
    placed = onehot.astype(jnp.float32)[:, :, None, None] * key_term
    grad_feat = grad_feat.reshape(seg_shape) + placed
    grad_feat = grad_feat.reshape(total_frames, width, chans)
    grad_uniting = jnp.stack([inner(feat_flat, cot_flat), inner(key_full, cot_flat)])
    grad_pre = (grad_feat * silu_grad(pres[-1])).astype(jnp.bfloat16)
    tgrads = [None] * LAYERS
    layer_grads = [None] * LAYERS
    for layer in range(LAYERS - 1, -1, -1):
        below = pres[layer - 1] if layer > 0 else None
        layer_grads[layer] = grad_pre
        grad_pre = temporal_backward_k(
            acts[layer], grad_pre, temporal_weight[layer], dilation[layer], below
        )
    grad_act0 = grad_pre
    grad_time = fm_to_frames(grad_act0, used).reshape(frames_in.shape)
    for layer in range(LAYERS):
        tgrads[layer] = temporal_wgrad_k(acts[layer], layer_grads[layer], dilation[layer])
    grad_spre = (grad_time.astype(jnp.float32) * spatial_slope).astype(jnp.bfloat16)
    grad_frames = spatial_back(grad_spre, spatial_weight).astype(jnp.bfloat16)
    grad_spatial = spatial_wgrad(frames_in, grad_spre)
    scale = 1.0 / jnp.sqrt(jnp.float32(total_frames * pixels))
    summed = all_sum((grad_spatial, jnp.stack(tgrads), grad_uniting), scale)
    return (
        united.reshape(frames_in.shape),
        grad_frames,
        summed[0],
        summed[1],
        summed[2],
    )


def solution(mesh):
    placed = (
        P(("seg", "grp"), None, None, None),
        P(),
        P(),
        P(),
        P(),
        P(),
        P(("seg", "grp"), None, None, None),
    )
    return jax.shard_map(
        local,
        mesh=mesh,
        in_specs=placed,
        out_specs=(
            P(("seg", "grp"), None, None, None),
            P(("seg", "grp"), None, None, None),
            P(),
            P(),
            P(),
        ),
        check_vma=False,
    )
```

```python
import functools

import jax
import jax.numpy as jnp
from jax import lax
from jax.sharding import PartitionSpec as P
from jax.experimental import pallas as pl
from jax.experimental.pallas import tpu as pltpu

LAYERS = 2
DMAX = 8


def from_root(value, axis, root):
    mine = lax.axis_index(axis) == root
    return lax.psum(jnp.where(mine, value, jnp.zeros_like(value)), axis)


def silu_grad(value):
    sigma = jax.nn.sigmoid(value)
    return sigma * (1.0 + value * (1.0 - sigma))


def inner(left, right):
    return lax.dot_general(
        left, right, (((0,), (0,)), ((), ())), preferred_element_type=jnp.float32
    )


def spatial_forward(frames, kernel):
    count, rows, cols, chans = frames.shape
    padded = jnp.pad(frames, ((0, 0), (1, 1), (1, 1), (0, 0)))
    total = jnp.zeros((count * rows * cols, chans), jnp.float32)
    for row_tap in range(3):
        for col_tap in range(3):
            piece = padded[:, row_tap : row_tap + rows, col_tap : col_tap + cols, :].reshape(
                -1, chans
            )
            total = total + jnp.dot(
                piece, kernel[3 * row_tap + col_tap], preferred_element_type=jnp.float32
            )
    return total.reshape(frames.shape)


def spatial_back(grads, kernel):
    count, rows, cols, chans = grads.shape
    padded = jnp.pad(grads, ((0, 0), (1, 1), (1, 1), (0, 0)))
    total = jnp.zeros((count * rows * cols, chans), jnp.float32)
    for row_tap in range(3):
        for col_tap in range(3):
            piece = padded[
                :, 2 - row_tap : 2 - row_tap + rows, 2 - col_tap : 2 - col_tap + cols, :
            ].reshape(-1, chans)
            total = total + jnp.dot(
                piece, kernel[3 * row_tap + col_tap].T, preferred_element_type=jnp.float32
            )
    return total.reshape(grads.shape)


def spatial_wgrad(frames, grads):
    count, rows, cols, chans = frames.shape
    padded = jnp.pad(frames, ((0, 0), (1, 1), (1, 1), (0, 0)))
    flat_grads = grads.reshape(-1, chans)
    result = []
    for row_tap in range(3):
        for col_tap in range(3):
            piece = padded[:, row_tap : row_tap + rows, col_tap : col_tap + cols, :].reshape(
                -1, chans
            )
            result.append(inner(piece, flat_grads))
    return jnp.stack(result)


def shifted(values, offset):
    padded = jnp.pad(values, ((2 * DMAX, 2 * DMAX), (0, 0), (0, 0)))
    start = 2 * DMAX + offset
    return lax.dynamic_slice_in_dim(padded, start, values.shape[0], 0)


def temporal_forward(acts, kernel, step_size):
    chans = acts.shape[2]
    total = jnp.zeros((acts.shape[0] * acts.shape[1], chans), jnp.float32)
    for tap in range(5):
        piece = shifted(acts, (tap - 2) * step_size).reshape(-1, chans)
        total = total + jnp.dot(piece, kernel[tap], preferred_element_type=jnp.float32)
    return total.reshape(acts.shape)


def temporal_back(grads, kernel, step_size):
    chans = grads.shape[2]
    total = jnp.zeros((grads.shape[0] * grads.shape[1], chans), jnp.float32)
    for tap in range(5):
        piece = shifted(grads, (2 - tap) * step_size).reshape(-1, chans)
        total = total + jnp.dot(piece, kernel[tap].T, preferred_element_type=jnp.float32)
    return total.reshape(grads.shape)


def temporal_wgrad(acts, grads, step_size):
    chans = acts.shape[2]
    flat_grads = grads.reshape(-1, chans)
    return jnp.stack(
        [
            inner(shifted(acts, (tap - 2) * step_size).reshape(-1, chans), flat_grads)
            for tap in range(5)
        ]
    )


def to_pixels(flat):
    count = lax.axis_size(("seg", "grp"))
    chans = flat.shape[-1]
    strided = flat.reshape(-1, count, chans)
    return lax.all_to_all(strided, ("seg", "grp"), split_axis=1, concat_axis=1, tiled=True)


def to_frames(blocks):
    out = lax.all_to_all(blocks, ("seg", "grp"), split_axis=1, concat_axis=1, tiled=True)
    return out.reshape(1, -1, blocks.shape[-1])


def shifted1(values, offset):
    padded = jnp.pad(values, ((0, 0), (2 * DMAX, 2 * DMAX), (0, 0)))
    start = 2 * DMAX + offset
    return lax.dynamic_slice_in_dim(padded, start, values.shape[1], 1)


def temporal_forward1(acts, kernel, step_size):
    chans = acts.shape[2]
    total = jnp.zeros((acts.shape[0] * acts.shape[1], chans), jnp.float32)
    for tap in range(5):
        piece = shifted1(acts, (tap - 2) * step_size).reshape(-1, chans)
        total = total + jnp.dot(piece, kernel[tap], preferred_element_type=jnp.float32)
    return total.reshape(acts.shape)


def temporal_back1(grads, kernel, step_size):
    chans = grads.shape[2]
    total = jnp.zeros((grads.shape[0] * grads.shape[1], chans), jnp.float32)
    for tap in range(5):
        piece = shifted1(grads, (2 - tap) * step_size).reshape(-1, chans)
        total = total + jnp.dot(piece, kernel[tap].T, preferred_element_type=jnp.float32)
    return total.reshape(grads.shape)


def temporal_wgrad1(acts, grads, step_size):
    chans = acts.shape[2]
    flat_grads = grads.reshape(-1, chans)
    return jnp.stack(
        [
            inner(shifted1(acts, (tap - 2) * step_size).reshape(-1, chans), flat_grads)
            for tap in range(5)
        ]
    )


HALO = 2 * DMAX
FB = 64


def fm_to_pixels(flat):
    count = lax.axis_size(("seg", "grp"))
    chans = flat.shape[-1]
    strided = flat.reshape(-1, count, chans)
    rows = -(-strided.shape[0] // 16) * 16
    strided = jnp.pad(strided, ((0, rows - strided.shape[0]), (0, 0), (0, 0)))
    out = lax.all_to_all(strided, ("seg", "grp"), split_axis=1, concat_axis=1, tiled=True)
    return jnp.transpose(out, (1, 0, 2))


def fm_to_frames(blocks, used):
    moved = jnp.transpose(blocks, (1, 0, 2))
    out = lax.all_to_all(moved, ("seg", "grp"), split_axis=1, concat_axis=1, tiled=True)
    return out[:used].reshape(1, -1, blocks.shape[-1])


def fill_halo(src_ref, pad_ref):
    frames = src_ref.shape[0]
    zeros = jnp.zeros((HALO,) + pad_ref.shape[1:], pad_ref.dtype)
    pad_ref[0:HALO] = zeros
    pad_ref[HALO + frames : 2 * HALO + frames] = zeros
    pad_ref[HALO : HALO + frames] = src_ref[...]


def tap_rows(pad_ref, start, rows):
    return pad_ref[pl.ds(start, FB)].reshape(rows, pad_ref.shape[-1])


def tfwd_kernel(dil_ref, act_ref, w_ref, pre_ref, out_ref, pad_ref):
    frames, width, chans = act_ref.shape
    fill_halo(act_ref, pad_ref)
    step = dil_ref[0]
    rows = FB * width
    for block in range(frames // FB):
        base = HALO + block * FB
        stacked = jnp.concatenate(
            [tap_rows(pad_ref, base + (tap - 2) * step, rows) for tap in range(5)], axis=1
        )
        pre = jnp.dot(stacked, w_ref[...], preferred_element_type=jnp.float32)
        pre_ref[block * FB : (block + 1) * FB] = pre.reshape(FB, width, chans)
        out_ref[block * FB : (block + 1) * FB] = (
            (pre / (1.0 + jnp.exp(-pre))).astype(jnp.bfloat16).reshape(FB, width, chans)
        )


def temporal_forward_k(acts, kernel, step_size):
    frames, width, chans = acts.shape
    return pl.pallas_call(
        tfwd_kernel,
        grid_spec=pltpu.PrefetchScalarGridSpec(
            num_scalar_prefetch=1,
            grid=(1,),
            in_specs=[
                pl.BlockSpec(acts.shape, lambda i, d: (0, 0, 0)),
                pl.BlockSpec((5 * chans, chans), lambda i, d: (0, 0)),
            ],
            out_specs=[
                pl.BlockSpec(acts.shape, lambda i, d: (0, 0, 0)),
                pl.BlockSpec(acts.shape, lambda i, d: (0, 0, 0)),
            ],
            scratch_shapes=[pltpu.VMEM((frames + 2 * HALO, width, chans), jnp.bfloat16)],
        ),
        out_shape=[
            jax.ShapeDtypeStruct(acts.shape, jnp.float32),
            jax.ShapeDtypeStruct(acts.shape, jnp.bfloat16),
        ],
        cost_estimate=pl.CostEstimate(
            flops=2 * frames * width * chans * chans * 5,
            transcendentals=frames * width * chans,
            bytes_accessed=frames * width * chans * 8,
        ),
    )(step_size.reshape(1), acts, kernel.reshape(5 * chans, chans))


def tbwd_kernel(with_pre, dil_ref, act_ref, grad_ref, wt_ref, *rest):
    if with_pre:
        pre_ref, out_ref, pad_ref = rest
    else:
        out_ref, pad_ref = rest
    frames, width, chans = act_ref.shape
    fill_halo(grad_ref, pad_ref)
    step = dil_ref[0]
    rows = FB * width
    for block in range(frames // FB):
        base = HALO + block * FB
        stacked = jnp.concatenate(
            [tap_rows(pad_ref, base - (tap - 2) * step, rows) for tap in range(5)], axis=1
        )
        grad_act = None
        for tap in range(5):
            term = lax.dot_general(
                stacked[:, tap * chans : (tap + 1) * chans],
                wt_ref[tap * chans : (tap + 1) * chans, :],
                (((1,), (1,)), ((), ())),
                preferred_element_type=jnp.float32,
            )
            grad_act = term if grad_act is None else grad_act + term
        if with_pre:
            pre = pre_ref[block * FB : (block + 1) * FB].reshape(rows, chans)
            sigma = 1.0 / (1.0 + jnp.exp(-pre))
            grad_act = grad_act * (sigma * (1.0 + pre * (1.0 - sigma)))
        out_ref[block * FB : (block + 1) * FB] = (
            grad_act.astype(jnp.bfloat16).reshape(FB, width, chans)
        )


def twgrad_kernel(dil_ref, act_ref, grad_ref, tg_ref, pad_ref):
    frames, width, chans = act_ref.shape
    fill_halo(grad_ref, pad_ref)
    step = dil_ref[0]
    rows = FB * width
    total = None
    for block in range(frames // FB):
        base = HALO + block * FB
        stacked = jnp.concatenate(
            [tap_rows(pad_ref, base - (tap - 2) * step, rows) for tap in range(5)], axis=1
        )
        flat_act = act_ref[block * FB : (block + 1) * FB].reshape(rows, chans)
        part = lax.dot_general(
            flat_act, stacked, (((0,), (0,)), ((), ())), preferred_element_type=jnp.float32
        )
        total = part if total is None else total + part
    for tap in range(5):
        tg_ref[tap] = total[:, tap * chans : (tap + 1) * chans]


def temporal_wgrad_k(acts, grads, step_size):
    frames, width, chans = acts.shape
    full = pl.BlockSpec(acts.shape, lambda i, d: (0, 0, 0))
    return pl.pallas_call(
        twgrad_kernel,
        grid_spec=pltpu.PrefetchScalarGridSpec(
            num_scalar_prefetch=1,
            grid=(1,),
            in_specs=[full, full],
            out_specs=pl.BlockSpec((5, chans, chans), lambda i, d: (0, 0, 0)),
            scratch_shapes=[pltpu.VMEM((frames + 2 * HALO, width, chans), jnp.bfloat16)],
        ),
        out_shape=jax.ShapeDtypeStruct((5, chans, chans), jnp.float32),
        cost_estimate=pl.CostEstimate(
            flops=2 * frames * width * chans * chans * 5,
            transcendentals=0,
            bytes_accessed=frames * width * chans * 4,
        ),
    )(step_size.reshape(1), acts, grads)


def temporal_backward_k(acts, grads, kernel, step_size, pre_below):
    frames, width, chans = acts.shape
    full = pl.BlockSpec(acts.shape, lambda i, d: (0, 0, 0))
    with_pre = pre_below is not None
    in_specs = [full, full, pl.BlockSpec((5 * chans, chans), lambda i, d: (0, 0))]
    operands = [step_size.reshape(1), acts, grads, kernel.reshape(5 * chans, chans)]
    if with_pre:
        in_specs.append(full)
        operands.append(pre_below)
    return pl.pallas_call(
        functools.partial(tbwd_kernel, with_pre),
        grid_spec=pltpu.PrefetchScalarGridSpec(
            num_scalar_prefetch=1,
            grid=(1,),
            in_specs=in_specs,
            out_specs=full,
            scratch_shapes=[pltpu.VMEM((frames + 2 * HALO, width, chans), jnp.bfloat16)],
        ),
        out_shape=jax.ShapeDtypeStruct(acts.shape, jnp.bfloat16),
        cost_estimate=pl.CostEstimate(
            flops=2 * frames * width * chans * chans * 5,
            transcendentals=frames * width * chans,
            bytes_accessed=frames * width * chans * 10,
        ),
    )(*operands)


def all_sum(parts, scale):
    chans = parts[0].shape[-1]
    count = lax.axis_size(("seg", "grp"))
    rows = [p.reshape(-1, chans) for p in parts]
    used = sum(r.shape[0] for r in rows)
    per = -(-used // (count * 8)) * 8
    rows.append(jnp.zeros((per * count - used, chans), jnp.float32))
    stack = jnp.concatenate(rows, axis=0).reshape(count, per, chans)
    pieces = lax.all_to_all(stack, ("seg", "grp"), split_axis=0, concat_axis=0, tiled=True)
    mine = (jnp.sum(pieces, axis=0, keepdims=True) * scale).astype(jnp.bfloat16)
    spread = jnp.broadcast_to(mine, stack.shape)
    whole = lax.all_to_all(spread, ("seg", "grp"), split_axis=0, concat_axis=0, tiled=True)
    whole = whole.astype(jnp.float32).reshape(-1, chans)
    out = []
    offset = 0
    for p in parts:
        size = p.size // chans
        out.append(whole[offset : offset + size].reshape(p.shape))
        offset += size
    return out


def local(
    frames_in, spatial_weight, temporal_weight, uniting_weight, key_index, dilation, cotangent
):
    local_frames, rows, cols, chans = frames_in.shape
    pixels = rows * cols
    seg_count = lax.axis_size("seg")
    count = lax.axis_size(("seg", "grp"))
    used = pixels // count
    pre_spatial = spatial_forward(frames_in, spatial_weight)
    act_zero = jax.nn.silu(pre_spatial).astype(jnp.bfloat16).reshape(local_frames, pixels, chans)
    cot_local = cotangent.reshape(local_frames, pixels, chans)
    act_blocks = fm_to_pixels(act_zero)
    act_blocks, cot_local = lax.optimization_barrier((act_blocks, cot_local))
    cot_blocks = fm_to_pixels(cot_local)
    acts = [act_blocks]
    total_frames, width = act_blocks.shape[0], act_blocks.shape[1]
    seg_frames = total_frames // seg_count
    pres = []
    for layer in range(LAYERS):
        pre, act = temporal_forward_k(acts[-1], temporal_weight[layer], dilation[layer])
        pres.append(pre)
        acts.append(act)
    feat = acts[-1]
    seg_shape = (seg_count, seg_frames, width, chans)
    feat_seg = feat.reshape(seg_shape)
    positions = jnp.arange(seg_frames, dtype=jnp.int32)
    onehot = positions[None, :] == key_index[:, None]
    keys = jnp.einsum(
        "ns,nsjc->njc", onehot.astype(jnp.bfloat16), feat_seg, preferred_element_type=jnp.float32
    ).astype(jnp.bfloat16)
    key_full = jnp.broadcast_to(keys[:, None], seg_shape).reshape(-1, chans)
    feat_flat = feat.reshape(-1, chans)
    key_part = jnp.dot(
        keys.reshape(-1, chans), uniting_weight[1], preferred_element_type=jnp.float32
    ).reshape(seg_count, 1, width, chans)
    main_part = jnp.dot(feat_flat, uniting_weight[0], preferred_element_type=jnp.float32)
    united_blocks = (main_part.reshape(seg_shape) + key_part).astype(jnp.bfloat16)
    united = fm_to_frames(united_blocks.reshape(total_frames, width, chans), used)
    cot_flat = cot_blocks.reshape(-1, chans)
    grad_feat = jnp.dot(cot_flat, uniting_weight[0].T, preferred_element_type=jnp.float32)
    seg_cot = jnp.sum(cot_blocks.reshape(seg_shape).astype(jnp.float32), axis=1)
    key_term = jnp.dot(
        seg_cot.reshape(-1, chans),
        uniting_weight[1].T.astype(jnp.float32),
        precision=lax.Precision.HIGHEST,
    ).reshape(seg_count, 1, width, chans)
    placed = onehot.astype(jnp.float32)[:, :, None, None] * key_term
    grad_feat = grad_feat.reshape(seg_shape) + placed
    grad_feat = grad_feat.reshape(total_frames, width, chans)
    grad_uniting = jnp.stack([inner(feat_flat, cot_flat), inner(key_full, cot_flat)])
    grad_pre = (grad_feat * silu_grad(pres[-1])).astype(jnp.bfloat16)
    tgrads = [None] * LAYERS
    layer_grads = [None] * LAYERS
    for layer in range(LAYERS - 1, -1, -1):
        below = pres[layer - 1] if layer > 0 else None
        layer_grads[layer] = grad_pre
        grad_pre = temporal_backward_k(
            acts[layer], grad_pre, temporal_weight[layer], dilation[layer], below
        )
    grad_act0 = grad_pre
    grad_time = fm_to_frames(grad_act0, used).reshape(frames_in.shape)
    for layer in range(LAYERS):
        tgrads[layer] = temporal_wgrad_k(acts[layer], layer_grads[layer], dilation[layer])
    grad_spre = (grad_time.astype(jnp.float32) * silu_grad(pre_spatial)).astype(jnp.bfloat16)
    grad_frames = spatial_back(grad_spre, spatial_weight).astype(jnp.bfloat16)
    grad_spatial = spatial_wgrad(frames_in, grad_spre)
    scale = 1.0 / jnp.sqrt(jnp.float32(total_frames * pixels))
    summed = all_sum((grad_spatial, jnp.stack(tgrads), grad_uniting), scale)
    return (
        united.reshape(frames_in.shape),
        grad_frames,
        summed[0],
        summed[1],
        summed[2],
    )


def solution(mesh):
    placed = (
        P(("seg", "grp"), None, None, None),
        P(),
        P(),
        P(),
        P(),
        P(),
        P(("seg", "grp"), None, None, None),
    )
    return jax.shard_map(
        local,
        mesh=mesh,
        in_specs=placed,
        out_specs=(
            P(("seg", "grp"), None, None, None),
            P(("seg", "grp"), None, None, None),
            P(),
            P(),
            P(),
        ),
        check_vma=False,
    )
```

```python
import functools

import jax
import jax.numpy as jnp
from jax import lax
from jax.sharding import PartitionSpec as P
from jax.experimental import pallas as pl
from jax.experimental.pallas import tpu as pltpu

LAYERS = 2
DMAX = 8


def from_root(value, axis, root):
    mine = lax.axis_index(axis) == root
    return lax.psum(jnp.where(mine, value, jnp.zeros_like(value)), axis)


def silu_grad(value):
    sigma = jax.nn.sigmoid(value)
    return sigma * (1.0 + value * (1.0 - sigma))


def inner(left, right):
    return lax.dot_general(
        left, right, (((0,), (0,)), ((), ())), preferred_element_type=jnp.float32
    )


def spatial_forward(frames, kernel):
    count, rows, cols, chans = frames.shape
    padded = jnp.pad(frames, ((0, 0), (1, 1), (1, 1), (0, 0)))
    total = jnp.zeros((count * rows * cols, chans), jnp.float32)
    for row_tap in range(3):
        for col_tap in range(3):
            piece = padded[:, row_tap : row_tap + rows, col_tap : col_tap + cols, :].reshape(
                -1, chans
            )
            total = total + jnp.dot(
                piece, kernel[3 * row_tap + col_tap], preferred_element_type=jnp.float32
            )
    return total.reshape(frames.shape)


def spatial_back(grads, kernel):
    count, rows, cols, chans = grads.shape
    padded = jnp.pad(grads, ((0, 0), (1, 1), (1, 1), (0, 0)))
    total = jnp.zeros((count * rows * cols, chans), jnp.float32)
    for row_tap in range(3):
        for col_tap in range(3):
            piece = padded[
                :, 2 - row_tap : 2 - row_tap + rows, 2 - col_tap : 2 - col_tap + cols, :
            ].reshape(-1, chans)
            total = total + jnp.dot(
                piece, kernel[3 * row_tap + col_tap].T, preferred_element_type=jnp.float32
            )
    return total.reshape(grads.shape)


def spatial_wgrad(frames, grads):
    count, rows, cols, chans = frames.shape
    padded = jnp.pad(frames, ((0, 0), (1, 1), (1, 1), (0, 0)))
    flat_grads = grads.reshape(-1, chans)
    result = []
    for row_tap in range(3):
        for col_tap in range(3):
            piece = padded[:, row_tap : row_tap + rows, col_tap : col_tap + cols, :].reshape(
                -1, chans
            )
            result.append(inner(piece, flat_grads))
    return jnp.stack(result)


def shifted(values, offset):
    padded = jnp.pad(values, ((2 * DMAX, 2 * DMAX), (0, 0), (0, 0)))
    start = 2 * DMAX + offset
    return lax.dynamic_slice_in_dim(padded, start, values.shape[0], 0)


def temporal_forward(acts, kernel, step_size):
    chans = acts.shape[2]
    total = jnp.zeros((acts.shape[0] * acts.shape[1], chans), jnp.float32)
    for tap in range(5):
        piece = shifted(acts, (tap - 2) * step_size).reshape(-1, chans)
        total = total + jnp.dot(piece, kernel[tap], preferred_element_type=jnp.float32)
    return total.reshape(acts.shape)


def temporal_back(grads, kernel, step_size):
    chans = grads.shape[2]
    total = jnp.zeros((grads.shape[0] * grads.shape[1], chans), jnp.float32)
    for tap in range(5):
        piece = shifted(grads, (2 - tap) * step_size).reshape(-1, chans)
        total = total + jnp.dot(piece, kernel[tap].T, preferred_element_type=jnp.float32)
    return total.reshape(grads.shape)


def temporal_wgrad(acts, grads, step_size):
    chans = acts.shape[2]
    flat_grads = grads.reshape(-1, chans)
    return jnp.stack(
        [
            inner(shifted(acts, (tap - 2) * step_size).reshape(-1, chans), flat_grads)
            for tap in range(5)
        ]
    )


def to_pixels(flat):
    count = lax.axis_size(("seg", "grp"))
    chans = flat.shape[-1]
    strided = flat.reshape(-1, count, chans)
    return lax.all_to_all(strided, ("seg", "grp"), split_axis=1, concat_axis=1, tiled=True)


def to_frames(blocks):
    out = lax.all_to_all(blocks, ("seg", "grp"), split_axis=1, concat_axis=1, tiled=True)
    return out.reshape(1, -1, blocks.shape[-1])


def shifted1(values, offset):
    padded = jnp.pad(values, ((0, 0), (2 * DMAX, 2 * DMAX), (0, 0)))
    start = 2 * DMAX + offset
    return lax.dynamic_slice_in_dim(padded, start, values.shape[1], 1)


def temporal_forward1(acts, kernel, step_size):
    chans = acts.shape[2]
    total = jnp.zeros((acts.shape[0] * acts.shape[1], chans), jnp.float32)
    for tap in range(5):
        piece = shifted1(acts, (tap - 2) * step_size).reshape(-1, chans)
        total = total + jnp.dot(piece, kernel[tap], preferred_element_type=jnp.float32)
    return total.reshape(acts.shape)


def temporal_back1(grads, kernel, step_size):
    chans = grads.shape[2]
    total = jnp.zeros((grads.shape[0] * grads.shape[1], chans), jnp.float32)
    for tap in range(5):
        piece = shifted1(grads, (2 - tap) * step_size).reshape(-1, chans)
        total = total + jnp.dot(piece, kernel[tap].T, preferred_element_type=jnp.float32)
    return total.reshape(grads.shape)


def temporal_wgrad1(acts, grads, step_size):
    chans = acts.shape[2]
    flat_grads = grads.reshape(-1, chans)
    return jnp.stack(
        [
            inner(shifted1(acts, (tap - 2) * step_size).reshape(-1, chans), flat_grads)
            for tap in range(5)
        ]
    )


HALO = 2 * DMAX
FB = 32


def fm_to_pixels(flat):
    count = lax.axis_size(("seg", "grp"))
    chans = flat.shape[-1]
    strided = flat.reshape(-1, count, chans)
    rows = -(-strided.shape[0] // 16) * 16
    strided = jnp.pad(strided, ((0, rows - strided.shape[0]), (0, 0), (0, 0)))
    out = lax.all_to_all(strided, ("seg", "grp"), split_axis=1, concat_axis=1, tiled=True)
    return jnp.transpose(out, (1, 0, 2))


def fm_to_frames(blocks, used):
    moved = jnp.transpose(blocks, (1, 0, 2))
    out = lax.all_to_all(moved, ("seg", "grp"), split_axis=1, concat_axis=1, tiled=True)
    return out[:used].reshape(1, -1, blocks.shape[-1])


def fill_halo(src_ref, pad_ref):
    frames = src_ref.shape[0]
    zeros = jnp.zeros((HALO,) + pad_ref.shape[1:], pad_ref.dtype)
    pad_ref[0:HALO] = zeros
    pad_ref[HALO + frames : 2 * HALO + frames] = zeros
    pad_ref[HALO : HALO + frames] = src_ref[...]


def tap_rows(pad_ref, start, rows):
    return pad_ref[pl.ds(start, FB)].reshape(rows, pad_ref.shape[-1])


def tfwd_kernel(dil_ref, act_ref, w_ref, pre_ref, out_ref, pad_ref):
    frames, width, chans = act_ref.shape
    fill_halo(act_ref, pad_ref)
    step = dil_ref[0]
    rows = FB * width
    for block in range(frames // FB):
        base = HALO + block * FB
        stacked = jnp.concatenate(
            [tap_rows(pad_ref, base + (tap - 2) * step, rows) for tap in range(5)], axis=1
        )
        pre = jnp.dot(stacked, w_ref[...], preferred_element_type=jnp.float32)
        pre_ref[block * FB : (block + 1) * FB] = pre.reshape(FB, width, chans)
        out_ref[block * FB : (block + 1) * FB] = (
            (pre / (1.0 + jnp.exp(-pre))).astype(jnp.bfloat16).reshape(FB, width, chans)
        )


def temporal_forward_k(acts, kernel, step_size):
    frames, width, chans = acts.shape
    return pl.pallas_call(
        tfwd_kernel,
        grid_spec=pltpu.PrefetchScalarGridSpec(
            num_scalar_prefetch=1,
            grid=(1,),
            in_specs=[
                pl.BlockSpec(acts.shape, lambda i, d: (0, 0, 0)),
                pl.BlockSpec((5 * chans, chans), lambda i, d: (0, 0)),
            ],
            out_specs=[
                pl.BlockSpec(acts.shape, lambda i, d: (0, 0, 0)),
                pl.BlockSpec(acts.shape, lambda i, d: (0, 0, 0)),
            ],
            scratch_shapes=[pltpu.VMEM((frames + 2 * HALO, width, chans), jnp.bfloat16)],
        ),
        out_shape=[
            jax.ShapeDtypeStruct(acts.shape, jnp.float32),
            jax.ShapeDtypeStruct(acts.shape, jnp.bfloat16),
        ],
        cost_estimate=pl.CostEstimate(
            flops=2 * frames * width * chans * chans * 5,
            transcendentals=frames * width * chans,
            bytes_accessed=frames * width * chans * 8,
        ),
    )(step_size.reshape(1), acts, kernel.reshape(5 * chans, chans))


def tbwd_kernel(with_pre, dil_ref, act_ref, grad_ref, wt_ref, *rest):
    if with_pre:
        pre_ref, out_ref, pad_ref = rest
    else:
        out_ref, pad_ref = rest
    frames, width, chans = act_ref.shape
    fill_halo(grad_ref, pad_ref)
    step = dil_ref[0]
    rows = FB * width
    for block in range(frames // FB):
        base = HALO + block * FB
        stacked = jnp.concatenate(
            [tap_rows(pad_ref, base - (tap - 2) * step, rows) for tap in range(5)], axis=1
        )
        grad_act = None
        for tap in range(5):
            term = lax.dot_general(
                stacked[:, tap * chans : (tap + 1) * chans],
                wt_ref[tap * chans : (tap + 1) * chans, :],
                (((1,), (1,)), ((), ())),
                preferred_element_type=jnp.float32,
            )
            grad_act = term if grad_act is None else grad_act + term
        if with_pre:
            pre = pre_ref[block * FB : (block + 1) * FB].reshape(rows, chans)
            sigma = 1.0 / (1.0 + jnp.exp(-pre))
            grad_act = grad_act * (sigma * (1.0 + pre * (1.0 - sigma)))
        out_ref[block * FB : (block + 1) * FB] = (
            grad_act.astype(jnp.bfloat16).reshape(FB, width, chans)
        )


def twgrad_kernel(dil_ref, act_ref, grad_ref, tg_ref, pad_ref):
    frames, width, chans = act_ref.shape
    fill_halo(grad_ref, pad_ref)
    step = dil_ref[0]
    rows = FB * width
    total = None
    for block in range(frames // FB):
        base = HALO + block * FB
        stacked = jnp.concatenate(
            [tap_rows(pad_ref, base - (tap - 2) * step, rows) for tap in range(5)], axis=1
        )
        flat_act = act_ref[block * FB : (block + 1) * FB].reshape(rows, chans)
        part = lax.dot_general(
            flat_act, stacked, (((0,), (0,)), ((), ())), preferred_element_type=jnp.float32
        )
        total = part if total is None else total + part
    for tap in range(5):
        tg_ref[tap] = total[:, tap * chans : (tap + 1) * chans]


def temporal_wgrad_k(acts, grads, step_size):
    frames, width, chans = acts.shape
    full = pl.BlockSpec(acts.shape, lambda i, d: (0, 0, 0))
    return pl.pallas_call(
        twgrad_kernel,
        grid_spec=pltpu.PrefetchScalarGridSpec(
            num_scalar_prefetch=1,
            grid=(1,),
            in_specs=[full, full],
            out_specs=pl.BlockSpec((5, chans, chans), lambda i, d: (0, 0, 0)),
            scratch_shapes=[pltpu.VMEM((frames + 2 * HALO, width, chans), jnp.bfloat16)],
        ),
        out_shape=jax.ShapeDtypeStruct((5, chans, chans), jnp.float32),
        cost_estimate=pl.CostEstimate(
            flops=2 * frames * width * chans * chans * 5,
            transcendentals=0,
            bytes_accessed=frames * width * chans * 4,
        ),
    )(step_size.reshape(1), acts, grads)


def temporal_backward_k(acts, grads, kernel, step_size, pre_below):
    frames, width, chans = acts.shape
    full = pl.BlockSpec(acts.shape, lambda i, d: (0, 0, 0))
    with_pre = pre_below is not None
    in_specs = [full, full, pl.BlockSpec((5 * chans, chans), lambda i, d: (0, 0))]
    operands = [step_size.reshape(1), acts, grads, kernel.reshape(5 * chans, chans)]
    if with_pre:
        in_specs.append(full)
        operands.append(pre_below)
    return pl.pallas_call(
        functools.partial(tbwd_kernel, with_pre),
        grid_spec=pltpu.PrefetchScalarGridSpec(
            num_scalar_prefetch=1,
            grid=(1,),
            in_specs=in_specs,
            out_specs=full,
            scratch_shapes=[pltpu.VMEM((frames + 2 * HALO, width, chans), jnp.bfloat16)],
        ),
        out_shape=jax.ShapeDtypeStruct(acts.shape, jnp.bfloat16),
        cost_estimate=pl.CostEstimate(
            flops=2 * frames * width * chans * chans * 5,
            transcendentals=frames * width * chans,
            bytes_accessed=frames * width * chans * 10,
        ),
    )(*operands)


def all_sum(parts, scale):
    chans = parts[0].shape[-1]
    count = lax.axis_size(("seg", "grp"))
    rows = [p.reshape(-1, chans) for p in parts]
    used = sum(r.shape[0] for r in rows)
    per = -(-used // (count * 8)) * 8
    rows.append(jnp.zeros((per * count - used, chans), jnp.float32))
    stack = jnp.concatenate(rows, axis=0).reshape(count, per, chans)
    pieces = lax.all_to_all(stack, ("seg", "grp"), split_axis=0, concat_axis=0, tiled=True)
    mine = (jnp.sum(pieces, axis=0, keepdims=True) * scale).astype(jnp.bfloat16)
    spread = jnp.broadcast_to(mine, stack.shape)
    whole = lax.all_to_all(spread, ("seg", "grp"), split_axis=0, concat_axis=0, tiled=True)
    whole = whole.astype(jnp.float32).reshape(-1, chans)
    out = []
    offset = 0
    for p in parts:
        size = p.size // chans
        out.append(whole[offset : offset + size].reshape(p.shape))
        offset += size
    return out


def local(
    frames_in, spatial_weight, temporal_weight, uniting_weight, key_index, dilation, cotangent
):
    local_frames, rows, cols, chans = frames_in.shape
    pixels = rows * cols
    seg_count = lax.axis_size("seg")
    count = lax.axis_size(("seg", "grp"))
    used = pixels // count
    pre_spatial = spatial_forward(frames_in, spatial_weight)
    act_zero = jax.nn.silu(pre_spatial).astype(jnp.bfloat16).reshape(local_frames, pixels, chans)
    cot_local = cotangent.reshape(local_frames, pixels, chans)
    act_blocks = fm_to_pixels(act_zero)
    cot_blocks = fm_to_pixels(cot_local)
    acts = [act_blocks]
    total_frames, width = act_blocks.shape[0], act_blocks.shape[1]
    seg_frames = total_frames // seg_count
    pres = []
    for layer in range(LAYERS):
        pre, act = temporal_forward_k(acts[-1], temporal_weight[layer], dilation[layer])
        pres.append(pre)
        acts.append(act)
    feat = acts[-1]
    seg_shape = (seg_count, seg_frames, width, chans)
    feat_seg = feat.reshape(seg_shape)
    positions = jnp.arange(seg_frames, dtype=jnp.int32)
    onehot = positions[None, :] == key_index[:, None]
    keys = jnp.einsum(
        "ns,nsjc->njc", onehot.astype(jnp.bfloat16), feat_seg, preferred_element_type=jnp.float32
    ).astype(jnp.bfloat16)
    key_full = jnp.broadcast_to(keys[:, None], seg_shape).reshape(-1, chans)
    feat_flat = feat.reshape(-1, chans)
    key_part = jnp.dot(
        keys.reshape(-1, chans), uniting_weight[1], preferred_element_type=jnp.float32
    ).reshape(seg_count, 1, width, chans)
    main_part = jnp.dot(feat_flat, uniting_weight[0], preferred_element_type=jnp.float32)
    united_blocks = (main_part.reshape(seg_shape) + key_part).astype(jnp.bfloat16)
    united = fm_to_frames(united_blocks.reshape(total_frames, width, chans), used)
    cot_flat = cot_blocks.reshape(-1, chans)
    grad_feat = jnp.dot(cot_flat, uniting_weight[0].T, preferred_element_type=jnp.float32)
    seg_cot = jnp.sum(cot_blocks.reshape(seg_shape).astype(jnp.float32), axis=1)
    key_term = jnp.dot(
        seg_cot.reshape(-1, chans),
        uniting_weight[1].T.astype(jnp.float32),
        precision=lax.Precision.HIGHEST,
    ).reshape(seg_count, 1, width, chans)
    placed = onehot.astype(jnp.float32)[:, :, None, None] * key_term
    grad_feat = grad_feat.reshape(seg_shape) + placed
    grad_feat = grad_feat.reshape(total_frames, width, chans)
    grad_uniting = jnp.stack([inner(feat_flat, cot_flat), inner(key_full, cot_flat)])
    grad_pre = (grad_feat * silu_grad(pres[-1])).astype(jnp.bfloat16)
    tgrads = [None] * LAYERS
    layer_grads = [None] * LAYERS
    for layer in range(LAYERS - 1, -1, -1):
        below = pres[layer - 1] if layer > 0 else None
        layer_grads[layer] = grad_pre
        grad_pre = temporal_backward_k(
            acts[layer], grad_pre, temporal_weight[layer], dilation[layer], below
        )
    grad_act0 = grad_pre
    grad_time = fm_to_frames(grad_act0, used).reshape(frames_in.shape)
    for layer in range(LAYERS):
        tgrads[layer] = temporal_wgrad_k(acts[layer], layer_grads[layer], dilation[layer])
    grad_spre = (grad_time.astype(jnp.float32) * silu_grad(pre_spatial)).astype(jnp.bfloat16)
    grad_frames = spatial_back(grad_spre, spatial_weight).astype(jnp.bfloat16)
    grad_spatial = spatial_wgrad(frames_in, grad_spre)
    scale = 1.0 / jnp.sqrt(jnp.float32(total_frames * pixels))
    summed = all_sum((grad_spatial, jnp.stack(tgrads), grad_uniting), scale)
    return (
        united.reshape(frames_in.shape),
        grad_frames,
        summed[0],
        summed[1],
        summed[2],
    )


def solution(mesh):
    placed = (
        P(("seg", "grp"), None, None, None),
        P(),
        P(),
        P(),
        P(),
        P(),
        P(("seg", "grp"), None, None, None),
    )
    return jax.shard_map(
        local,
        mesh=mesh,
        in_specs=placed,
        out_specs=(
            P(("seg", "grp"), None, None, None),
            P(("seg", "grp"), None, None, None),
            P(),
            P(),
            P(),
        ),
        check_vma=False,
    )
```
